32 devices in a mesh: dp: 8 (over z, x), fsdp: 4 (over y, core).
Axes of the slice: x: 2, y: 2, z: 4, core: 2. Of those that a mesh axis runs over, the one named last changes fastest.
Arguments:
- frames: bfloat16 [32, 768, 768], P(('dp', 'fsdp')), may hold values from -6 to 6
- lengths: int32 [32], P(('dp', 'fsdp')), may hold values from 1 to 768, 15360 in all
- attn_params: bfloat16 [2363136], P(('dp', 'fsdp')), may hold values from -4 to 4
- ffn_params: bfloat16 [4723968], P(('dp', 'fsdp')), may hold values from -4 to 4
- cotangent: bfloat16 [32, 768, 768], P(('dp', 'fsdp')), may hold values from -6 to 6
Outputs:
- layer_out: bfloat16 [32, 768, 768], P(('dp', 'fsdp'))
- input_grad: bfloat16 [32, 768, 768], P(('dp', 'fsdp'))
- attn_grad: float32 [2363136], P(('dp', 'fsdp'))
- ffn_grad: float32 [4723968], P(('dp', 'fsdp'))
The draws below stay inside these ranges and needn't reach their ends.
All inputs are finite; a program needn't handle non-finite values. No bound on the sum of `lengths` on one device may be relied on, other than what follows from the above.
Results may differ from the reference program's by a relative error of at most 0.013.
Values may be sent and summed in bfloat16 or wider, within the bound.
A program may use at most 192 MiB of HBM per device.

```python
import math
import jax
import jax.numpy as jnp
import numpy as np
from jax import lax

D = 768
H = 12
FF = 3072
DH = 64
MAXLEN = 768
UTT = 32
ATT_LEN = 2363136
ATT_PAD = 2363136
FFN_LEN = 4723968
FFN_PAD = 4723968


def base_values(key, count):
    return jnp.clip(jax.random.normal(key, (count,), jnp.float32), -3.0, 3.0)


def draw_attn_params(key, part):
    base = base_values(jax.random.fold_in(key, 11), ATT_PAD)
    place = jnp.arange(ATT_PAD)
    square = D * D
    start = 4 * square
    scale = jnp.where(place < 3 * square, D ** (-0.5), jnp.where(place < start, (MAXLEN / (8.0 * D)) ** 0.5, jnp.where(place < start + D, 0.2, jnp.where(place < start + 2 * D, 0.02, jnp.where(place < start + 3 * D, 0.1, 0.2)))))
    value = scale * base
    gains = (place >= start + 3 * D) & (place < start + 4 * D)
    value = jnp.where(gains, 1.0 + 0.06 * base, value)
    value = jnp.where(place < ATT_LEN, value, 0.0)
    return value.astype(jnp.bfloat16)


def draw_ffn_params(key, part):
    base = base_values(jax.random.fold_in(key, 23), FFN_PAD)
    place = jnp.arange(FFN_PAD)
    span = D * FF
    start = 2 * span
    scale = jnp.where(place < span, D ** (-0.5), jnp.where(place < start, FF ** (-0.5), jnp.where(place < start + FF, 0.2, jnp.where(place < start + FF + D, 0.1, 0.2))))
    value = scale * base
    gains = (place >= start + FF + D) & (place < start + FF + 2 * D)
    value = jnp.where(gains, 1.0 + 0.06 * base, value)
    value = jnp.where(place < FFN_LEN, value, 0.0)
    return value.astype(jnp.bfloat16)


def shard_levels(stream_key, dims, pieces, low, largest):
    level = 1.0
    for position, blocks in pieces:
        steps = jax.random.uniform(jax.random.fold_in(jax.random.fold_in(stream_key, 6), position), (blocks,), jnp.float32, low / len(pieces), largest / len(pieces))
        level = level * jnp.repeat(jnp.exp(steps), dims[position] // blocks).reshape((-1,) + (1,) * (len(dims) - 1 - position))
    return level


def length_profile(number_of, total, most, slope):
    portions = [(1 << 20) // math.isqrt(standing ** slope) + 1 for standing in range(2, number_of + 1)]
    surplus, counts = total - most - (number_of - 1), [1] * (number_of - 1)
    while surplus > 0:
        candidates = [i for i in range(number_of - 1) if counts[i] < most]
        mass, remaining = sum([portions[i] for i in candidates]), surplus
        for i in candidates:
            extra = min(most - counts[i], max(1, remaining * portions[i] // mass), surplus)
            counts[i] = counts[i] + extra
            surplus = surplus - extra
    return np.array([most] + counts)


def uneven_parts(key, number_of, total, most, skew):
    if number_of == 2:
        one = jax.random.randint(key, (), max(1, total - most), min(most, total - 1) + 1)
        return jnp.stack([one, total - one])
    tallies = jnp.asarray(length_profile(number_of, total, most, skew), jnp.int32)
    couples = (number_of - 1) // 2
    giver, taker = tallies[1:1 + 2 * couples:2], tallies[2:2 + 2 * couples:2]
    room = jnp.minimum(giver - 1, most - taker)
    moved = jax.random.randint(jax.random.fold_in(key, 1), (couples,), 0, 1 << 20) % (room + 1)
    tallies = tallies.at[1:1 + 2 * couples:2].set(giver - moved).at[2:2 + 2 * couples:2].set(taker + moved)
    return tallies[jax.random.permutation(jax.random.fold_in(key, 2), number_of)]


def normal_values(key, shape, deviation, limit, pieces=(), kind=jnp.bfloat16):
    array = deviation * jax.random.normal(key, shape, jnp.float32)
    if pieces:
        array = array * shard_levels(key, shape, pieces, -0.22, 0.18)
    return jnp.clip(array, -limit, limit).astype(kind)


def setup_inputs(seed: int = 0) -> dict:
    seeds = jax.random.split(jax.random.key(seed), 6)
    frames = normal_values(seeds[0], (UTT, MAXLEN, D), 1.0, 6.0, ((0, 32),))
    lengths = uneven_parts(seeds[1], UTT, UTT * (MAXLEN * 5 // 8), MAXLEN, 1).astype(jnp.int32)
    attn_params = draw_attn_params(jax.random.fold_in(seeds[5], 71), 0)
    ffn_params = draw_ffn_params(jax.random.fold_in(seeds[5], 71), 0)
    cotangent = normal_values(seeds[4], (UTT, MAXLEN, D), 1.0, 6.0, ((0, 32),))
    return dict(frames=frames, lengths=lengths, attn_params=attn_params, ffn_params=ffn_params, cotangent=cotangent)


@jax.custom_vjp
def low(v):
    return lax.optimization_barrier(v.astype(jnp.bfloat16)).astype(jnp.float32)

@jax.custom_vjp
def low_back(v):
    return v

def low_keep(v):
    return (low(v), None)

def low_pass(kept, grad):
    return (grad,)

def back_keep(v):
    return (v, None)

def back_low(kept, grad):
    return (low(grad),)
low.defvjp(low_keep, low_pass)
low_back.defvjp(back_keep, back_low)

def matmul(left, right):
    return jnp.dot(left, right, precision=lax.Precision.HIGHEST)

def layer_norm(resid, gain, shift):
    mean = lax.optimization_barrier(jnp.mean(resid, axis=-1, keepdims=True))
    centered = resid - mean
    var = lax.optimization_barrier(jnp.mean(centered * centered, axis=-1, keepdims=True))
    return centered * lax.rsqrt(var + 1e-05) * gain + shift

def attend_one(item):
    query, keys, values, live = item
    scores = jnp.einsum('qhd,khd->hqk', query, keys, precision=lax.Precision.HIGHEST) * 0.125
    scores = low_back(scores)
    scores = jnp.where(live[None, None, :] > 0.5, scores, -1e+30)
    top = lax.optimization_barrier(jnp.max(scores, axis=-1, keepdims=True))
    expo = jnp.exp(scores - top)
    probs = low(expo / lax.optimization_barrier(jnp.sum(expo, axis=-1, keepdims=True)))
    return jnp.einsum('hqk,khd->qhd', probs, values, precision=lax.Precision.HIGHEST)

def reference(frames, lengths, attn_params, ffn_params, cotangent):
    square = D * D
    span = D * FF
    w_qkv = attn_params[:3 * square].reshape(D, 3 * D).astype(jnp.float32)
    w_out = attn_params[3 * square:4 * square].reshape(D, D).astype(jnp.float32)
    attn_vec = attn_params[4 * square:4 * square + 5 * D].reshape(5, D).astype(jnp.float32)
    w_in = ffn_params[:span].reshape(D, FF).astype(jnp.float32)
    w_fc = ffn_params[span:2 * span].reshape(FF, D).astype(jnp.float32)
    b_in = ffn_params[2 * span:2 * span + FF].astype(jnp.float32)
    ffn_vec = ffn_params[2 * span + FF:2 * span + FF + 3 * D].reshape(3, D).astype(jnp.float32)
    valid = (jnp.arange(MAXLEN, dtype=jnp.int32)[None, :] < lengths[:, None]).astype(jnp.float32)
    rows = UTT * MAXLEN

    def forward(inputs, w_qkv, w_out, attn_vec, w_in, w_fc, b_in, ffn_vec):
        flat_in = inputs.reshape(rows, D)
        bias = jnp.concatenate([attn_vec[0], jnp.zeros((D,), jnp.float32), attn_vec[1]])
        qkv = low_back(low(matmul(flat_in, w_qkv) + bias))
        query = qkv[:, :D].reshape(UTT, MAXLEN, H, DH)
        keys = qkv[:, D:2 * D].reshape(UTT, MAXLEN, H, DH)
        values = qkv[:, 2 * D:].reshape(UTT, MAXLEN, H, DH)
        mixed = lax.map(jax.checkpoint(attend_one), (query, keys, values, valid))
        mixed = low_back(low(mixed.reshape(rows, D)))
        attn_out = low_back(matmul(mixed, w_out) + attn_vec[2])
        resid1 = flat_in + attn_out
        normed1 = layer_norm(resid1, attn_vec[3], attn_vec[4])
        normed1_low = low(normed1)
        pre = low_back(matmul(normed1_low, w_in) + b_in)
        act = low(jax.nn.gelu(pre, approximate=False))
        ffn_out = low_back(matmul(act, w_fc) + ffn_vec[0])
        resid2 = normed1 + ffn_out
        result = layer_norm(resid2, ffn_vec[1], ffn_vec[2]) * valid.reshape(rows, 1)
        return result.reshape(UTT, MAXLEN, D)
    output, back = jax.vjp(forward, frames.astype(jnp.float32), w_qkv, w_out, attn_vec, w_in, w_fc, b_in, ffn_vec)
    grads = back(cotangent.astype(jnp.float32))
    attn_grad = jnp.concatenate([grads[1].reshape(-1), grads[2].reshape(-1), grads[3].reshape(-1), jnp.zeros((ATT_PAD - ATT_LEN,), jnp.float32)])
    ffn_grad = jnp.concatenate([grads[4].reshape(-1), grads[5].reshape(-1), grads[6], grads[7].reshape(-1), jnp.zeros((FFN_PAD - FFN_LEN,), jnp.float32)])
    return (output.astype(jnp.bfloat16), grads[0].astype(jnp.bfloat16), attn_grad, ffn_grad)
```

```python
from functools import partial

import jax
import jax.numpy as jnp
from jax import lax
from jax.experimental import pallas as pl
from jax.experimental.pallas import tpu as pltpu
from jax.sharding import PartitionSpec as P

D = 768
H = 12
FF = 3072
R = 768
PAIRS = 6
ATT_MAT = 4 * D * D
FFN_MAT = 2 * D * FF
ATT_VEC = 5 * D
FFN_VEC = FF + 3 * D
ATT_ROWS = 576
FFN_ROWS = 1152
VEC_ROWS = 80
AXES = ("dp", "fsdp")
bf16 = jnp.bfloat16
f32 = jnp.float32
MESH = pl.DeviceIdType.MESH

B_Q, B_V, B_OUT, G1, B1 = 0, 6, 12, 18, 24
B_IN, B_FC, G2, B2 = 32, 56, 62, 68


def nn(a, b):
    return jnp.dot(a, b, preferred_element_type=f32)


def nt(a, b):
    return lax.dot_general(a, b, (((1,), (1,)), ((), ())), preferred_element_type=f32)


def tn(a, b):
    return lax.dot_general(a, b, (((0,), (0,)), ((), ())), preferred_element_type=f32)


def split3(v):
    hi = v.astype(bf16)
    rest = v - hi.astype(f32)
    mid = rest.astype(bf16)
    return hi, mid, (rest - mid.astype(f32)).astype(bf16)


def place(chunk):
    z, x, y, c = chunk // 8, chunk // 4 % 2, chunk // 2 % 2, chunk % 2
    return z, c, (y * 2 + x if c == 0 else x * 2 + y)


def block(ref, chunk, rows):
    z, c, i = place(chunk)
    return ref[z, c, i, rows, :]


def aligned(start, size):
    return pl.ds(pl.multiple_of(start, size), size)


def w_qkv_pair(attn, i):
    blocks = [block(attn, d, aligned(i * 96, 96)) for d in range(24)]
    return jnp.concatenate(
        [jnp.concatenate([b[32 * p : 32 * p + 32] for b in blocks], axis=0) for p in range(3)], axis=1
    )


def put_w_qkv_pair(attn, i, value):
    for d in range(24):
        z, c, s = place(d)
        for p in range(3):
            attn[z, c, s, pl.ds(pl.multiple_of(i * 96 + 32 * p, 32), 32), :] = value[
                32 * d : 32 * d + 32, 128 * p : 128 * p + 128
            ]


def w_out_cols(attn, j):
    blocks = [block(attn, d, slice(192 * j, 192 * j + 192)) for d in range(24, 32)]
    return jnp.concatenate(
        [jnp.concatenate([b[96 * p : 96 * p + 96] for b in blocks], axis=0) for p in range(2)], axis=1
    )


def w_out_rows(attn, chunks):
    return jnp.concatenate(
        [
            jnp.concatenate([block(attn, d, slice(96 * j, 96 * j + 96)) for j in range(6)], axis=1)
            for d in chunks
        ],
        axis=0,
    )


def w_in_cols(ffn, j, tiles):
    blocks = [block(ffn, d, aligned(j * 48 * tiles, 48 * tiles)) for d in range(16)]
    return jnp.concatenate(
        [jnp.concatenate([b[48 * p : 48 * p + 48] for b in blocks], axis=0) for p in range(tiles)], axis=1
    )


def put_w_in_cols(ffn, j, tiles, value):
    for d in range(16):
        z, c, s = place(d)
        for p in range(tiles):
            ffn[z, c, s, pl.ds(pl.multiple_of(j * 48 * tiles + 48 * p, 48), 48), :] = value[
                48 * d : 48 * d + 48, 128 * p : 128 * p + 128
            ]


def w_fc_cols(ffn, j):
    blocks = [block(ffn, d, aligned(j * 384, 384)) for d in range(16, 32)]
    return jnp.concatenate(
        [jnp.concatenate([b[192 * p : 192 * p + 192] for b in blocks], axis=0) for p in range(2)], axis=1
    )


def chip_slot(m):
    z, x, y = 2 + m // 4, m // 2 % 2, m % 2
    return z, (y * 2 + x, x * 2 + y)


def w_fc_rows(ffn, m):
    z, at = chip_slot(m)
    return jnp.concatenate(
        [
            jnp.concatenate([ffn[z, c, at[c], 192 * j : 192 * j + 192, :] for j in range(6)], axis=1)
            for c in range(2)
        ],
        axis=0,
    )


def put_w_fc_rows(ffn, m, value):
    z, at = chip_slot(m)
    for c in range(2):
        for j in range(6):
            ffn[z, c, at[c], 192 * j : 192 * j + 192, :] = value[192 * c : 192 * c + 192, 128 * j : 128 * j + 128]


def wide(vec, row, n=6):
    return jnp.concatenate([vec[row + j : row + j + 1, :] for j in range(n)], axis=1)


def put_wide(vec, row, value):
    for j in range(value.shape[1] // 128):
        vec[row + j : row + j + 1, :] = value[:, 128 * j : 128 * j + 128]


def lane_ids():
    return lax.broadcasted_iota(jnp.int32, (R, 128), 1)


def attend_pair(qp, kp, vp, dead, lane):
    one, zero = jnp.ones((), bf16), jnp.zeros((), bf16)
    v_one = jnp.concatenate([vp, jnp.ones((R, 128), bf16)], axis=1)
    outs, augmented = [], []
    for h in range(2):
        own = (lane < 64) if h == 0 else (lane >= 64)
        e = 64 if h == 0 else 0
        qh = jnp.where(own, qp, jnp.where(lane == e, one, zero))
        kh = jnp.where(own, kp, jnp.where(lane == e, dead, zero))
        mixed, lses = [], []
        for b in range(3):
            rows = slice(256 * b, 256 * b + 256)
            s = nt(qh[rows], kh)
            top = jnp.max(s, axis=-1, keepdims=True)
            p = jnp.exp(s - top).astype(bf16)
            both = nn(p, v_one)
            total = both[:, 128:]
            mixed.append(both[:, :128] / total)
            lses.append(top + jnp.log(total))
        outs.append(jnp.concatenate(mixed, axis=0))
        hi, mid, low = split3(jnp.concatenate(lses, axis=0))
        for k, part in enumerate((hi, mid, low)):
            qh = jnp.where(lane == e + 1 + k, part, qh)
        augmented.append(qh)
    return jnp.where(lane < 64, outs[0], outs[1]), augmented


def attend_pair_back(q_aug, kp, vp, dop, mixed, dead, lane):
    zero, minus = jnp.zeros((), bf16), -jnp.ones((), bf16)
    weighted = dop.astype(f32) * mixed.astype(f32)
    k_t = kp.T
    dks, dvs, dqs = [], [], []
    for h in range(2):
        own = (lane < 64) if h == 0 else (lane >= 64)
        e = 64 if h == 0 else 0
        dot = jnp.sum(jnp.where(own, weighted, 0.0), axis=-1, keepdims=True)
        do_aug = jnp.where(own, dop, zero)
        for k, part in enumerate(split3(dot)):
            do_aug = jnp.where(lane == e + k, part, do_aug)
        v_aug = jnp.where(own, vp, jnp.where((lane >= e) & (lane < e + 3), minus, zero))
        k_aug = jnp.where(own, kp, jnp.where((lane > e) & (lane < e + 4), minus, jnp.where(lane == e, dead, zero)))
        p = jnp.exp(nt(k_aug, q_aug[h]))
        ds = (p * nt(v_aug, do_aug)).astype(bf16)
        dvs.append(nn(p.astype(bf16), dop))
        dks.append(nn(ds, q_aug[h]))
        dqs.append(nn(k_t, ds))
    row = lax.broadcasted_iota(jnp.int32, (128, R), 0)
    dq = (jnp.where(row < 64, dqs[0], dqs[1]) * 0.125).astype(bf16).T
    dk = jnp.where(lane < 64, dks[0], dks[1]).astype(bf16)
    dv = jnp.where(lane < 64, dvs[0], dvs[1]).astype(bf16)
    return dq, dk, dv


def norm_back(g, xhat, gain, rstd):
    gg = g * gain
    m1 = jnp.mean(gg, axis=-1, keepdims=True)
    m2 = jnp.mean(gg * xhat, axis=-1, keepdims=True)
    return rstd * (gg - m1 - xhat * m2)


def column_sum(v):
    return jnp.sum(v.astype(f32), axis=0, keepdims=True)


ROWS = 128
BLOCKS = R // ROWS


def layer_kernel(gather, refs):
    length = refs["length"][0]
    x, cot = refs["x"], refs["cot"]
    attn, ffn, vec, vg = refs["attn"], refs["ffn"], refs["vec"], refs["vg"]
    qx, kk, vv, mix = refs["qx"], refs["k"], refs["v"], refs["mix"]
    xh1, rs1, n1 = refs["xh1"], refs["rs1"], refs["n1"]
    act, gp, r2, gf, do = refs["act"], refs["gp"], refs["r2"], refs["gf"], refs["do"]
    out, gin = refs["out"], refs["gin"]

    def dead_keys():
        row = lax.broadcasted_iota(jnp.int32, (R, 128), 0)
        return jnp.where(row < length, 0.0, -1e30).astype(bf16)

    gather.start()

    def forward_pair(i, carry):
        gather.before_pair(i)
        lane = lane_ids()
        cols = aligned(i * 128, 128)
        bias = jnp.concatenate(
            [vec[pl.ds(B_Q + i, 1), :], jnp.zeros((1, 128), f32), vec[pl.ds(B_V + i, 1), :]], axis=1
        )
        qkv = (nn(x[...], w_qkv_pair(attn, i)) + bias).astype(bf16)
        qp, kp, vp = qkv[:, :128] * jnp.asarray(0.125, bf16), qkv[:, 128:256], qkv[:, 256:]
        kk[:, cols] = kp
        vv[:, cols] = vp
        mixed, augmented = attend_pair(qp, kp, vp, dead_keys(), lane)
        mix[:, cols] = mixed.astype(bf16)
        for h in range(2):
            qx[:, pl.ds(pl.multiple_of(i * 256 + 128 * h, 128), 128)] = augmented[h]
        return carry

    lax.fori_loop(0, PAIRS, forward_pair, 0)
    gather.step("out")
    for j in range(3):
        cols = slice(256 * j, 256 * j + 256)
        xh1[:, cols] = nn(mix[...], w_out_cols(attn, j)) + wide(vec, B_OUT + 2 * j, 2) + x[:, cols].astype(f32)

    def norm1(b, carry):
        rows = aligned(b * ROWS, ROWS)
        r = xh1[rows, :]
        cen = r - jnp.mean(r, axis=-1, keepdims=True)
        rstd = lax.rsqrt(jnp.mean(cen * cen, axis=-1, keepdims=True) + 1e-05)
        xhat = cen * rstd
        xh1[rows, :] = xhat
        rs1[rows, :] = jnp.broadcast_to(rstd, (ROWS, 128))
        n1[rows, :] = (xhat * wide(vec, G1) + wide(vec, B1)).astype(bf16)
        return carry

    lax.fori_loop(0, BLOCKS, norm1, 0)
    gather.step("norm1")

    def ffn_in(j, carry):
        gather.before_in(j)
        cols = aligned(j * 256, 256)
        bias = jnp.concatenate([vec[pl.ds(B_IN + 2 * j, 1), :], vec[pl.ds(B_IN + 2 * j + 1, 1), :]], axis=1)
        pre = nn(n1[...], w_in_cols(ffn, j, 2)) + bias
        cdf = 0.5 + 0.5 * lax.erf(pre * 0.7071067811865476)
        act[:, cols] = (pre * cdf).astype(bf16)
        gp[:, cols] = (cdf + pre * (jnp.exp(-0.5 * pre * pre) * 0.3989422804014327)).astype(bf16)
        return carry

    lax.fori_loop(0, 12, ffn_in, 0)

    def ffn_out(j, carry):
        gather.before_out(j)
        cols = aligned(j * 256, 256)
        row = lambda base: jnp.concatenate(
            [vec[pl.ds(base + 2 * j, 1), :], vec[pl.ds(base + 2 * j + 1, 1), :]], axis=1
        )
        n1_full = xh1[:, cols] * row(G1) + row(B1)
        r2[:, cols] = nn(act[...], w_fc_cols(ffn, j)) + row(B_FC) + n1_full
        return carry

    lax.fori_loop(0, 3, ffn_out, 0)
    gather.finish()

    def norm2(b, sums):
        rows = aligned(b * ROWS, ROWS)
        r = r2[rows, :]
        cen = r - jnp.mean(r, axis=-1, keepdims=True)
        rstd = lax.rsqrt(jnp.mean(cen * cen, axis=-1, keepdims=True) + 1e-05)
        xhat = cen * rstd
        row = lax.broadcasted_iota(jnp.int32, (ROWS, D), 0) + b * ROWS
        valid = jnp.where(row < length, 1.0, 0.0)
        out[rows, :] = ((xhat * wide(vec, G2) + wide(vec, B2)) * valid).astype(bf16)
        g = cot[rows, :].astype(f32) * valid
        grad = norm_back(g, xhat, wide(vec, G2), rstd)
        r2[rows, :] = grad
        low = grad.astype(bf16)
        gf[rows, :] = low
        return sums[0] + column_sum(g * xhat), sums[1] + column_sum(g), sums[2] + column_sum(low)

    zeros = jnp.zeros((1, D), f32)
    d_g2, d_b2, d_bfc = lax.fori_loop(0, BLOCKS, norm2, (zeros, zeros, zeros))
    put_wide(vg, G2, d_g2)
    put_wide(vg, B2, d_b2)
    put_wide(vg, B_FC, d_bfc)

    def back_fc(m, carry):
        cols = aligned(m * 384, 384)
        grad_act = nt(gf[...], w_fc_rows(ffn, m))
        low = (grad_act * gp[:, cols].astype(f32)).astype(bf16)
        gp[:, cols] = low
        sums = column_sum(low)
        for j in range(3):
            vg[pl.ds(B_IN + 3 * m + j, 1), :] = sums[:, 128 * j : 128 * j + 128]
        put_w_fc_rows(ffn, m, tn(act[:, cols], gf[...]).astype(bf16))
        return carry

    lax.fori_loop(0, 8, back_fc, 0)

    def back_in(j, carry):
        cols = aligned(j * 512, 512)
        g = gp[:, cols]
        r2[...] += nt(g, w_in_cols(ffn, j, 4))
        put_w_in_cols(ffn, j, 4, tn(n1[...], g).astype(bf16))
        return carry

    lax.fori_loop(0, 6, back_in, 0)

    def back_norm1(b, sums):
        rows = aligned(b * ROWS, ROWS)
        g, xhat = r2[rows, :], xh1[rows, :]
        grad = norm_back(g, xhat, wide(vec, G1), rs1[rows, 0:1])
        r2[rows, :] = grad
        low = grad.astype(bf16)
        gf[rows, :] = low
        return sums[0] + column_sum(g * xhat), sums[1] + column_sum(g), sums[2] + column_sum(low)

    d_g1, d_b1, d_bout = lax.fori_loop(0, BLOCKS, back_norm1, (zeros, zeros, zeros))
    put_wide(vg, G1, d_g1)
    put_wide(vg, B1, d_b1)
    put_wide(vg, B_OUT, d_bout)

    for half in range(2):
        do[:, 384 * half : 384 * half + 384] = nt(
            gf[...], w_out_rows(attn, range(24 + 4 * half, 28 + 4 * half))
        ).astype(bf16)
    for half in range(2):
        cols = slice(384 * half, 384 * half + 384)
        grad = tn(mix[:, cols], gf[...]).astype(bf16)
        for d in range(4):
            z, c, s = place(24 + 4 * half + d)
            for j in range(6):
                attn[z, c, s, 96 * j : 96 * j + 96, :] = grad[96 * d : 96 * d + 96, 128 * j : 128 * j + 128]

    def backward_pair(i, carry):
        lane = lane_ids()
        cols = aligned(i * 128, 128)
        q_aug = [qx[:, pl.ds(pl.multiple_of(i * 256 + 128 * h, 128), 128)] for h in range(2)]
        dq, dk, dv = attend_pair_back(q_aug, kk[:, cols], vv[:, cols], do[:, cols], mix[:, cols], dead_keys(), lane)
        vg[pl.ds(B_Q + i, 1), :] = column_sum(dq)
        vg[pl.ds(B_V + i, 1), :] = column_sum(dv)
        grad = jnp.concatenate([dq, dk, dv], axis=1)
        r2[...] += nt(grad, w_qkv_pair(attn, i))
        put_w_qkv_pair(attn, i, tn(x[...], grad).astype(bf16))
        return carry

    lax.fori_loop(0, PAIRS, backward_pair, 0)
    gin[...] = r2[...].astype(bf16)


class Loaded:
    def __init__(self, refs):
        self.refs = refs

    def start(self):
        r = self.refs
        copies = [
            pltpu.make_async_copy(r["attn_in"], r["attn"], r["sems"].at[0]),
            pltpu.make_async_copy(r["ffn_in"], r["ffn"], r["sems"].at[1]),
        ]
        for c in copies:
            c.start()
        r["vec"][...] = r["vec_in"][...].astype(f32)
        for c in copies:
            c.wait()

    def before_pair(self, i):
        pass

    before_in = before_out = step = before_pair

    def finish(self):
        pass


def position():
    dp, fs = lax.axis_index("dp"), lax.axis_index("fsdp")
    return lax.div(dp, 2), lax.rem(dp, 2), lax.div(fs, 2), lax.rem(fs, 2)


def device(z, x, y, c):
    return (z * 2 + x, y * 2 + c)


def remote(src, dst, send, recv, target):
    return pltpu.make_async_remote_copy(
        src_ref=src, dst_ref=dst, send_sem=send, recv_sem=recv, device_id=target, device_id_type=MESH
    )


GROUPS = 10


class Gather:
    def __init__(self, refs):
        self.refs = refs
        self.z, self.x, self.y, self.c = z, x, y, c = position()
        first = c == 0
        a, b = jnp.where(first, x, y), jnp.where(first, y, x)
        self.slot, self.pair = b * 2 + a, b * 2
        self.other_slot, self.other_pair = b * 2 + 1 - a, (1 - b) * 2
        self.dev_a = device(z, jnp.where(first, 1 - x, x), jnp.where(first, y, 1 - y), c)
        self.dev_b = device(z, jnp.where(first, x, 1 - x), jnp.where(first, 1 - y, y), c)
        self.dev_c = device(z, x, y, 1 - c)
        self.zs = [lax.rem(z + k, 4) for k in (1, 2, 3)]
        self.dev_z = [device(t, x, y, c) for t in self.zs]

    def barrier(self):
        bar = pltpu.get_barrier_semaphore()
        targets = [self.dev_a, self.dev_b, self.dev_c] + self.dev_z
        for t in targets:
            pl.semaphore_signal(bar, inc=1, device_id=t, device_id_type=MESH)
        pl.semaphore_wait(bar, len(targets))

    def part(self, g):
        if isinstance(g, int) and g >= PAIRS:
            n = g - PAIRS
            return self.refs["ffn"], (slice(0, 2) if n < 2 else slice(2, 4)), slice(576 * (n % 2), 576 * (n % 2) + 576)
        return self.refs["attn"], slice(0, 4), aligned(g * 96, 96)

    def send_z(self, g):
        buf, zz, rows = self.part(g)
        own = self.refs["own_a"] if buf is self.refs["attn"] else self.refs["own_f"]
        r = self.refs

        def go():
            dst = buf.at[self.z, self.c, self.slot, rows]
            pltpu.make_async_copy(own.at[rows], dst, r["own_sem"].at[g]).start()
            for k in range(3):
                remote(own.at[rows], dst, r["zs"].at[g, k], r["zr"].at[g, k], self.dev_z[k]).start()

        self.if_in(zz, go)

    def if_in(self, zz, fn):
        if zz == slice(0, 4):
            fn()
        else:
            pl.when((self.z >= zz.start) & (self.z < zz.stop))(fn)

    def relay_a(self, g):
        buf, zz, rows = self.part(g)
        r = self.refs
        one = buf.at[self.z, self.c, self.slot, rows]
        own = self.refs["own_a"] if buf is self.refs["attn"] else self.refs["own_f"]
        self.if_in(zz, lambda: pltpu.make_async_copy(own.at[rows], one, r["own_sem"].at[g]).wait())
        for k in range(3):
            source = lax.rem(self.z + 3 - k, 4)

            def got(k=k, source=source):
                dst = buf.at[source, self.c, self.slot, rows]
                remote(dst, dst, r["zs"].at[g, k], r["zr"].at[g, k], self.dev_z[k]).wait_recv()

            if zz == slice(0, 4):
                got()
            else:
                pl.when((source >= zz.start) & (source < zz.stop))(got)
        mine = buf.at[zz, self.c, self.slot, rows]
        remote(mine, mine, r["as"].at[g], r["ar"].at[g], self.dev_a).start()

    def relay_b(self, g):
        buf, zz, rows = self.part(g)
        r = self.refs
        got = buf.at[zz, self.c, self.other_slot, rows]
        remote(got, got, r["as"].at[g], r["ar"].at[g], self.dev_a).wait_recv()
        mine = buf.at[zz, self.c, pl.ds(self.pair, 2), rows]
        remote(mine, mine, r["bs"].at[g], r["br"].at[g], self.dev_b).start()

    def relay_c(self, g):
        buf, zz, rows = self.part(g)
        r = self.refs
        got = buf.at[zz, self.c, pl.ds(self.other_pair, 2), rows]
        remote(got, got, r["bs"].at[g], r["br"].at[g], self.dev_b).wait_recv()
        mine = buf.at[zz, self.c, :, rows]
        remote(mine, mine, r["cs"].at[g], r["cr"].at[g], self.dev_c).start()

    def ready(self, g):
        buf, zz, rows = self.part(g)
        r = self.refs
        got = buf.at[zz, 1 - self.c, :, rows]
        remote(got, got, r["cs"].at[g], r["cr"].at[g], self.dev_c).wait_recv()

    def vectors(self, stage):
        r = self.refs
        buf, own = r["vec_all"], r["own_v"]
        one = buf.at[self.c, self.slot]
        if stage == 0:

            @pl.when(self.z == 3)
            def _():
                pltpu.make_async_copy(own, one, r["vsem"].at[0]).start()
                for k in range(3):
                    remote(own, one, r["vsem"].at[4 + k], r["vsem"].at[1], self.dev_z[k]).start()

        elif stage == 1:

            @pl.when(self.z == 3)
            def _():
                pltpu.make_async_copy(own, one, r["vsem"].at[0]).wait()
                for k in range(3):
                    remote(own, one, r["vsem"].at[4 + k], r["vsem"].at[1], self.dev_z[k]).wait_send()

            @pl.when(self.z != 3)
            def _():
                remote(one, one, r["vsem"].at[4], r["vsem"].at[1], self.dev_z[0]).wait_recv()

            remote(one, one, r["vsem"].at[7], r["vsem"].at[2], self.dev_a).start()
        elif stage == 2:
            got = buf.at[self.c, self.other_slot]
            remote(got, got, r["vsem"].at[7], r["vsem"].at[2], self.dev_a).wait()
            mine = buf.at[self.c, pl.ds(self.pair, 2)]
            remote(mine, mine, r["vsem"].at[8], r["vsem"].at[3], self.dev_b).start()
        elif stage == 3:
            got = buf.at[self.c, pl.ds(self.other_pair, 2)]
            remote(got, got, r["vsem"].at[8], r["vsem"].at[3], self.dev_b).wait()
            mine = buf.at[self.c]
            remote(mine, mine, r["vsem"].at[9], r["vsem"].at[10], self.dev_c).start()
        else:
            got = buf.at[1 - self.c]
            remote(got, got, r["vsem"].at[9], r["vsem"].at[10], self.dev_c).wait()
            r["vec"][...] = buf[1, 3].astype(f32)

    def start(self):
        self.barrier()
        self.vectors(0)
        for g in range(GROUPS):
            self.send_z(g)
        self.vectors(1)
        self.relay_a(0)
        self.vectors(2)
        self.relay_b(0)
        self.relay_a(1)
        self.vectors(3)
        self.relay_c(0)
        self.relay_b(1)
        self.relay_a(2)
        self.vectors(4)

    def before_pair(self, i):
        @pl.when(i + 3 < PAIRS)
        def _():
            self.relay_a(i + 3)

        @pl.when(i + 2 < PAIRS)
        def _():
            self.relay_b(i + 2)

        @pl.when(i + 1 < PAIRS)
        def _():
            self.relay_c(i + 1)

        @pl.when(i == 3)
        def _():
            self.relay_a(6)

        @pl.when(i == 4)
        def _():
            self.relay_b(6)

        @pl.when(i == 5)
        def _():
            self.relay_a(7)

        self.ready(i)

    def step(self, name):
        if name == "out":
            self.relay_c(6)
            self.relay_b(7)
            self.relay_a(8)
        elif name == "norm1":
            self.ready(6)

    def before_in(self, j):
        @pl.when(j == 2)
        def _():
            self.relay_c(7)
            self.relay_b(8)
            self.relay_a(9)

        @pl.when(j == 6)
        def _():
            self.ready(7)

        @pl.when(j == 9)
        def _():
            self.relay_c(8)
            self.relay_b(9)

    def before_out(self, j):
        @pl.when(j == 0)
        def _():
            self.ready(8)
            self.relay_c(9)
            self.ready(9)

    def finish(self):
        r = self.refs
        for g in range(GROUPS):
            buf, zz, rows = self.part(g)
            own = r["own_a"] if buf is r["attn"] else r["own_f"]

            def sent(g=g, own=own, rows=rows, buf=buf):
                dst = buf.at[self.z, self.c, self.slot, rows]
                for k in range(3):
                    remote(own.at[rows], dst, r["zs"].at[g, k], r["zr"].at[g, k], self.dev_z[k]).wait_send()

            self.if_in(zz, sent)
            for refs, s, v, t in (
                (buf.at[zz, self.c, self.slot, rows], "as", "ar", self.dev_a),
                (buf.at[zz, self.c, pl.ds(self.pair, 2), rows], "bs", "br", self.dev_b),
                (buf.at[zz, self.c, :, rows], "cs", "cr", self.dev_c),
            ):
                remote(refs, refs, r[s].at[g], r[v].at[g], t).wait_send()


SCRATCH = dict(
    attn=((4, 2, 4, ATT_ROWS, 128), bf16),
    ffn=((4, 2, 4, FFN_ROWS, 128), bf16),
    vec=((VEC_ROWS, 128), f32),
    qx=((R, 1536), bf16),
    k=((R, D), bf16),
    v=((R, D), bf16),
    mix=((R, D), bf16),
    xh1=((R, D), f32),
    rs1=((R, 128), f32),
    n1=((R, D), bf16),
    act=((R, FF), bf16),
    gp=((R, FF), bf16),
    r2=((R, D), f32),
    gf=((R, D), bf16),
    do=((R, D), bf16),
)


def run_layer(linked, length, x, cot, attn_in, ffn_in, vec_in):
    dma = pltpu.SemaphoreType.DMA
    vmem, anywhere = pl.BlockSpec(memory_space=pltpu.VMEM), pl.BlockSpec(memory_space=pl.ANY)
    names = ["length", "x", "cot"] + (["own_a", "own_f", "own_v"] if linked else ["attn_in", "ffn_in", "vec_in"])
    names += ["out", "gin", "attn_g", "ffn_g", "vg"]
    scratch = [pltpu.VMEM(*s) for s in SCRATCH.values()]
    names += list(SCRATCH)
    if linked:
        sems = dict(
            vec_all=pltpu.VMEM((2, 4, VEC_ROWS, 128), bf16),
            own_sem=dma((GROUPS,)),
            zs=dma((GROUPS, 3)),
            zr=dma((GROUPS, 3)),
            vsem=dma((11,)),
            **{k: dma((GROUPS,)) for k in ("as", "ar", "bs", "br", "cs", "cr")},
        )
    else:
        sems = {}
    sems["sems"] = dma((2,))
    scratch += list(sems.values())
    names += list(sems)

    def body(*args):
        refs = dict(zip(names, args, strict=True))
        refs["vg"][...] = jnp.zeros((VEC_ROWS, 128), f32)
        layer_kernel((Gather if linked else Loaded)(refs), refs)
        copies = [
            pltpu.make_async_copy(refs["attn"], refs["attn_g"], refs["sems"].at[0]),
            pltpu.make_async_copy(refs["ffn"], refs["ffn_g"], refs["sems"].at[1]),
        ]
        for c in copies:
            c.start()
        for c in copies:
            c.wait()

    big = anywhere if not linked else vmem
    return pl.pallas_call(
        body,
        out_shape=(
            jax.ShapeDtypeStruct((R, D), bf16),
            jax.ShapeDtypeStruct((R, D), bf16),
            jax.ShapeDtypeStruct(SCRATCH["attn"][0], bf16),
            jax.ShapeDtypeStruct(SCRATCH["ffn"][0], bf16),
            jax.ShapeDtypeStruct((VEC_ROWS, 128), f32),
        ),
        in_specs=[pl.BlockSpec(memory_space=pltpu.SMEM), vmem, vmem, big, big, vmem],
        out_specs=(vmem, vmem, anywhere, anywhere, vmem),
        scratch_shapes=scratch,
        compiler_params=pltpu.CompilerParams(
            vmem_limit_bytes=64 * 1024 * 1024 - 65536,
            has_side_effects=True,
            **(dict(collective_id=0) if linked else {}),
        ),
    )(length, x, cot, attn_in, ffn_in, vec_in)


def qkv_chunk(flat):
    return flat.reshape(-1, 32, 3, 6, 128).transpose(0, 3, 2, 1, 4).reshape(-1, ATT_ROWS, 128)


def qkv_flat(chunk):
    return chunk.reshape(-1, 6, 3, 32, 128).transpose(0, 3, 2, 1, 4).reshape(-1)


def tiled_chunk(flat, rows, tiles):
    return flat.reshape(-1, rows, tiles, 128).transpose(0, 2, 1, 3).reshape(-1, rows * tiles, 128)


def tiled_flat(chunk, rows, tiles):
    return chunk.reshape(-1, tiles, rows, 128).transpose(0, 2, 1, 3).reshape(-1)


def pack_vectors(attn_vec, ffn_vec):
    return jnp.concatenate(
        [
            attn_vec.reshape(30, 128),
            jnp.zeros((2, 128), attn_vec.dtype),
            ffn_vec.reshape(42, 128),
            jnp.zeros((6, 128), attn_vec.dtype),
        ]
    )


def shards_linked(frames, lengths, attn_params, ffn_params, cotangent):
    me = lax.axis_index("dp") * 4 + lax.axis_index("fsdp")
    z = me // 8
    tails = jnp.concatenate([attn_params[-ATT_VEC:], ffn_params[-FFN_VEC:]])
    before = lax.ppermute(tails, AXES, [(i, i + 1) for i in range(31)])
    a = lax.dynamic_slice(
        jnp.concatenate([before[:ATT_VEC], attn_params]), (ATT_VEC - 120 * me,), (ATT_ROWS * 128,)
    )
    f = lax.dynamic_slice(
        jnp.concatenate([before[ATT_VEC:], ffn_params]), (FFN_VEC - 168 * me,), (FFN_ROWS * 128,)
    )
    own_a = jnp.where(z == 3, tiled_chunk(a, 96, 6)[0], qkv_chunk(a)[0])
    own_f = jnp.where(z >= 2, tiled_chunk(f, 192, 6)[0], tiled_chunk(f, 48, 24)[0])
    own_v = pack_vectors(tails[:ATT_VEC], tails[ATT_VEC:])
    out, gin, attn_g, ffn_g, vg = run_layer(True, lengths, frames[0], cotangent[0], own_a, own_f, own_v)

    def scatter(g):
        p0 = g[:, 0].reshape(4, 2, 2, -1, 128).transpose(0, 2, 1, 3, 4)
        p1 = g[:, 1].reshape(4, 2, 2, -1, 128)
        chunks = jnp.stack([p0, p1], axis=3).reshape(32, -1, 128)
        return lax.psum_scatter(chunks.astype(f32), AXES, scatter_dimension=0, tiled=True)[0]

    ga, gfn, vsum = scatter(attn_g), scatter(ffn_g), lax.psum(vg, AXES)
    a = jnp.where(z == 3, tiled_flat(ga, 96, 6), qkv_flat(ga))
    f = jnp.where(z >= 2, tiled_flat(gfn, 192, 6), tiled_flat(gfn, 48, 24))
    heads = jnp.concatenate([a[:ATT_VEC], f[:FFN_VEC]])
    vecs = jnp.concatenate([vsum[:30].reshape(-1), vsum[32:74].reshape(-1)])
    after = jnp.where(me == 31, vecs, lax.ppermute(heads, AXES, [(i + 1, i) for i in range(31)]))
    attn_grad = lax.dynamic_slice(jnp.concatenate([a, after[:ATT_VEC]]), (120 * me,), attn_params.shape)
    ffn_grad = lax.dynamic_slice(jnp.concatenate([f, after[ATT_VEC:]]), (168 * me,), ffn_params.shape)
    return out[None], gin[None], attn_grad, ffn_grad


def in_places(chunks):
    g = chunks.reshape(4, 2, 2, 2, -1, 128)
    p0 = g[:, :, :, 0].transpose(0, 2, 1, 3, 4).reshape(4, 4, -1, 128)
    p1 = g[:, :, :, 1].reshape(4, 4, -1, 128)
    return jnp.stack([p0, p1], axis=1)


def from_places(g):
    p0 = g[:, 0].reshape(4, 2, 2, -1, 128).transpose(0, 2, 1, 3, 4)
    p1 = g[:, 1].reshape(4, 2, 2, -1, 128)
    return jnp.stack([p0, p1], axis=3).reshape(32, -1, 128)


def shards_any(frames, lengths, attn_params, ffn_params, cotangent):
    devices = lax.axis_size(AXES)
    attn_flat = lax.all_gather(attn_params, AXES, axis=0, tiled=True)
    ffn_flat = lax.all_gather(ffn_params, AXES, axis=0, tiled=True)
    cut_a, cut_f = 3 * D * D, D * FF
    attn_in = in_places(
        jnp.concatenate([qkv_chunk(attn_flat[:cut_a]), tiled_chunk(attn_flat[cut_a:ATT_MAT], 96, 6)])
    )
    ffn_in = in_places(
        jnp.concatenate([tiled_chunk(ffn_flat[:cut_f], 48, 24), tiled_chunk(ffn_flat[cut_f:FFN_MAT], 192, 6)])
    )
    vec_in = pack_vectors(attn_flat[ATT_MAT : ATT_MAT + ATT_VEC], ffn_flat[FFN_MAT : FFN_MAT + FFN_VEC])
    outs, gins, sums = [], [], None
    for u in range(frames.shape[0]):
        out, gin, *grads = run_layer(False, lengths[u : u + 1], frames[u], cotangent[u], attn_in, ffn_in, vec_in)
        outs.append(out)
        gins.append(gin)
        grads = [g.astype(f32) for g in grads]
        sums = grads if sums is None else [s + g for s, g in zip(sums, grads)]
    attn_c, ffn_c = from_places(sums[0]), from_places(sums[1])
    pad_a = attn_params.shape[0] * devices - ATT_MAT - ATT_VEC
    pad_f = ffn_params.shape[0] * devices - FFN_MAT - FFN_VEC
    attn_terms = jnp.concatenate(
        [qkv_flat(attn_c[:24]), tiled_flat(attn_c[24:], 96, 6), sums[2][:30].reshape(-1), jnp.zeros((pad_a,), f32)]
    )
    ffn_terms = jnp.concatenate(
        [
            tiled_flat(ffn_c[:16], 48, 24),
            tiled_flat(ffn_c[16:], 192, 6),
            sums[2][32:74].reshape(-1),
            jnp.zeros((pad_f,), f32),
        ]
    )
    attn_grad = lax.psum_scatter(attn_terms, AXES, scatter_dimension=0, tiled=True)
    ffn_grad = lax.psum_scatter(ffn_terms, AXES, scatter_dimension=0, tiled=True)
    return jnp.stack(outs), jnp.stack(gins), attn_grad, ffn_grad


def solution(mesh):
    linked = tuple(mesh.shape[a] for a in AXES) == (8, 4)
    return jax.shard_map(
        shards_linked if linked else shards_any,
        mesh=mesh,
        in_specs=(P(AXES, None, None), P(AXES), P(AXES), P(AXES), P(AXES, None, None)),
        out_specs=(P(AXES, None, None), P(AXES, None, None), P(AXES), P(AXES)),
        check_vma=False,
    )
```

```python
from functools import partial

import jax
import jax.numpy as jnp
from jax import lax
from jax.experimental import pallas as pl
from jax.experimental.pallas import tpu as pltpu
from jax.sharding import PartitionSpec as P

D = 768
H = 12
FF = 3072
R = 768
PAIRS = 6
ATT_MAT = 4 * D * D
FFN_MAT = 2 * D * FF
ATT_VEC = 5 * D
FFN_VEC = FF + 3 * D
ATT_ROWS = 576
FFN_ROWS = 1152
VEC_ROWS = 80
AXES = ("dp", "fsdp")
bf16 = jnp.bfloat16
f32 = jnp.float32
MESH = pl.DeviceIdType.MESH

B_Q, B_V, B_OUT, G1, B1 = 0, 6, 12, 18, 24
B_IN, B_FC, G2, B2 = 32, 56, 62, 68


def nn(a, b):
    return jnp.dot(a, b, preferred_element_type=f32)


def nt(a, b):
    return lax.dot_general(a, b, (((1,), (1,)), ((), ())), preferred_element_type=f32)


def tn(a, b):
    return lax.dot_general(a, b, (((0,), (0,)), ((), ())), preferred_element_type=f32)


def split3(v):
    hi = v.astype(bf16)
    rest = v - hi.astype(f32)
    mid = rest.astype(bf16)
    return hi, mid, (rest - mid.astype(f32)).astype(bf16)


def place(chunk):
    z, x, y, c = chunk // 8, chunk // 4 % 2, chunk // 2 % 2, chunk % 2
    return z, c, (y * 2 + x if c == 0 else x * 2 + y)


def block(ref, chunk, rows):
    z, c, i = place(chunk)
    return ref[z, c, i, rows, :]


def aligned(start, size):
    return pl.ds(pl.multiple_of(start, size), size)


def w_qkv_pair(attn, i):
    blocks = [block(attn, d, aligned(i * 96, 96)) for d in range(24)]
    return jnp.concatenate(
        [jnp.concatenate([b[32 * p : 32 * p + 32] for b in blocks], axis=0) for p in range(3)], axis=1
    )


def put_w_qkv_pair(attn, i, value):
    for d in range(24):
        z, c, s = place(d)
        for p in range(3):
            attn[z, c, s, pl.ds(pl.multiple_of(i * 96 + 32 * p, 32), 32), :] = value[
                32 * d : 32 * d + 32, 128 * p : 128 * p + 128
            ]


def w_qkv_rows(attn, chunks, part):
    return jnp.concatenate(
        [
            jnp.concatenate(
                [block(attn, d, slice(96 * i + 32 * part, 96 * i + 32 * part + 32)) for i in range(PAIRS)], axis=1
            )
            for d in chunks
        ],
        axis=0,
    )


def w_out_cols(attn, j):
    blocks = [block(attn, d, slice(192 * j, 192 * j + 192)) for d in range(24, 32)]
    return jnp.concatenate(
        [jnp.concatenate([b[96 * p : 96 * p + 96] for b in blocks], axis=0) for p in range(2)], axis=1
    )


def w_out_rows(attn, chunks):
    return jnp.concatenate(
        [
            jnp.concatenate([block(attn, d, slice(96 * j, 96 * j + 96)) for j in range(6)], axis=1)
            for d in chunks
        ],
        axis=0,
    )


def w_in_cols(ffn, j, tiles):
    blocks = [block(ffn, d, aligned(j * 48 * tiles, 48 * tiles)) for d in range(16)]
    return jnp.concatenate(
        [jnp.concatenate([b[48 * p : 48 * p + 48] for b in blocks], axis=0) for p in range(tiles)], axis=1
    )


def put_w_in_cols(ffn, j, tiles, value):
    for d in range(16):
        z, c, s = place(d)
        for p in range(tiles):
            ffn[z, c, s, pl.ds(pl.multiple_of(j * 48 * tiles + 48 * p, 48), 48), :] = value[
                48 * d : 48 * d + 48, 128 * p : 128 * p + 128
            ]


def w_fc_cols(ffn, j):
    blocks = [block(ffn, d, aligned(j * 384, 384)) for d in range(16, 32)]
    return jnp.concatenate(
        [jnp.concatenate([b[192 * p : 192 * p + 192] for b in blocks], axis=0) for p in range(2)], axis=1
    )


def chip_slot(m):
    z, x, y = 2 + m // 4, m // 2 % 2, m % 2
    return z, (y * 2 + x, x * 2 + y)


def w_fc_rows(ffn, m):
    z, at = chip_slot(m)
    return jnp.concatenate(
        [
            jnp.concatenate([ffn[z, c, at[c], 192 * j : 192 * j + 192, :] for j in range(6)], axis=1)
            for c in range(2)
        ],
        axis=0,
    )


def put_w_fc_rows(ffn, m, value):
    z, at = chip_slot(m)
    for c in range(2):
        for j in range(6):
            ffn[z, c, at[c], 192 * j : 192 * j + 192, :] = value[192 * c : 192 * c + 192, 128 * j : 128 * j + 128]


def wide(vec, row, n=6):
    return jnp.concatenate([vec[row + j : row + j + 1, :] for j in range(n)], axis=1)


def put_wide(vec, row, value):
    for j in range(value.shape[1] // 128):
        vec[row + j : row + j + 1, :] = value[:, 128 * j : 128 * j + 128]


def lane_ids():
    return lax.broadcasted_iota(jnp.int32, (R, 128), 1)


def attend_pair(qp, kp, vp, dead, lane):
    one, zero = jnp.ones((), bf16), jnp.zeros((), bf16)
    v_one = jnp.concatenate([vp, jnp.ones((R, 128), bf16)], axis=1)
    outs, augmented = [], []
    for h in range(2):
        own = (lane < 64) if h == 0 else (lane >= 64)
        e = 64 if h == 0 else 0
        qh = jnp.where(own, qp, jnp.where(lane == e, one, zero))
        kh = jnp.where(own, kp, jnp.where(lane == e, dead, zero))
        mixed, lses = [], []
        for b in range(3):
            rows = slice(256 * b, 256 * b + 256)
            s = nt(qh[rows], kh)
            top = jnp.max(s, axis=-1, keepdims=True)
            p = jnp.exp(s - top).astype(bf16)
            both = nn(p, v_one)
            total = both[:, 128:]
            mixed.append(both[:, :128] / total)
            lses.append(top + jnp.log(total))
        outs.append(jnp.concatenate(mixed, axis=0))
        hi, mid, low = split3(jnp.concatenate(lses, axis=0))
        for k, part in enumerate((hi, mid, low)):
            qh = jnp.where(lane == e + 1 + k, part, qh)
        augmented.append(qh)
    return jnp.where(lane < 64, outs[0], outs[1]), augmented


def attend_pair_back(q_aug, kp, vp, dop, mixed, dead, lane):
    zero, minus = jnp.zeros((), bf16), -jnp.ones((), bf16)
    weighted = dop.astype(f32) * mixed.astype(f32)
    k_t = kp.T
    dks, dvs, dqs = [], [], []
    for h in range(2):
        own = (lane < 64) if h == 0 else (lane >= 64)
        e = 64 if h == 0 else 0
        dot = jnp.sum(jnp.where(own, weighted, 0.0), axis=-1, keepdims=True)
        do_aug = jnp.where(own, dop, zero)
        for k, part in enumerate(split3(dot)):
            do_aug = jnp.where(lane == e + k, part, do_aug)
        v_aug = jnp.where(own, vp, jnp.where((lane >= e) & (lane < e + 3), minus, zero))
        k_aug = jnp.where(own, kp, jnp.where((lane > e) & (lane < e + 4), minus, jnp.where(lane == e, dead, zero)))
        p = jnp.exp(nt(k_aug, q_aug[h]))
        ds = (p * nt(v_aug, do_aug)).astype(bf16)
        dvs.append(nn(p.astype(bf16), dop))
        dks.append(nn(ds, q_aug[h]))
        dqs.append(nn(k_t, ds))
    row = lax.broadcasted_iota(jnp.int32, (128, R), 0)
    dq = (jnp.where(row < 64, dqs[0], dqs[1]) * 0.125).astype(bf16).T
    dk = jnp.where(lane < 64, dks[0], dks[1]).astype(bf16)
    dv = jnp.where(lane < 64, dvs[0], dvs[1]).astype(bf16)
    return dq, dk, dv


def norm_back(g, xhat, gain, rstd):
    gg = g * gain
    m1 = jnp.mean(gg, axis=-1, keepdims=True)
    m2 = jnp.mean(gg * xhat, axis=-1, keepdims=True)
    return rstd * (gg - m1 - xhat * m2)


def column_sum(v):
    return jnp.sum(v.astype(f32), axis=0, keepdims=True)


ROWS = 128
BLOCKS = R // ROWS


def layer_kernel(gather, scatter, refs):
    length = refs["length"][0]
    x, io = refs["x"], refs["io"]

    def cot_copy(b):
        slot = lax.rem(b, 2)
        return pltpu.make_async_copy(refs["cot"].at[aligned(b * ROWS, ROWS)], refs["cot_b"].at[slot], io.at[6 + slot])

    def out_copy(b):
        slot = lax.rem(b, 2)
        return pltpu.make_async_copy(refs["out_b"].at[slot], refs["out"].at[aligned(b * ROWS, ROWS)], io.at[8 + slot])

    x_copy = pltpu.make_async_copy(refs["x_in"], x, io.at[0])
    x_copy.start()
    cot_copy(0).start()
    attn, ffn, vec, vg = refs["attn"], refs["ffn"], refs["vec"], refs["vg"]
    qx, kk, vv = refs["qx"], refs["k"], refs["v"]
    xh1, rs1, n1 = refs["xh1"], refs["rs1"], refs["n1"]
    act, gp, r2, gf = refs["act"], refs["gp"], refs["r2"], refs["gf"]
    do, mix = n1, refs["mix"]

    def dead_keys():
        row = lax.broadcasted_iota(jnp.int32, (R, 128), 0)
        return jnp.where(row < length, 0.0, -1e30).astype(bf16)

    gather.start()
    x_copy.wait()

    def forward_pair(i, carry):
        gather.before_pair(i)
        lane = lane_ids()
        cols = aligned(i * 128, 128)
        bias = jnp.concatenate(
            [vec[pl.ds(B_Q + i, 1), :], jnp.zeros((1, 128), f32), vec[pl.ds(B_V + i, 1), :]], axis=1
        )
        qkv = (nn(x[...], w_qkv_pair(attn, i)) + bias).astype(bf16)
        qp, kp, vp = qkv[:, :128] * jnp.asarray(0.125, bf16), qkv[:, 128:256], qkv[:, 256:]
        kk[:, cols] = kp
        vv[:, cols] = vp
        mixed, augmented = attend_pair(qp, kp, vp, dead_keys(), lane)
        mix[:, cols] = mixed.astype(bf16)
        for h in range(2):
            qx[:, pl.ds(pl.multiple_of(i * 256 + 128 * h, 128), 128)] = augmented[h]
        return carry

    lax.fori_loop(0, PAIRS, forward_pair, 0)
    gather.step(0)
    for j in range(3):
        cols = slice(256 * j, 256 * j + 256)
        xh1[:, cols] = nn(mix[...], w_out_cols(attn, j)) + wide(vec, B_OUT + 2 * j, 2) + x[:, cols].astype(f32)

    def norm1(b, carry):
        rows = aligned(b * ROWS, ROWS)
        r = xh1[rows, :]
        cen = r - jnp.mean(r, axis=-1, keepdims=True)
        rstd = lax.rsqrt(jnp.mean(cen * cen, axis=-1, keepdims=True) + 1e-05)
        xhat = cen * rstd
        xh1[rows, :] = xhat
        rs1[rows, :] = jnp.broadcast_to(rstd, (ROWS, 128))
        n1[rows, :] = (xhat * wide(vec, G1) + wide(vec, B1)).astype(bf16)
        return carry

    gather.step(1)
    lax.fori_loop(0, BLOCKS, norm1, 0)

    def ffn_in(j, carry):
        gather.before_in(j)
        cols = aligned(j * 256, 256)
        bias = jnp.concatenate([vec[pl.ds(B_IN + 2 * j, 1), :], vec[pl.ds(B_IN + 2 * j + 1, 1), :]], axis=1)
        pre = nn(n1[...], w_in_cols(ffn, j, 2)) + bias
        cdf = 0.5 + 0.5 * lax.erf(pre * 0.7071067811865476)
        act[:, cols] = (pre * cdf).astype(bf16)
        gp[:, cols] = (cdf + pre * (jnp.exp(-0.5 * pre * pre) * 0.3989422804014327)).astype(bf16)
        return carry

    lax.fori_loop(0, 12, ffn_in, 0)

    def ffn_out(j, carry):
        gather.before_out(j)
        cols = aligned(j * 256, 256)
        row = lambda base: jnp.concatenate(
            [vec[pl.ds(base + 2 * j, 1), :], vec[pl.ds(base + 2 * j + 1, 1), :]], axis=1
        )
        n1_full = xh1[:, cols] * row(G1) + row(B1)
        r2[:, cols] = nn(act[...], w_fc_cols(ffn, j)) + row(B_FC) + n1_full
        return carry

    lax.fori_loop(0, 3, ffn_out, 0)
    gather.finish()

    def norm2(b, sums):
        rows = aligned(b * ROWS, ROWS)
        r = r2[rows, :]
        cen = r - jnp.mean(r, axis=-1, keepdims=True)
        rstd = lax.rsqrt(jnp.mean(cen * cen, axis=-1, keepdims=True) + 1e-05)
        xhat = cen * rstd
        pl.when(b + 1 < BLOCKS)(lambda: cot_copy(b + 1).start())
        cot_copy(b).wait()
        pl.when(b >= 2)(lambda: out_copy(b - 2).wait())
        row = lax.broadcasted_iota(jnp.int32, (ROWS, D), 0) + b * ROWS
        valid = jnp.where(row < length, 1.0, 0.0)
        slot = lax.rem(b, 2)
        refs["out_b"][slot] = ((xhat * wide(vec, G2) + wide(vec, B2)) * valid).astype(bf16)
        out_copy(b).start()
        g = refs["cot_b"][slot].astype(f32) * valid
        grad = norm_back(g, xhat, wide(vec, G2), rstd)
        r2[rows, :] = grad
        low = grad.astype(bf16)
        gf[rows, :] = low
        return sums[0] + column_sum(g * xhat), sums[1] + column_sum(g), sums[2] + column_sum(low)

    zeros = jnp.zeros((1, D), f32)
    d_g2, d_b2, d_bfc = lax.fori_loop(0, BLOCKS, norm2, (zeros, zeros, zeros))
    for b in (BLOCKS - 2, BLOCKS - 1):
        out_copy(b).wait()
    put_wide(vg, G2, d_g2)
    put_wide(vg, B2, d_b2)
    put_wide(vg, B_FC, d_bfc)

    def back_fc(m, carry):
        scatter.in_fc(m)
        cols = aligned(m * 384, 384)
        grad_act = nt(gf[...], w_fc_rows(ffn, m))
        low = (grad_act * gp[:, cols].astype(f32)).astype(bf16)
        gp[:, cols] = low
        sums = column_sum(low)
        for j in range(3):
            vg[pl.ds(B_IN + 3 * m + j, 1), :] = sums[:, 128 * j : 128 * j + 128]
        put_w_fc_rows(ffn, m, tn(act[:, cols], gf[...]).astype(bf16))
        return carry

    lax.fori_loop(0, 8, back_fc, 0)

    def back_in(j, carry):
        scatter.in_in(j)
        cols = aligned(j * 512, 512)
        g = gp[:, cols]
        r2[...] += nt(g, w_in_cols(ffn, j, 4))
        put_w_in_cols(ffn, j, 4, tn(n1[...], g).astype(bf16))
        return carry

    lax.fori_loop(0, 6, back_in, 0)
    scatter.between(0)

    def back_norm1(b, sums):
        rows = aligned(b * ROWS, ROWS)
        g, xhat = r2[rows, :], xh1[rows, :]
        grad = norm_back(g, xhat, wide(vec, G1), rs1[rows, 0:1])
        r2[rows, :] = grad
        low = grad.astype(bf16)
        gf[rows, :] = low
        return sums[0] + column_sum(g * xhat), sums[1] + column_sum(g), sums[2] + column_sum(low)

    d_g1, d_b1, d_bout = lax.fori_loop(0, BLOCKS, back_norm1, (zeros, zeros, zeros))
    put_wide(vg, G1, d_g1)
    put_wide(vg, B1, d_b1)
    put_wide(vg, B_OUT, d_bout)
    scatter.between(1)

    for half in range(2):
        do[:, 384 * half : 384 * half + 384] = nt(
            gf[...], w_out_rows(attn, range(24 + 4 * half, 28 + 4 * half))
        ).astype(bf16)
    scatter.between(2)
    for half in range(2):
        cols = slice(384 * half, 384 * half + 384)
        grad = tn(mix[:, cols], gf[...]).astype(bf16)
        for d in range(4):
            z, c, s = place(24 + 4 * half + d)
            for j in range(6):
                attn[z, c, s, 96 * j : 96 * j + 96, :] = grad[96 * d : 96 * d + 96, 128 * j : 128 * j + 128]

    def backward_pair(i, carry):
        scatter.pair_start(i)
        lane = lane_ids()
        cols = aligned(i * 128, 128)
        q_aug = [qx[:, pl.ds(pl.multiple_of(i * 256 + 128 * h, 128), 128)] for h in range(2)]
        dq, dk, dv = attend_pair_back(
            q_aug, kk[:, cols], vv[:, cols], do[:, cols], mix[:, cols], dead_keys(), lane
        )
        do[:, cols] = dq
        kk[:, cols] = dk
        vv[:, cols] = dv
        scatter.pair_end(i)
        vg[pl.ds(B_Q + i, 1), :] = column_sum(dq)
        vg[pl.ds(B_V + i, 1), :] = column_sum(dv)
        put_w_qkv_pair(refs["qkv_g"], i, tn(x[...], jnp.concatenate([dq, dk, dv], axis=1)).astype(bf16))
        return carry

    lax.fori_loop(0, PAIRS, backward_pair, 0)
    gin_copies = []
    for n in range(3):
        scatter.tail(n)
        cols = slice(256 * n, 256 * n + 256)
        total = r2[:, cols]
        for p, g in enumerate((do, kk, vv)):
            total = total + nt(g[...], w_qkv_rows(attn, range(8 * n, 8 * n + 8), p))
        mix[:, cols] = total.astype(bf16)
        gin_copies.append(pltpu.make_async_copy(mix.at[:, cols], refs["gin"].at[:, cols], io.at[1 + n]))
        gin_copies[-1].start()
    scatter.tail(3)
    for copy in gin_copies:
        copy.wait()


class Loaded:
    def __init__(self, refs):
        self.refs = refs

    def start(self):
        r = self.refs
        copies = [
            pltpu.make_async_copy(r["attn_in"], r["attn"], r["io"].at[8]),
            pltpu.make_async_copy(r["ffn_in"], r["ffn"], r["io"].at[9]),
        ]
        for c in copies:
            c.start()
        r["vec"][...] = r["vec_in"][...].astype(f32)
        for c in copies:
            c.wait()

    def before_pair(self, i):
        pass

    before_in = before_out = step = before_pair

    def finish(self):
        pass


def position():
    dp, fs = lax.axis_index("dp"), lax.axis_index("fsdp")
    return lax.div(dp, 2), lax.rem(dp, 2), lax.div(fs, 2), lax.rem(fs, 2)


def device(z, x, y, c):
    return (z * 2 + x, y * 2 + c)


def remote(src, dst, send, recv, target):
    return pltpu.make_async_remote_copy(
        src_ref=src, dst_ref=dst, send_sem=send, recv_sem=recv, device_id=target, device_id_type=MESH
    )


ATT_GROUPS = (192, 192, 192)
FFN_GROUPS = (192, 96, 288, 288, 288)
PLANE_GROUPS = 2
Z, PASS, A, B, C, HOP = range(1, 7)
VECTOR_MARKS = (3003, 4003, 5003)
GATHER_ENDS = {
    0: (3030, 3040, 1000, 1010, 1020, 1050, 3000, 3010, 3020, 3050, 3060, 3070, 4030, 4040, 3001, 4000, 4010, 4020, 3011, 4050, 3002, 3021, 6030, 6040, 1060, 1070, 4060, 4070, 3003, 5000, 3012, 4001, 4011, 5010, 4002, 3022, 4021, 5020, 4003, 6031, 4012, 4022, 5050, 6041, 3013, 5060, 3023, 5070, 3051, 4013, 5001, 4023, 3061, 5011, 4051, 5002, 3071, 3052, 4061, 5021, 3053, 5003,),
    2: (5012, 4052, 4071, 3062,),
    4: (6032, 5013, 5022, 4053, 5023,),
    6: (6042, 5051, 4062, 3072, 3063,),
    8: (5052, 5061, 3073,),
    10: (4072,),
    12: (5071, 4063, 4073,),
    13: (5053, 5062,),
    14: (6033, 5063, 6043, 5072,),
    15: (5073,),
}
GATHER_MIDDLE = {
    0: (3030, 3040, 1000, 1010, 1020, 3000, 3010, 3020, 3050, 3060, 3070, 4030, 4040, 3001, 3002, 4000, 4010, 4020, 2003, 3003, 3011, 4050, 6030, 3012, 6040, 4060, 2013, 3013, 3021, 4070, 5000, 3022, 4001, 4002, 5010, 2023, 1050, 1060, 1070, 4003, 3023, 4011, 5020, 3051, 4012, 4013, 4021, 2053, 5050, 3053, 4022, 6032, 4023, 5060, 6042, 6031, 4051, 3052, 4053, 6041, 5070, 5001, 3061, 5002, 4052, 5003, 3062, 4061, 2063, 3063,),
    2: (5011, 5012, 3071,),
    4: (5013, 2073, 4062, 4063, 5021, 3072, 3073,),
    6: (5022, 4071,),
    8: (5023, 4072, 4073, 5051,),
    10: (6033, 5053,),
    12: (6043, 5052, 5061,),
    13: (5062, 5063,),
    14: (5071,),
    15: (5072,),
    17: (5073,),
}
SCATTER = {
    4: (100, 101, 102, 103,),
    5: (200,),
    6: (201, 202, 203,),
    8: (300, 104, 105, 106, 107,),
    9: (301, 204, 205, 108,),
    10: (302, 206, 207, 400, 208, 109,),
    11: (401, 303, 209, 110,),
    12: (402, 210, 111,),
    13: (304, 211, 403, 112,),
    14: (305, 212, 113, 500,),
    15: (404, 306, 213, 405, 307,),
    16: (501,),
    17: (114,),
    19: (502, 406, 308, 407, 214,),
    20: (503, 309, 115,),
    22: (408, 310, 215, 504,),
    23: (116,),
    25: (409, 410, 311, 216, 505,),
    26: (312, 117,),
    28: (411, 313, 217,),
    29: (506, 118,),
    31: (508, 412, 413, 218, 314, 509,),
    32: (507, 119,),
    34: (315, 316, 219, 510,),
    35: (414, 120,),
    36: (317, 220,),
    37: (511, 415, 318,),
    38: (416, 512, 417, 319, 418, 320, 419, 513, 420, 514, 515, 516, 517, 518, 519, 520,),
}


ATT, FFN = 0, 1


def group_of(g):
    if g < len(ATT_GROUPS):
        return ATT, pl.ds(sum(ATT_GROUPS[:g]), ATT_GROUPS[g])
    g -= len(ATT_GROUPS)
    return FFN, pl.ds(sum(FFN_GROUPS[:g]), FFN_GROUPS[g])


ATT_HEAD, FFN_HEAD = 30, 42

N_GROUPS = len(ATT_GROUPS) + len(FFN_GROUPS)
PLANE_ROWS = sum(FFN_GROUPS[:PLANE_GROUPS])


def is_plane_group(g):
    return len(ATT_GROUPS) <= g < len(ATT_GROUPS) + PLANE_GROUPS


class Gather:
    def __init__(self, refs):
        self.refs = refs
        self.z, self.x, self.y, self.c = z, x, y, c = position()
        self.me = z * 8 + x * 4 + y * 2 + c
        first = c == 0
        a, b = jnp.where(first, x, y), jnp.where(first, y, x)
        self.slot, self.pair = b * 2 + a, b * 2
        self.other_slot, self.other_pair = b * 2 + 1 - a, (1 - b) * 2
        self.dev_a = device(z, jnp.where(first, 1 - x, x), jnp.where(first, y, 1 - y), c)
        self.dev_b = device(z, jnp.where(first, x, 1 - x), jnp.where(first, 1 - y, y), c)
        self.dev_c = device(z, x, y, 1 - c)
        self.zs = [lax.rem(z + k, 4) for k in (1, 2, 3)]
        self.dev_z = [device(t, x, y, c) for t in self.zs]
        upper = lax.div(z, 2)
        self.near = [z, z + 1 - 2 * lax.rem(z, 2), 2 - upper, 3 - 3 * upper]
        self.dev_near = [device(t, x, y, c) for t in self.near]
        self.is_end = (z == 0) | (z == 3)
        self.is_middle = (z == 1) | (z == 2)
        self.from_me = 2 + jnp.where(self.is_end, 1, 0)
        self.half = upper * 2
        self.other_half = 2 - upper * 2
        last = lax.rem(self.me + 1, 32)
        before = lax.rem(self.me + 31, 32)
        self.dev_after = (lax.div(last, 4), lax.rem(last, 4))
        self.dev_before = (lax.div(before, 4), lax.rem(before, 4))
        self.buf = (refs["attn"], refs["ffn"])

    def barrier(self):
        bar = pltpu.get_barrier_semaphore()
        targets = [self.dev_a, self.dev_b, self.dev_c, self.dev_after, self.dev_before] + self.dev_z
        for t in targets:
            pl.semaphore_signal(bar, inc=1, device_id=t, device_id_type=MESH)
        pl.semaphore_wait(bar, len(targets))

    def z_copy(self, g, k):
        kind, rows = group_of(g)
        ref = self.buf[kind].at[self.z, self.c, self.slot, rows]
        index = 1 if k == 1 else self.from_me
        r = self.refs
        return remote(ref, ref, r["gs"].at[8 + 3 * kind + k - 1], r["zr"].at[g, index], self.dev_near[k])

    def pass_copy(self, g):
        kind, rows = group_of(g)
        ref = self.buf[kind].at[self.near[3], self.c, self.slot, rows]
        return remote(ref, ref, self.refs["gs"].at[14 + kind], self.refs["zr"].at[g, 3], self.dev_near[1])

    def z_arrival(self, g, k):
        kind, rows = group_of(g)
        wide_ = pl.ds(0, 4) if is_plane_group(g) else self.slot
        ref = self.buf[kind].at[self.near[k], self.c, wide_, rows]
        return remote(ref, ref, self.refs["gs"].at[8], self.refs["zr"].at[g, k], self.dev_near[1])

    def hop_copy(self, g, k, n):
        _, rows = group_of(g)
        layer = self.near[max(n - 1, 0)]
        ref = self.refs["ffn"].at[layer, self.c, :, rows]
        target = self.dev_near[2 if n in (1, 2) else 1]
        index = (1, 2, 3, 2, 3)[n]
        return remote(ref, ref, self.refs["gs"].at[16 + n], self.refs["zr"].at[g, index], target)

    def plane_copy(self, step, g, k):
        kind, rows = group_of(g)
        r = self.refs
        at = self.buf[kind].at[self.near[k], self.c]
        later = 0 if kind == ATT else 1 if k == 0 else 2
        if step == A:
            src, send, recv, target = at.at[self.slot, rows], later, "ar", self.dev_a
        elif step == B:
            src, send, recv, target = at.at[pl.ds(self.pair, 2), rows], 3 + later, "br", self.dev_b
        else:
            src, send, recv, target = at.at[:, rows], 6 + kind, "cr", self.dev_c
        return remote(src, src, r["gs"].at[send], r[recv].at[g, k], target)

    def run(self, code):
        kind, g, k = code // 1000, code // 10 % 100, code % 10
        if kind == Z:
            self.z_copy(g, 1).start()
            self.z_copy(g, 2).start()
            pl.when(self.is_middle)(lambda: self.z_copy(g, 3).start())
            return
        if kind == PASS:
            self.z_arrival(g, 3).wait_recv()
            self.pass_copy(g).start()
            return
        if kind == HOP:
            if k == 0:
                self.plane_copy(B, g, 0).wait_recv()
                self.hop_copy(g, 0, 0).start()
                pl.when(self.is_middle)(lambda: self.hop_copy(g, 0, 1).start())
            else:
                self.z_arrival(g, k).wait_recv()
                pl.when(self.is_middle)(lambda: self.hop_copy(g, k, k + 1).start())
            self.plane_copy(C, g, k).start()
            return
        if kind == A and k in (1, 2):
            self.z_arrival(g, k).wait_recv()
        elif kind == A and k == 3:
            pl.when(self.is_end)(lambda: self.z_arrival(g, 3).wait_recv())
        elif kind == B:
            self.plane_copy(A, g, k).wait_recv()
        elif kind == C:
            self.plane_copy(B, g, k).wait_recv()
        self.plane_copy(kind, g, k).start()

    def ready(self, g, first, count):
        kind, rows = group_of(g)
        r = self.refs
        for n in range(count):
            ref = self.buf[kind].at[0, 1 - self.c, :, rows]
            remote(ref, ref, r["gs"].at[6 + kind], r["cr"].at[g, first + n], self.dev_c).wait_recv()

    def steps(self, key):
        for who, table in ((self.is_end, GATHER_ENDS), (self.is_middle, GATHER_MIDDLE)):
            if key in table:

                @pl.when(who)
                def _(table=table):
                    for s in table[key]:
                        self.run(s)

    def vectors(self, stage):
        r = self.refs
        buf, own, v = r["vec_all"], r["tail"], r["vsem"]
        one = buf.at[self.c, self.slot]
        if stage == 0:

            @pl.when(self.z == 3)
            def _():
                one[...] = own[...]
                for k in range(3):
                    remote(own, one, v.at[4 + k], v.at[1], self.dev_z[k]).start()

        elif stage == 1:

            @pl.when(self.z == 3)
            def _():
                for k in range(3):
                    remote(own, one, v.at[4 + k], v.at[1], self.dev_z[k]).wait_send()

            @pl.when(self.z != 3)
            def _():
                remote(one, one, v.at[4], v.at[1], self.dev_z[0]).wait_recv()

            remote(one, one, v.at[7], v.at[2], self.dev_a).start()
        elif stage == 2:
            got = buf.at[self.c, self.other_slot]
            remote(got, got, v.at[7], v.at[2], self.dev_a).wait()
            mine = buf.at[self.c, pl.ds(self.pair, 2)]
            remote(mine, mine, v.at[8], v.at[3], self.dev_b).start()
        elif stage == 3:
            got = buf.at[self.c, pl.ds(self.other_pair, 2)]
            remote(got, got, v.at[8], v.at[3], self.dev_b).wait()
            mine = buf.at[self.c]
            remote(mine, mine, v.at[9], v.at[10], self.dev_c).start()
        else:
            got = buf.at[1 - self.c]
            remote(got, got, v.at[9], v.at[10], self.dev_c).wait()
            r["vec"][...] = buf[1, 3].astype(f32)

    def tail_copy(self):
        t = self.refs["tail"]
        return remote(t, self.refs["tail_in"], self.refs["vsem"].at[11], self.refs["vsem"].at[12], self.dev_after)

    def load_own(self):
        r = self.refs
        flat_a, flat_f = r["flat_a"], r["flat_f"]
        own_a, own_f = r["attn_own"], r["ffn_own"]
        whole_a, whole_f = ATT_ROWS * 128, FFN_ROWS * 128
        flat_a[ATT_HEAD + ATT_ROWS : ATT_HEAD + ATT_ROWS + 16, :] = jnp.zeros((16, 128), f32)
        flat_f[FFN_HEAD + FFN_ROWS : FFN_HEAD + FFN_ROWS + 16, :] = jnp.zeros((16, 128), f32)
        flat_a[pl.ds(ATT_HEAD, ATT_ROWS), :] = own_a[0:whole_a].reshape(ATT_ROWS, 128).astype(f32)
        flat_f[pl.ds(FFN_HEAD, FFN_ROWS), :] = own_f[0:whole_f].reshape(FFN_ROWS, 128).astype(f32)
        at = ATT_HEAD + ATT_ROWS
        flat_a[at : at + 1, 0:120] = own_a[whole_a : whole_a + 120].reshape(1, 120).astype(f32)
        at = FFN_HEAD + FFN_ROWS
        flat_f[at : at + 1, :] = own_f[whole_f : whole_f + 128].reshape(1, 128).astype(f32)
        flat_f[at + 1 : at + 2, 0:40] = own_f[whole_f + 128 : whole_f + 168].reshape(1, 40).astype(f32)
        lane = lax.broadcasted_iota(jnp.int32, (32, 128), 1)
        v = pltpu.roll(flat_a[ATT_HEAD + 546 : ATT_HEAD + 586, :], 8, 1)
        r["tail"][0:32, :] = jnp.where(lane < 8, v[0:32], v[1:33]).astype(bf16)
        lane = lax.broadcasted_iota(jnp.int32, (48, 128), 1)
        v = pltpu.roll(flat_f[FFN_HEAD + 1111 : FFN_HEAD + 1167, :], 88, 1)
        r["tail"][32:80, :] = jnp.where(lane < 88, v[0:48], v[1:49]).astype(bf16)

    def place_own(self, kind):
        r = self.refs
        if kind == ATT:
            flat, rows, head, size, moved, at = r["flat_a"], r["rows_a"], ATT_HEAD, ATT_ROWS, 120, 0
        else:
            flat, rows, head, size, moved, at = r["flat_f"], r["rows_f"], FFN_HEAD, FFN_ROWS, 168, 32
        flat[0:head, :] = r["tail_in"][at : at + head, :].astype(f32)
        self.shifted(flat, rows, head * 128 - moved * self.me, size)
        slot = self.buf[kind].at[self.z, self.c, self.slot]
        self.by_kind(kind, lambda tiles, n, at: self.to_tiles(rows, slot, tiles, n, at))

    def by_kind(self, kind, fn):
        if kind == ATT:
            pl.when(self.z < 3)(lambda: fn(18, 32, lambda t: (t % 6 * 3 + t // 6) * 32))
            pl.when(self.z == 3)(lambda: fn(6, 96, lambda t: t * 96))
        else:
            pl.when(self.z < 2)(lambda: fn(24, 48, lambda t: t * 48))
            pl.when(self.z >= 2)(lambda: fn(6, 192, lambda t: t * 192))

    def to_tiles(self, rows, slot, tiles, n, at):
        for t in range(tiles):
            slot[at(t) : at(t) + n, :] = rows[pl.ds(t, n, stride=tiles), :].astype(bf16)

    def from_tiles(self, total, flat, tiles, n, at):
        for t in range(tiles):
            flat[pl.ds(t, n, stride=tiles), :] = total[at(t) : at(t) + n, :]

    def shifted(self, src, dst, shift, count):
        row, turn = lax.div(shift, 128), lax.rem(shift, 128)

        def step(n, carry):
            lane = lax.broadcasted_iota(jnp.int32, (64, 128), 1)
            back = lax.rem(128 - turn, 128)
            low = pltpu.roll(src[pl.ds(n * 64 + row, 64), :], back, 1)
            high = pltpu.roll(src[pl.ds(n * 64 + row + 1, 64), :], back, 1)
            dst[pl.ds(pl.multiple_of(n * 64, 64), 64), :] = jnp.where(lane < 128 - turn, low, high)
            return carry

        lax.fori_loop(0, count // 64, step, 0)

    def start(self):
        self.load_own()
        self.barrier()
        pl.when(self.me < 31)(lambda: self.tail_copy().start())
        self.vectors(0)
        pl.when(self.me > 0)(lambda: self.tail_copy().wait_recv())
        self.place_own(ATT)
        for g in range(len(ATT_GROUPS)):
            self.run(1000 * Z + 10 * g)
        self.place_own(FFN)
        for who, table in ((self.is_end, GATHER_ENDS), (self.is_middle, GATHER_MIDDLE)):

            @pl.when(who)
            def _(table=table):
                first = [v for v in table[0] if v >= 1000 * Z + 10 * len(ATT_GROUPS)]
                cuts = [0] + [first.index(v) + 1 for v in VECTOR_MARKS] + [len(first)]
                for stage in range(4):
                    for s in first[cuts[stage] : cuts[stage + 1]]:
                        self.run(s)
                    self.vectors(stage + 1)

    def before_pair(self, i):
        for v in range(PAIRS):

            @pl.when(i == v)
            def _(v=v):
                if v:
                    self.steps(2 * v)
                if v * len(ATT_GROUPS) % PAIRS == 0:
                    self.ready(v * len(ATT_GROUPS) // PAIRS, 0, 4)

    def step(self, n):
        self.steps(12 + n)

    def before_in(self, j):
        at = 0
        for n, rows in enumerate(FFN_GROUPS):

            @pl.when(j == at // 96)
            def _(n=n):
                self.steps(14 + n)
                self.ready(len(ATT_GROUPS) + n, self.half, 2)

            at += rows

    def before_out(self, j):
        seen = 0
        for v in range(3):
            more, at = [], 0
            for n, rows in enumerate(FFN_GROUPS):
                if n >= seen and at < 384 * (v + 1):
                    more.append(n)
                at += rows
            seen += len(more)

            @pl.when(j == v)
            def _(v=v, more=more):
                self.steps(14 + len(FFN_GROUPS) + v)
                for n in more:
                    self.ready(len(ATT_GROUPS) + n, self.other_half, 2)

    def finish(self):
        self.steps(17 + len(FFN_GROUPS))
        r = self.refs
        z, c, gs = self.z, self.c, r["gs"]
        attn, ffn = self.buf
        rest = pl.ds(PLANE_ROWS, FFN_ROWS - PLANE_ROWS)
        front = pl.ds(0, PLANE_ROWS)

        def sent(n, ref):
            remote(ref, ref, gs.at[n], r["zr"].at[0, 0], self.dev_c).wait_send()

        sent(0, attn.at[:, c, self.slot])
        sent(1, ffn.at[z, c, self.slot])
        sent(2, ffn.at[pl.ds(0, 3), c, self.slot, rest])
        sent(3, attn.at[:, c, pl.ds(self.pair, 2)])
        sent(4, ffn.at[z, c, pl.ds(self.pair, 2)])
        sent(5, ffn.at[pl.ds(0, 3), c, pl.ds(self.pair, 2), rest])
        sent(6, attn.at[:, c])
        sent(7, ffn.at[:, c])
        for k in range(2):
            sent(8 + k, attn.at[z, c, self.slot])
            sent(11 + k, ffn.at[z, c, self.slot, rest])
        if PLANE_GROUPS:
            sent(16, ffn.at[z, c, :, front])

        @pl.when(self.is_middle)
        def _():
            sent(10, attn.at[z, c, self.slot])
            sent(13, ffn.at[z, c, self.slot, rest])
            sent(14, attn.at[z, c, self.slot])
            sent(15, ffn.at[z, c, self.slot, rest])
            if PLANE_GROUPS:
                for n in range(17, 21):
                    sent(n, ffn.at[z, c, :, front])

        pl.when(self.me < 31)(lambda: self.tail_copy().wait_send())


W_FC, W_IN, W_OUT, W_QKV = 0, 8, 14, 15
N_ITEMS = W_QKV + PAIRS


class Scatter:
    def __init__(self, refs, gather):
        self.refs, self.g = refs, gather

    def part(self, item):
        if item >= W_QKV:
            return "qkv_g", "attn", range(0, 3), pl.ds(96 * (item - W_QKV), 96), 96, 2
        if item == W_OUT:
            return "attn", "attn", range(3, 4), pl.ds(0, 576), 576, 1
        if item >= W_IN:
            return "ffn", "ffn", range(0, 2), pl.ds(192 * (item - W_IN), 192), 192, 0
        z = 2 + item // 4
        return "ffn", "ffn", range(z, z + 1), pl.ds(288 * (item % 4), 288), 288, 0

    def span(self, zz):
        return pl.ds(zz[0], len(zz))

    def add(self, pairs, rows, count):
        def step(n, carry):
            at = pl.ds(pl.multiple_of(rows.start + n * 96, 96), 96)
            for dst, src in pairs:
                d = dst.at[at]
                d[...] = d[...] + src.at[at][...]
            return carry

        if count == 96:
            step(0, 0)
        else:
            lax.fori_loop(0, count // 96, step, 0)

    def c_copy(self, g):
        buf, kind, zz, rows, _, s = self.part(g)
        r, t = self.refs, self.g
        return remote(
            r[buf].at[self.span(zz), 1 - t.c, :, rows],
            r[kind + "_rc"].at[self.span(zz), :, rows],
            r["ss"].at[s, 0],
            r["sr"].at[0, g],
            t.dev_c,
        )

    def b_copy(self, g):
        buf, kind, zz, rows, _, s = self.part(g)
        r, t = self.refs, self.g
        return remote(
            r[buf].at[self.span(zz), t.c, pl.ds(t.other_pair, 2), rows],
            r[kind + "_rb"].at[self.span(zz), :, rows],
            r["ss"].at[s, 1],
            r["sr"].at[1, g],
            t.dev_b,
        )

    def a_copy(self, g):
        buf, kind, zz, rows, _, s = self.part(g)
        r, t = self.refs, self.g
        return remote(
            r[buf].at[self.span(zz), t.c, t.other_slot, rows],
            r[kind + "_ra"].at[self.span(zz), rows],
            r["ss"].at[s, 2],
            r["sr"].at[2, g],
            t.dev_a,
        )

    def z_copy(self, g, k):
        buf, kind, zz, rows, _, s = self.part(g)
        r, t = self.refs, self.g
        return remote(
            r[buf].at[t.zs[k], t.c, t.slot, rows],
            r[kind + "_rz"].at[k, rows],
            r["ss"].at[s, 3 + k],
            r["sr"].at[3, g],
            t.dev_z[k],
        )

    def inside(self, value, zz):
        return (value >= zz[0]) & (value <= zz[-1])

    def c_send(self, g):
        self.c_copy(g).start()

    def b_send(self, g):
        buf, kind, zz, rows, n, _ = self.part(g)
        r, t = self.refs, self.g
        self.c_copy(g).wait_recv()
        self.add([(r[buf].at[z, t.c, i], r[kind + "_rc"].at[z, i]) for z in zz for i in range(4)], rows, n)
        self.b_copy(g).start()

    def a_send(self, g):
        buf, kind, zz, rows, n, _ = self.part(g)
        r, t = self.refs, self.g
        self.b_copy(g).wait_recv()
        self.add([(r[buf].at[z, t.c, t.pair + i], r[kind + "_rb"].at[z, i]) for z in zz for i in range(2)], rows, n)
        self.a_copy(g).start()

    def z_send(self, g):
        buf, kind, zz, rows, n, _ = self.part(g)
        r, t = self.refs, self.g
        self.a_copy(g).wait_recv()
        self.add([(r[buf].at[z, t.c, t.slot], r[kind + "_ra"].at[z]) for z in zz], rows, n)
        for k in range(3):

            @pl.when(self.inside(t.zs[k], zz))
            def _():
                self.z_copy(g, k).start()

    def take(self, g):
        buf, kind, zz, rows, n, _ = self.part(g)
        r, t = self.refs, self.g

        @pl.when(self.inside(t.z, zz))
        def _():
            got = r[kind + "_rz"].at[:, rows]
            remote(got, got, r["ss"].at[0, 3], r["sr"].at[3, g], t.dev_c).wait_recv()

            def step(i, carry):
                at = pl.ds(pl.multiple_of(rows.start + i * 96, 96), 96)
                total = r[buf][t.z, t.c, t.slot, at, :].astype(f32)
                for k in range(3):
                    total = total + r[kind + "_rz"][k, at, :].astype(f32)
                r[kind + "_sum"][at, :] = total
                return carry

            lax.fori_loop(0, n // 96, step, 0)

    def vectors(self, stage):
        r, t = self.refs, self.g
        own, got, s, v = r["vg"], r["vg_r"], r["vs"], r["vr"]
        if stage > 0:
            target = (t.dev_c, t.dev_b, t.dev_a)[stage - 1]
            remote(own, got.at[stage - 1], s.at[stage - 1], v.at[stage - 1], target).wait()
            own[...] = own[...] + got[stage - 1]
        if stage < 3:
            target = (t.dev_c, t.dev_b, t.dev_a)[stage]
            remote(own, got.at[stage], s.at[stage], v.at[stage], target).start()
        else:
            for k in range(3):

                @pl.when(t.zs[k] == 3)
                def _():
                    remote(own, got.at[3 + k], s.at[3 + k], v.at[3 + k], t.dev_z[k]).start()

    def take_vectors(self):
        r, t = self.refs, self.g
        own, got, s, v = r["vg"], r["vg_r"], r["vs"], r["vr"]
        for k in range(3):

            @pl.when(t.zs[k] == 3)
            def _():
                remote(own, got.at[3 + k], s.at[3 + k], v.at[3 + k], t.dev_z[k]).wait_send()

        @pl.when(t.z == 3)
        def _():
            for k in range(3):
                remote(own, got.at[3 + k], s.at[3 + k], v.at[3 + k], t.dev_z[k]).wait_recv()
            own[...] = own[...] + got[3] + got[4] + got[5]

    def sent(self):
        r, t = self.refs, self.g
        ss = r["ss"]

        def one(s, n, ref):
            remote(ref, ref, ss.at[s, n], r["sr"].at[0, 0], t.dev_c).wait_send()

        for s, ref in enumerate((r["ffn"], r["attn"].at[pl.ds(3, 1)], r["qkv_g"])):
            one(s, 0, ref.at[:, 1 - t.c])
            one(s, 1, ref.at[:, t.c, pl.ds(t.other_pair, 2)])
            one(s, 2, ref.at[:, t.c, t.other_slot])
        for k in range(3):
            one(0, 3 + k, r["ffn"].at[0, t.c, t.slot])
            pl.when(t.zs[k] == 3)(lambda k=k: one(1, 3 + k, r["attn"].at[3, t.c, t.slot]))
            pl.when(t.zs[k] != 3)(lambda k=k: one(2, 3 + k, r["qkv_g"].at[0, t.c, t.slot]))

    def step(self, key):
        for s in SCATTER.get(key, ()):
            self.one(s)

    def one(self, s):
        kinds = (None, self.c_send, self.b_send, self.a_send, self.z_send, self.take)
        kinds[s // 100](s % 100)

    def loop(self, i, first, stride, count):
        for v in range(count):
            if first + stride * v in SCATTER:
                pl.when(i == v)(lambda v=v: self.step(first + stride * v))

    def in_fc(self, m):
        self.loop(m, 0, 1, 8)

    def in_in(self, j):
        self.loop(j, 8, 1, 6)

    def between(self, n):
        self.step(14 + n)

    def pair_start(self, i):
        self.loop(i, 17, 3, PAIRS)

    def pair_end(self, i):
        self.loop(i, 19, 3, PAIRS)

    def tail(self, n):
        if n < 3:
            self.step(35 + n)
            self.vectors(n)
            return
        self.vectors(3)
        order = SCATTER[38]
        ffn_left = max(i for i, s in enumerate(order) if s // 100 == 5 and s % 100 < W_OUT) + 1
        relays_left = max(i for i, s in enumerate(order) if s // 100 < 5) + 1
        for s in order[:ffn_left]:
            self.one(s)
        self.hand_over(FFN)
        for s in order[ffn_left:relays_left]:
            self.one(s)
        self.take_vectors()
        self.finish(FFN)
        for s in order[relays_left:]:
            self.one(s)
        self.hand_over(ATT)
        self.finish(ATT)
        self.sent()

    def head_copy(self, kind):
        r, t = self.refs, self.g
        count = (32, 48)[kind]
        head, got = r[("flat_a", "flat_f")[kind]].at[pl.ds(0, count)], r["head_in"].at[pl.ds(32 * kind, count)]
        return remote(head, got, r["hs"].at[2 * kind], r["hs"].at[2 * kind + 1], t.dev_before)

    def hand_over(self, kind):
        r, t = self.refs, self.g
        total, flat = r[("attn_sum", "ffn_sum")[kind]], r[("flat_a", "flat_f")[kind]]
        t.by_kind(kind, lambda tiles, n, at: t.from_tiles(total, flat, tiles, n, at))
        pl.when(t.me > 0)(self.head_copy(kind).start)

    def finish(self, kind):
        r, t = self.refs, self.g
        size, count, moved = ((ATT_ROWS, 32, 120), (FFN_ROWS, 48, 168))[kind]
        flat, rows = r[("flat_a", "flat_f")[kind]], r[("rows_a", "rows_f")[kind]]
        copy = self.head_copy(kind)
        pl.when(t.me < 31)(copy.wait_recv)
        mine = jnp.where(t.me == 31, r["vg"][32 * kind : 32 * kind + count, :], r["head_in"][32 * kind : 32 * kind + count, :])
        flat[size : size + count, :] = mine
        t.shifted(flat, rows, moved * t.me, size + 64)
        whole = size * 128
        out = r[("attn_out", "ffn_out")[kind]]
        out[0:whole] = rows[0:size, :].reshape(whole)
        if kind == ATT:
            out[whole : whole + 120] = rows[size : size + 1, 0:120].reshape(120)
        else:
            out[whole : whole + 128] = rows[size : size + 1, :].reshape(128)
            out[whole + 128 : whole + 168] = rows[size + 1 : size + 2, 0:40].reshape(40)
        pl.when(t.me > 0)(copy.wait_send)


class Kept:
    def in_fc(self, m):
        pass

    in_in = between = pair_start = pair_end = tail = in_fc


SCRATCH = dict(
    x=((R, D), bf16),
    mix=((R, D), bf16),
    cot_b=((2, ROWS, D), bf16),
    out_b=((2, ROWS, D), bf16),
    attn=((4, 2, 4, ATT_ROWS, 128), bf16),
    ffn=((4, 2, 4, FFN_ROWS, 128), bf16),
    vec=((VEC_ROWS, 128), f32),
    qx=((R, 1536), bf16),
    k=((R, D), bf16),
    v=((R, D), bf16),
    xh1=((R, D), f32),
    rs1=((R, 128), f32),
    n1=((R, D), bf16),
    act=((R, FF), bf16),
    gp=((R, FF), bf16),
    r2=((R, D), f32),
    gf=((R, D), bf16),
    qkv_g=((3, 2, 4, ATT_ROWS, 128), bf16),
)


def run_layer(linked, length, x, cot, attn_in, ffn_in, vec_in=None):
    dma = pltpu.SemaphoreType.DMA
    vmem, anywhere = pl.BlockSpec(memory_space=pltpu.VMEM), pl.BlockSpec(memory_space=pl.ANY)
    names = ["length", "x_in", "cot"] + (["attn_own", "ffn_own"] if linked else ["attn_in", "ffn_in", "vec_in"])
    names += ["out", "gin"] + (["attn_out", "ffn_out"] if linked else ["attn_g", "ffn_g", "vg"])
    more = dict(io=dma((10,)))
    if linked:
        more.update(
            vg=pltpu.VMEM((VEC_ROWS, 128), f32),
            vec_all=pltpu.VMEM((2, 4, VEC_ROWS, 128), bf16),
            tail=pltpu.VMEM((VEC_ROWS, 128), bf16),
            tail_in=pltpu.VMEM((VEC_ROWS, 128), bf16),
            head_in=pltpu.VMEM((VEC_ROWS, 128), f32),
            flat_a=pltpu.VMEM((704, 128), f32),
            flat_f=pltpu.VMEM((1280, 128), f32),
            rows_a=pltpu.VMEM((640, 128), f32),
            rows_f=pltpu.VMEM((1216, 128), f32),
            gs=dma((21,)),
            zr=dma((N_GROUPS, 4)),
            ar=dma((N_GROUPS, 4)),
            br=dma((N_GROUPS, 4)),
            cr=dma((N_GROUPS, 4)),
            vsem=dma((13,)),
            ss=dma((3, 6)),
            sr=dma((4, N_ITEMS)),
            vs=dma((6,)),
            vr=dma((6,)),
            hs=dma((4,)),
            vg_r=pltpu.VMEM((6, VEC_ROWS, 128), f32),
        )
        for kind, rows in (("attn", ATT_ROWS), ("ffn", FFN_ROWS)):
            more[kind + "_rc"] = pltpu.VMEM((4, 4, rows, 128), bf16)
            more[kind + "_rb"] = pltpu.VMEM((4, 2, rows, 128), bf16)
            more[kind + "_ra"] = pltpu.VMEM((4, rows, 128), bf16)
            more[kind + "_rz"] = pltpu.VMEM((3, rows, 128), bf16)
            more[kind + "_sum"] = pltpu.VMEM((rows, 128), f32)
    names += list(SCRATCH) + list(more)
    scratch = [pltpu.VMEM(*s) for s in SCRATCH.values()] + list(more.values())

    def body(*args):
        refs = dict(zip(names, args, strict=True))
        refs["vg"][...] = jnp.zeros((VEC_ROWS, 128), f32)
        if linked:
            gather = Gather(refs)
            layer_kernel(gather, Scatter(refs, gather), refs)
            return
        layer_kernel(Loaded(refs), Kept(), refs)
        copies = [
            pltpu.make_async_copy(refs["qkv_g"], refs["attn_g"].at[0:3], refs["io"].at[0]),
            pltpu.make_async_copy(refs["attn"].at[3], refs["attn_g"].at[3], refs["io"].at[1]),
            pltpu.make_async_copy(refs["ffn"], refs["ffn_g"], refs["io"].at[2]),
        ]
        for c in copies:
            c.start()
        for c in copies:
            c.wait()

    act_out = jax.ShapeDtypeStruct((R, D), bf16)
    if linked:
        grads = tuple(jax.ShapeDtypeStruct(a.shape, f32) for a in (attn_in, ffn_in))
    else:
        grads = tuple(jax.ShapeDtypeStruct(SCRATCH[k][0], bf16) for k in ("attn", "ffn"))
        grads += (jax.ShapeDtypeStruct((VEC_ROWS, 128), f32),)
    smem = pl.BlockSpec(memory_space=pltpu.SMEM)
    args = (length, x, cot, attn_in, ffn_in) + (() if linked else (vec_in,))
    return pl.pallas_call(
        body,
        out_shape=(act_out, act_out) + grads,
        in_specs=[smem, anywhere, anywhere] + ([vmem, vmem] if linked else [anywhere, anywhere, vmem]),
        out_specs=(anywhere,) * 2 + ((vmem,) * 2 if linked else (anywhere, anywhere, vmem)),
        scratch_shapes=scratch,
        compiler_params=pltpu.CompilerParams(
            vmem_limit_bytes=64 * 1024 * 1024 - 65536,
            has_side_effects=True,
            **(dict(collective_id=0) if linked else {}),
        ),
    )(*args)


def qkv_chunk(flat):
    return flat.reshape(-1, 32, 3, 6, 128).transpose(0, 3, 2, 1, 4).reshape(-1, ATT_ROWS, 128)


def qkv_flat(chunk):
    return chunk.reshape(-1, 6, 3, 32, 128).transpose(0, 3, 2, 1, 4).reshape(-1)


def tiled_chunk(flat, rows, tiles):
    return flat.reshape(-1, rows, tiles, 128).transpose(0, 2, 1, 3).reshape(-1, rows * tiles, 128)


def tiled_flat(chunk, rows, tiles):
    return chunk.reshape(-1, tiles, rows, 128).transpose(0, 2, 1, 3).reshape(-1)


def pack_vectors(attn_vec, ffn_vec):
    return jnp.concatenate(
        [
            attn_vec.reshape(30, 128),
            jnp.zeros((2, 128), attn_vec.dtype),
            ffn_vec.reshape(42, 128),
            jnp.zeros((6, 128), attn_vec.dtype),
        ]
    )


def shards_linked(frames, lengths, attn_params, ffn_params, cotangent):
    out, gin, attn_grad, ffn_grad = run_layer(True, lengths, frames[0], cotangent[0], attn_params, ffn_params)
    return out[None], gin[None], attn_grad, ffn_grad


def in_places(chunks):
    g = chunks.reshape(4, 2, 2, 2, -1, 128)
    p0 = g[:, :, :, 0].transpose(0, 2, 1, 3, 4).reshape(4, 4, -1, 128)
    p1 = g[:, :, :, 1].reshape(4, 4, -1, 128)
    return jnp.stack([p0, p1], axis=1)


def from_places(g):
    p0 = g[:, 0].reshape(4, 2, 2, -1, 128).transpose(0, 2, 1, 3, 4)
    p1 = g[:, 1].reshape(4, 2, 2, -1, 128)
    return jnp.stack([p0, p1], axis=3).reshape(32, -1, 128)


def shards_any(frames, lengths, attn_params, ffn_params, cotangent):
    devices = lax.axis_size(AXES)
    attn_flat = lax.all_gather(attn_params, AXES, axis=0, tiled=True)
    ffn_flat = lax.all_gather(ffn_params, AXES, axis=0, tiled=True)
    cut_a, cut_f = 3 * D * D, D * FF
    attn_in = in_places(
        jnp.concatenate([qkv_chunk(attn_flat[:cut_a]), tiled_chunk(attn_flat[cut_a:ATT_MAT], 96, 6)])
    )
    ffn_in = in_places(
        jnp.concatenate([tiled_chunk(ffn_flat[:cut_f], 48, 24), tiled_chunk(ffn_flat[cut_f:FFN_MAT], 192, 6)])
    )
    vec_in = pack_vectors(attn_flat[ATT_MAT : ATT_MAT + ATT_VEC], ffn_flat[FFN_MAT : FFN_MAT + FFN_VEC])
    outs, gins, sums = [], [], None
    for u in range(frames.shape[0]):
        out, gin, attn_g, ffn_g, vg = run_layer(False, lengths[u : u + 1], frames[u], cotangent[u], attn_in, ffn_in, vec_in)
        outs.append(out)
        gins.append(gin)
        grads = [g.astype(f32) for g in (attn_g, ffn_g, vg)]
        sums = grads if sums is None else [s + g for s, g in zip(sums, grads)]
    attn_c, ffn_c = from_places(sums[0]), from_places(sums[1])
    pad_a = attn_params.shape[0] * devices - ATT_MAT - ATT_VEC
    pad_f = ffn_params.shape[0] * devices - FFN_MAT - FFN_VEC
    attn_terms = jnp.concatenate(
        [qkv_flat(attn_c[:24]), tiled_flat(attn_c[24:], 96, 6), sums[2][:30].reshape(-1), jnp.zeros((pad_a,), f32)]
    )
    ffn_terms = jnp.concatenate(
        [
            tiled_flat(ffn_c[:16], 48, 24),
            tiled_flat(ffn_c[16:], 192, 6),
            sums[2][32:74].reshape(-1),
            jnp.zeros((pad_f,), f32),
        ]
    )
    attn_grad = lax.psum_scatter(attn_terms, AXES, scatter_dimension=0, tiled=True)
    ffn_grad = lax.psum_scatter(ffn_terms, AXES, scatter_dimension=0, tiled=True)
    return jnp.stack(outs), jnp.stack(gins), attn_grad, ffn_grad


def solution(mesh):
    linked = tuple(mesh.shape[a] for a in AXES) == (8, 4)
    return jax.shard_map(
        shards_linked if linked else shards_any,
        mesh=mesh,
        in_specs=(P(AXES, None, None), P(AXES), P(AXES), P(AXES), P(AXES, None, None)),
        out_specs=(P(AXES, None, None), P(AXES, None, None), P(AXES), P(AXES)),
        check_vma=False,
    )
```

```python
from functools import partial

import jax
import jax.numpy as jnp
from jax import lax
from jax.experimental import pallas as pl
from jax.experimental.pallas import tpu as pltpu
from jax.sharding import PartitionSpec as P

D = 768
H = 12
FF = 3072
R = 768
PAIRS = 6
ATT_MAT = 4 * D * D
FFN_MAT = 2 * D * FF
ATT_VEC = 5 * D
FFN_VEC = FF + 3 * D
ATT_ROWS = 576
FFN_ROWS = 1152
VEC_ROWS = 80
AXES = ("dp", "fsdp")
bf16 = jnp.bfloat16
f32 = jnp.float32
MESH = pl.DeviceIdType.MESH

B_Q, B_V, B_OUT, G1, B1 = 0, 6, 12, 18, 24
B_IN, B_FC, G2, B2 = 32, 56, 62, 68


def nn(a, b):
    return jnp.dot(a, b, preferred_element_type=f32)


def nt(a, b):
    return lax.dot_general(a, b, (((1,), (1,)), ((), ())), preferred_element_type=f32)


def tn(a, b):
    return lax.dot_general(a, b, (((0,), (0,)), ((), ())), preferred_element_type=f32)


def split3(v):
    hi = v.astype(bf16)
    rest = v - hi.astype(f32)
    mid = rest.astype(bf16)
    return hi, mid, (rest - mid.astype(f32)).astype(bf16)


def place(chunk):
    z, x, y, c = chunk // 8, chunk // 4 % 2, chunk // 2 % 2, chunk % 2
    return z, c, (y * 2 + x if c == 0 else x * 2 + y)


def block(ref, chunk, rows):
    z, c, i = place(chunk)
    return ref[z, c, i, rows, :]


def aligned(start, size):
    return pl.ds(pl.multiple_of(start, size), size)


def w_qkv_pair(attn, i):
    blocks = [block(attn, d, aligned(i * 96, 96)) for d in range(24)]
    return jnp.concatenate(
        [jnp.concatenate([b[32 * p : 32 * p + 32] for b in blocks], axis=0) for p in range(3)], axis=1
    )


def put_w_qkv_pair(attn, i, value):
    for d in range(24):
        z, c, s = place(d)
        for p in range(3):
            attn[z, c, s, pl.ds(pl.multiple_of(i * 96 + 32 * p, 32), 32), :] = value[
                32 * d : 32 * d + 32, 128 * p : 128 * p + 128
            ]


def w_qkv_rows(attn, chunks, part):
    return jnp.concatenate(
        [
            jnp.concatenate(
                [block(attn, d, slice(96 * i + 32 * part, 96 * i + 32 * part + 32)) for i in range(PAIRS)], axis=1
            )
            for d in chunks
        ],
        axis=0,
    )


def w_out_cols(attn, j):
    blocks = [block(attn, d, slice(192 * j, 192 * j + 192)) for d in range(24, 32)]
    return jnp.concatenate(
        [jnp.concatenate([b[96 * p : 96 * p + 96] for b in blocks], axis=0) for p in range(2)], axis=1
    )


def w_out_rows(attn, chunks):
    return jnp.concatenate(
        [
            jnp.concatenate([block(attn, d, slice(96 * j, 96 * j + 96)) for j in range(6)], axis=1)
            for d in chunks
        ],
        axis=0,
    )


def w_in_cols(ffn, j, tiles):
    blocks = [block(ffn, d, aligned(j * 48 * tiles, 48 * tiles)) for d in range(16)]
    return jnp.concatenate(
        [jnp.concatenate([b[48 * p : 48 * p + 48] for b in blocks], axis=0) for p in range(tiles)], axis=1
    )


def put_w_in_cols(ffn, j, tiles, value):
    for d in range(16):
        z, c, s = place(d)
        for p in range(tiles):
            ffn[z, c, s, pl.ds(pl.multiple_of(j * 48 * tiles + 48 * p, 48), 48), :] = value[
                48 * d : 48 * d + 48, 128 * p : 128 * p + 128
            ]


def w_fc_cols(ffn, j):
    blocks = [block(ffn, d, aligned(j * 384, 384)) for d in range(16, 32)]
    return jnp.concatenate(
        [jnp.concatenate([b[192 * p : 192 * p + 192] for b in blocks], axis=0) for p in range(2)], axis=1
    )


def chip_slot(m):
    z, x, y = 2 + m // 4, m // 2 % 2, m % 2
    return z, (y * 2 + x, x * 2 + y)


def w_fc_rows(ffn, m):
    z, at = chip_slot(m)
    return jnp.concatenate(
        [
            jnp.concatenate([ffn[z, c, at[c], 192 * j : 192 * j + 192, :] for j in range(6)], axis=1)
            for c in range(2)
        ],
        axis=0,
    )


def put_w_fc_rows(ffn, m, value, tiles=range(6), base=0):
    z, at = chip_slot(m)
    z = z - base
    for c in range(2):
        for n, j in enumerate(tiles):
            ffn[z, c, at[c], 192 * j : 192 * j + 192, :] = value[192 * c : 192 * c + 192, 128 * n : 128 * n + 128]


def wide(vec, row, n=6):
    return jnp.concatenate([vec[row + j : row + j + 1, :] for j in range(n)], axis=1)


def put_wide(vec, row, value):
    for j in range(value.shape[1] // 128):
        vec[row + j : row + j + 1, :] = value[:, 128 * j : 128 * j + 128]


def lane_ids():
    return lax.broadcasted_iota(jnp.int32, (R, 128), 1)


def attend_pair(qp, kp, vp, dead, lane):
    one, zero = jnp.ones((), bf16), jnp.zeros((), bf16)
    v_one = jnp.concatenate([vp, jnp.ones((R, 128), bf16)], axis=1)
    outs, augmented = [], []
    for h in range(2):
        own = (lane < 64) if h == 0 else (lane >= 64)
        e = 64 if h == 0 else 0
        qh = jnp.where(own, qp, jnp.where(lane == e, one, zero))
        kh = jnp.where(own, kp, jnp.where(lane == e, dead, zero))
        mixed, lses = [], []
        for b in range(3):
            rows = slice(256 * b, 256 * b + 256)
            s = nt(qh[rows], kh)
            top = jnp.max(s, axis=-1, keepdims=True)
            p = jnp.exp(s - top).astype(bf16)
            both = nn(p, v_one)
            total = both[:, 128:]
            mixed.append(both[:, :128] / total)
            lses.append(top + jnp.log(total))
        outs.append(jnp.concatenate(mixed, axis=0))
        hi, mid, low = split3(jnp.concatenate(lses, axis=0))
        for k, part in enumerate((hi, mid, low)):
            qh = jnp.where(lane == e + 1 + k, part, qh)
        augmented.append(qh)
    return jnp.where(lane < 64, outs[0], outs[1]), augmented


def attend_pair_back(q_aug, kp, vp, dop, mixed, dead, lane):
    zero, minus = jnp.zeros((), bf16), -jnp.ones((), bf16)
    weighted = dop.astype(f32) * mixed.astype(f32)
    k_t = kp.T
    dks, dvs, dqs = [], [], []
    for h in range(2):
        own = (lane < 64) if h == 0 else (lane >= 64)
        e = 64 if h == 0 else 0
        dot = jnp.sum(jnp.where(own, weighted, 0.0), axis=-1, keepdims=True)
        do_aug = jnp.where(own, dop, zero)
        for k, part in enumerate(split3(dot)):
            do_aug = jnp.where(lane == e + k, part, do_aug)
        v_aug = jnp.where(own, vp, jnp.where((lane >= e) & (lane < e + 3), minus, zero))
        k_aug = jnp.where(own, kp, jnp.where((lane > e) & (lane < e + 4), minus, jnp.where(lane == e, dead, zero)))
        p = jnp.exp(nt(k_aug, q_aug[h]))
        ds = (p * nt(v_aug, do_aug)).astype(bf16)
        dvs.append(nn(p.astype(bf16), dop))
        dks.append(nn(ds, q_aug[h]))
        dqs.append(nn(k_t, ds))
    row = lax.broadcasted_iota(jnp.int32, (128, R), 0)
    dq = (jnp.where(row < 64, dqs[0], dqs[1]) * 0.125).astype(bf16).T
    dk = jnp.where(lane < 64, dks[0], dks[1]).astype(bf16)
    dv = jnp.where(lane < 64, dvs[0], dvs[1]).astype(bf16)
    return dq, dk, dv


def norm_back(g, xhat, gain, rstd):
    gg = g * gain
    m1 = jnp.mean(gg, axis=-1, keepdims=True)
    m2 = jnp.mean(gg * xhat, axis=-1, keepdims=True)
    return rstd * (gg - m1 - xhat * m2)


def column_sum(v):
    return jnp.sum(v.astype(f32), axis=0, keepdims=True)


ROWS = 128
BLOCKS = R // ROWS


def layer_kernel(gather, scatter, refs):
    length = refs["length"][0]
    x, io = refs["x"], refs["io"]

    def cot_copy(b):
        slot = lax.rem(b, 2)
        return pltpu.make_async_copy(refs["cot"].at[aligned(b * ROWS, ROWS)], refs["cot_b"].at[slot], io.at[6 + slot])

    def out_copy(b):
        slot = lax.rem(b, 2)
        return pltpu.make_async_copy(refs["out_b"].at[slot], refs["out"].at[aligned(b * ROWS, ROWS)], io.at[8 + slot])

    x_copy = pltpu.make_async_copy(refs["x_in"], x, io.at[0])
    x_copy.start()
    cot_copy(0).start()
    attn, ffn, vec, vg = refs["attn"], refs["ffn"], refs["vec"], refs["vg"]
    qx, kk, vv = refs["qx"], refs["k"], refs["v"]
    xh1, rs1, n1 = refs["xh1"], refs["rs1"], refs["n1"]
    act, gp, r2, gf = refs["act"], refs["gp"], refs["r2"], refs["gf"]
    do, mix = n1, refs["mix"]

    def dead_keys():
        row = lax.broadcasted_iota(jnp.int32, (R, 128), 0)
        return jnp.where(row < length, 0.0, -1e30).astype(bf16)

    gather.start()
    x_copy.wait()

    def forward_pair(i, carry):
        gather.before_pair(i)
        lane = lane_ids()
        cols = aligned(i * 128, 128)
        bias = jnp.concatenate(
            [vec[pl.ds(B_Q + i, 1), :], jnp.zeros((1, 128), f32), vec[pl.ds(B_V + i, 1), :]], axis=1
        )
        qkv = (nn(x[...], w_qkv_pair(attn, i)) + bias).astype(bf16)
        qp, kp, vp = qkv[:, :128] * jnp.asarray(0.125, bf16), qkv[:, 128:256], qkv[:, 256:]
        kk[:, cols] = kp
        vv[:, cols] = vp
        mixed, augmented = attend_pair(qp, kp, vp, dead_keys(), lane)
        mix[:, cols] = mixed.astype(bf16)
        for h in range(2):
            qx[:, pl.ds(pl.multiple_of(i * 256 + 128 * h, 128), 128)] = augmented[h]
        return carry

    lax.fori_loop(0, PAIRS, forward_pair, 0)
    gather.step(0)
    for j in range(3):
        cols = slice(256 * j, 256 * j + 256)
        xh1[:, cols] = nn(mix[...], w_out_cols(attn, j)) + wide(vec, B_OUT + 2 * j, 2) + x[:, cols].astype(f32)

    def norm1(b, carry):
        rows = aligned(b * ROWS, ROWS)
        r = xh1[rows, :]
        cen = r - jnp.mean(r, axis=-1, keepdims=True)
        rstd = lax.rsqrt(jnp.mean(cen * cen, axis=-1, keepdims=True) + 1e-05)
        xhat = cen * rstd
        xh1[rows, :] = xhat
        rs1[rows, :] = jnp.broadcast_to(rstd, (ROWS, 128))
        n1[rows, :] = (xhat * wide(vec, G1) + wide(vec, B1)).astype(bf16)
        return carry

    gather.step(1)
    lax.fori_loop(0, BLOCKS, norm1, 0)

    def ffn_in(j, carry):
        gather.before_in(j)
        cols = aligned(j * 256, 256)
        bias = jnp.concatenate([vec[pl.ds(B_IN + 2 * j, 1), :], vec[pl.ds(B_IN + 2 * j + 1, 1), :]], axis=1)
        pre = nn(n1[...], w_in_cols(ffn, j, 2)) + bias
        cdf = 0.5 + 0.5 * lax.erf(pre * 0.7071067811865476)
        act[:, cols] = (pre * cdf).astype(bf16)
        gp[:, cols] = (cdf + pre * (jnp.exp(-0.5 * pre * pre) * 0.3989422804014327)).astype(bf16)
        return carry

    lax.fori_loop(0, 12, ffn_in, 0)

    def ffn_out(j, carry):
        gather.before_out(j)
        cols = aligned(j * 256, 256)
        row = lambda base: jnp.concatenate(
            [vec[pl.ds(base + 2 * j, 1), :], vec[pl.ds(base + 2 * j + 1, 1), :]], axis=1
        )
        n1_full = xh1[:, cols] * row(G1) + row(B1)
        r2[:, cols] = nn(act[...], w_fc_cols(ffn, j)) + row(B_FC) + n1_full
        return carry

    lax.fori_loop(0, 3, ffn_out, 0)
    gather.finish()

    def norm2(b, sums):
        rows = aligned(b * ROWS, ROWS)
        r = r2[rows, :]
        cen = r - jnp.mean(r, axis=-1, keepdims=True)
        rstd = lax.rsqrt(jnp.mean(cen * cen, axis=-1, keepdims=True) + 1e-05)
        xhat = cen * rstd
        pl.when(b + 1 < BLOCKS)(lambda: cot_copy(b + 1).start())
        cot_copy(b).wait()
        pl.when(b >= 2)(lambda: out_copy(b - 2).wait())
        row = lax.broadcasted_iota(jnp.int32, (ROWS, D), 0) + b * ROWS
        valid = jnp.where(row < length, 1.0, 0.0)
        slot = lax.rem(b, 2)
        refs["out_b"][slot] = ((xhat * wide(vec, G2) + wide(vec, B2)) * valid).astype(bf16)
        out_copy(b).start()
        g = refs["cot_b"][slot].astype(f32) * valid
        grad = norm_back(g, xhat, wide(vec, G2), rstd)
        r2[rows, :] = grad
        low = grad.astype(bf16)
        gf[rows, :] = low
        return sums[0] + column_sum(g * xhat), sums[1] + column_sum(g), sums[2] + column_sum(low)

    zeros = jnp.zeros((1, D), f32)
    d_g2, d_b2, d_bfc = lax.fori_loop(0, BLOCKS, norm2, (zeros, zeros, zeros))
    for b in (BLOCKS - 2, BLOCKS - 1):
        out_copy(b).wait()
    put_wide(vg, G2, d_g2)
    put_wide(vg, B2, d_b2)
    put_wide(vg, B_FC, d_bfc)

    def back_first(m, carry):
        scatter.in_first(m)
        grad = tn(act[:, aligned(m * 384, 384)], gf[:, 0:384]).astype(bf16)
        put_w_fc_rows(refs["fc_g"], m, grad, range(0, 3), 2)
        return carry

    lax.fori_loop(0, 4, back_first, 0)

    def back_hidden(m):
        scatter.in_fc(m)
        cols = aligned(m * 384, 384)
        grad_act = nt(gf[...], w_fc_rows(ffn, m))
        low = (grad_act * gp[:, cols].astype(f32)).astype(bf16)
        gp[:, cols] = low
        sums = column_sum(low)
        for j in range(3):
            vg[pl.ds(B_IN + 3 * m + j, 1), :] = sums[:, 128 * j : 128 * j + 128]
        return cols

    def back_near(m, carry):
        cols = back_hidden(m)
        put_w_fc_rows(ffn, m, tn(act[:, cols], gf[:, 384:768]).astype(bf16), range(3, 6))
        return carry

    def back_fc(m, carry):
        cols = back_hidden(m)
        put_w_fc_rows(ffn, m, tn(act[:, cols], gf[...]).astype(bf16))
        return carry

    lax.fori_loop(0, 4, back_near, 0)
    lax.fori_loop(4, 8, back_fc, 0)

    def back_in(j, carry):
        scatter.in_in(j)
        cols = aligned(j * 512, 512)
        g = gp[:, cols]
        r2[...] += nt(g, w_in_cols(ffn, j, 4))
        put_w_in_cols(ffn, j, 4, tn(n1[...], g).astype(bf16))
        return carry

    lax.fori_loop(0, 6, back_in, 0)
    scatter.between(0)

    def back_norm1(b, sums):
        rows = aligned(b * ROWS, ROWS)
        g, xhat = r2[rows, :], xh1[rows, :]
        grad = norm_back(g, xhat, wide(vec, G1), rs1[rows, 0:1])
        r2[rows, :] = grad
        low = grad.astype(bf16)
        gf[rows, :] = low
        return sums[0] + column_sum(g * xhat), sums[1] + column_sum(g), sums[2] + column_sum(low)

    d_g1, d_b1, d_bout = lax.fori_loop(0, BLOCKS, back_norm1, (zeros, zeros, zeros))
    put_wide(vg, G1, d_g1)
    put_wide(vg, B1, d_b1)
    put_wide(vg, B_OUT, d_bout)
    scatter.between(1)

    for half in range(2):
        do[:, 384 * half : 384 * half + 384] = nt(
            gf[...], w_out_rows(attn, range(24 + 4 * half, 28 + 4 * half))
        ).astype(bf16)
    scatter.between(2)
    for half in range(2):
        cols = slice(384 * half, 384 * half + 384)
        grad = tn(mix[:, cols], gf[...]).astype(bf16)
        for d in range(4):
            z, c, s = place(24 + 4 * half + d)
            for j in range(6):
                attn[z, c, s, 96 * j : 96 * j + 96, :] = grad[96 * d : 96 * d + 96, 128 * j : 128 * j + 128]

    def backward_pair(i, carry):
        scatter.pair_start(i)
        lane = lane_ids()
        cols = aligned(i * 128, 128)
        q_aug = [qx[:, pl.ds(pl.multiple_of(i * 256 + 128 * h, 128), 128)] for h in range(2)]
        dq, dk, dv = attend_pair_back(
            q_aug, kk[:, cols], vv[:, cols], do[:, cols], mix[:, cols], dead_keys(), lane
        )
        do[:, cols] = dq
        kk[:, cols] = dk
        vv[:, cols] = dv
        scatter.pair_end(i)
        vg[pl.ds(B_Q + i, 1), :] = column_sum(dq)
        vg[pl.ds(B_V + i, 1), :] = column_sum(dv)
        put_w_qkv_pair(refs["qkv_g"], i, tn(x[...], jnp.concatenate([dq, dk, dv], axis=1)).astype(bf16))
        return carry

    lax.fori_loop(0, PAIRS, backward_pair, 0)
    gin_copies = []
    for n in range(3):
        scatter.tail(n)
        cols = slice(256 * n, 256 * n + 256)
        total = r2[:, cols]
        for p, g in enumerate((do, kk, vv)):
            total = total + nt(g[...], w_qkv_rows(attn, range(8 * n, 8 * n + 8), p))
        mix[:, cols] = total.astype(bf16)
        gin_copies.append(pltpu.make_async_copy(mix.at[:, cols], refs["gin"].at[:, cols], io.at[1 + n]))
        gin_copies[-1].start()
    scatter.tail(3)
    for copy in gin_copies:
        copy.wait()


class Loaded:
    def __init__(self, refs):
        self.refs = refs

    def start(self):
        r = self.refs
        copies = [
            pltpu.make_async_copy(r["attn_in"], r["attn"], r["io"].at[8]),
            pltpu.make_async_copy(r["ffn_in"], r["ffn"], r["io"].at[9]),
        ]
        for c in copies:
            c.start()
        r["vec"][...] = r["vec_in"][...].astype(f32)
        for c in copies:
            c.wait()

    def before_pair(self, i):
        pass

    before_in = before_out = step = before_pair

    def finish(self):
        pass


def position():
    dp, fs = lax.axis_index("dp"), lax.axis_index("fsdp")
    return lax.div(dp, 2), lax.rem(dp, 2), lax.div(fs, 2), lax.rem(fs, 2)


def device(z, x, y, c):
    return (z * 2 + x, y * 2 + c)


def remote(src, dst, send, recv, target):
    return pltpu.make_async_remote_copy(
        src_ref=src, dst_ref=dst, send_sem=send, recv_sem=recv, device_id=target, device_id_type=MESH
    )


ATT_GROUPS = (288, 288)
FFN_GROUPS = (192, 96, 192, 192, 192, 288)
PLANE_GROUPS = 2
Z, PASS, A, B, C, HOP = range(1, 7)
VECTOR_MARKS = (3003, 4003, 5003)
GATHER_ENDS = {
    0: (3020, 3030, 1000, 1010, 1040, 3000, 3040, 3050, 3060, 3010, 3070, 4020, 4030, 4000, 3001, 4040, 3011, 6020, 4010, 6030, 1050, 1060, 1070, 3002, 3003, 4001, 5000, 4011, 5040, 4002, 3012, 4003, 6021, 5010, 6031, 4012, 5001, 3013, 5011, 3041, 5002, 3051, 4050, 4013, 3061, 3042, 5003,),
    2: (4041, 3043, 3052, 4042, 4051, 3071, 5012, 5050,),
    4: (4060, 3062, 5013,),
    6: (5041, 4043, 6022, 4052,),
    8: (5042, 5051, 4061, 6032, 4070, 3072, 5060,),
    10: (5043, 5052, 3053, 3063, 4062,),
    12: (5061, 4071, 3073,),
    13: (5070, 5062, 4053, 4063, 4072,),
    14: (6023, 5071, 4073,),
    15: (5053, 6033, 5063,),
    17: (5072,),
    18: (5073,),
}
GATHER_MIDDLE = {
    0: (3020, 3030, 1000, 1010, 3000, 3040, 3050, 3060, 3010, 3070, 4020, 4030, 4000, 4040, 3002, 2003, 3003, 6020, 3001, 4010, 6030, 3012, 4002, 2013, 1040, 1050, 1060, 1070, 5000, 4003, 3011, 3013, 5040, 4001, 2043, 3043, 3041, 4012, 5010, 4011, 6022, 4013, 6021, 5002, 6032, 3042, 6031, 5003, 5001, 2053, 3053, 3051, 3052,),
    2: (4041, 5012,),
    4: (2063, 4050, 3061, 4042, 4051, 3062, 3063, 5011, 5013,),
    6: (2073, 5041, 4060, 3071, 3072, 3073,),
    8: (5050, 5042, 4043, 4052,),
    10: (5051, 4061,),
    12: (6023, 5060, 4070, 5043, 4053,),
    13: (6033, 5052, 5061, 4062, 4071,),
    14: (5070, 5053, 4063, 4072,),
    15: (5062, 4073,),
    16: (5071,),
    17: (5063,),
    19: (5072, 5073,),
}
SCATTER = {
    0: (100, 101,),
    2: (200, 201,),
    4: (102, 103,),
    5: (202,),
    6: (300, 203,),
    7: (301,),
    8: (302, 104, 105, 106, 107,),
    9: (400, 204, 205, 206, 108,),
    10: (401, 402, 303, 207, 208, 109,),
    11: (304, 209, 110,),
    12: (403, 210, 305, 111, 500,),
    13: (211, 404, 112,),
    14: (306, 212, 113,),
    15: (501, 405, 307, 213, 406,),
    16: (502, 308,),
    17: (114,),
    19: (503, 309, 407, 214, 408,),
    20: (310, 504, 115,),
    22: (409, 311, 215,),
    23: (116, 505,),
    25: (410, 411, 312, 216,),
    26: (506, 313, 117,),
    28: (508, 509, 412, 217,),
    29: (507, 118,),
    31: (314, 413, 315, 510, 218,),
    32: (316, 119,),
    34: (414, 511, 317, 219,),
    35: (415, 318, 120,),
    36: (416, 220,),
    37: (512, 417,),
    38: (418, 319, 513, 320, 419, 515, 420, 514, 516, 517, 518, 519, 520,),
}

ATT, FFN = 0, 1


def group_of(g):
    if g < len(ATT_GROUPS):
        return ATT, pl.ds(sum(ATT_GROUPS[:g]), ATT_GROUPS[g])
    g -= len(ATT_GROUPS)
    return FFN, pl.ds(sum(FFN_GROUPS[:g]), FFN_GROUPS[g])


ATT_HEAD, FFN_HEAD = 30, 42

N_GROUPS = len(ATT_GROUPS) + len(FFN_GROUPS)
PLANE_ROWS = sum(FFN_GROUPS[:PLANE_GROUPS])


def is_plane_group(g):
    return len(ATT_GROUPS) <= g < len(ATT_GROUPS) + PLANE_GROUPS


class Gather:
    def __init__(self, refs):
        self.refs = refs
        self.z, self.x, self.y, self.c = z, x, y, c = position()
        self.me = z * 8 + x * 4 + y * 2 + c
        first = c == 0
        a, b = jnp.where(first, x, y), jnp.where(first, y, x)
        self.slot, self.pair = b * 2 + a, b * 2
        self.other_slot, self.other_pair = b * 2 + 1 - a, (1 - b) * 2
        self.dev_a = device(z, jnp.where(first, 1 - x, x), jnp.where(first, y, 1 - y), c)
        self.dev_b = device(z, jnp.where(first, x, 1 - x), jnp.where(first, 1 - y, y), c)
        self.dev_c = device(z, x, y, 1 - c)
        self.zs = [lax.rem(z + k, 4) for k in (1, 2, 3)]
        self.dev_z = [device(t, x, y, c) for t in self.zs]
        upper = lax.div(z, 2)
        self.near = [z, z + 1 - 2 * lax.rem(z, 2), 2 - upper, 3 - 3 * upper]
        self.dev_near = [device(t, x, y, c) for t in self.near]
        self.is_end = (z == 0) | (z == 3)
        self.is_middle = (z == 1) | (z == 2)
        self.from_me = 2 + jnp.where(self.is_end, 1, 0)
        self.half = upper * 2
        self.other_half = 2 - upper * 2
        last = lax.rem(self.me + 1, 32)
        before = lax.rem(self.me + 31, 32)
        self.dev_after = (lax.div(last, 4), lax.rem(last, 4))
        self.dev_before = (lax.div(before, 4), lax.rem(before, 4))
        self.buf = (refs["attn"], refs["ffn"])

    def barrier(self):
        bar = pltpu.get_barrier_semaphore()
        targets = [self.dev_a, self.dev_b, self.dev_c, self.dev_after, self.dev_before] + self.dev_z
        for t in targets:
            pl.semaphore_signal(bar, inc=1, device_id=t, device_id_type=MESH)
        pl.semaphore_wait(bar, len(targets))

    def z_copy(self, g, k):
        kind, rows = group_of(g)
        ref = self.buf[kind].at[self.z, self.c, self.slot, rows]
        index = 1 if k == 1 else self.from_me
        r = self.refs
        return remote(ref, ref, r["gs"].at[8 + 3 * kind + k - 1], r["zr"].at[g, index], self.dev_near[k])

    def pass_copy(self, g):
        kind, rows = group_of(g)
        ref = self.buf[kind].at[self.near[3], self.c, self.slot, rows]
        return remote(ref, ref, self.refs["gs"].at[14 + kind], self.refs["zr"].at[g, 3], self.dev_near[1])

    def z_arrival(self, g, k):
        kind, rows = group_of(g)
        wide_ = pl.ds(0, 4) if is_plane_group(g) else self.slot
        ref = self.buf[kind].at[self.near[k], self.c, wide_, rows]
        return remote(ref, ref, self.refs["gs"].at[8], self.refs["zr"].at[g, k], self.dev_near[1])

    def hop_copy(self, g, k, n):
        _, rows = group_of(g)
        layer = self.near[max(n - 1, 0)]
        ref = self.refs["ffn"].at[layer, self.c, :, rows]
        target = self.dev_near[2 if n in (1, 2) else 1]
        index = (1, 2, 3, 2, 3)[n]
        return remote(ref, ref, self.refs["gs"].at[16 + n], self.refs["zr"].at[g, index], target)

    def plane_copy(self, step, g, k):
        kind, rows = group_of(g)
        r = self.refs
        at = self.buf[kind].at[self.near[k], self.c]
        later = 0 if kind == ATT else 1 if k == 0 else 2
        if step == A:
            src, send, recv, target = at.at[self.slot, rows], later, "ar", self.dev_a
        elif step == B:
            src, send, recv, target = at.at[pl.ds(self.pair, 2), rows], 3 + later, "br", self.dev_b
        else:
            src, send, recv, target = at.at[:, rows], 6 + kind, "cr", self.dev_c
        return remote(src, src, r["gs"].at[send], r[recv].at[g, k], target)

    def run(self, code):
        kind, g, k = code // 1000, code // 10 % 100, code % 10
        if kind == Z:
            self.z_copy(g, 1).start()
            self.z_copy(g, 2).start()
            pl.when(self.is_middle)(lambda: self.z_copy(g, 3).start())
            return
        if kind == PASS:
            self.z_arrival(g, 3).wait_recv()
            self.pass_copy(g).start()
            return
        if kind == HOP:
            if k == 0:
                self.plane_copy(B, g, 0).wait_recv()
                self.hop_copy(g, 0, 0).start()
                pl.when(self.is_middle)(lambda: self.hop_copy(g, 0, 1).start())
            else:
                self.z_arrival(g, k).wait_recv()
                pl.when(self.is_middle)(lambda: self.hop_copy(g, k, k + 1).start())
            self.plane_copy(C, g, k).start()
            return
        if kind == A and k in (1, 2):
            self.z_arrival(g, k).wait_recv()
        elif kind == A and k == 3:
            pl.when(self.is_end)(lambda: self.z_arrival(g, 3).wait_recv())
        elif kind == B:
            self.plane_copy(A, g, k).wait_recv()
        elif kind == C:
            self.plane_copy(B, g, k).wait_recv()
        self.plane_copy(kind, g, k).start()

    def ready(self, g, first, count):
        kind, rows = group_of(g)
        r = self.refs
        for n in range(count):
            ref = self.buf[kind].at[0, 1 - self.c, :, rows]
            remote(ref, ref, r["gs"].at[6 + kind], r["cr"].at[g, first + n], self.dev_c).wait_recv()

    def steps(self, key):
        for who, table in ((self.is_end, GATHER_ENDS), (self.is_middle, GATHER_MIDDLE)):
            if key in table:

                @pl.when(who)
                def _(table=table):
                    for s in table[key]:
                        self.run(s)

    def vectors(self, stage):
        r = self.refs
        buf, own, v = r["vec_all"], r["tail"], r["vsem"]
        one = buf.at[self.c, self.slot]
        if stage == 0:

            @pl.when(self.z == 3)
            def _():
                one[...] = own[...]
                for k in range(3):
                    remote(own, one, v.at[4 + k], v.at[1], self.dev_z[k]).start()

        elif stage == 1:

            @pl.when(self.z == 3)
            def _():
                for k in range(3):
                    remote(own, one, v.at[4 + k], v.at[1], self.dev_z[k]).wait_send()

            @pl.when(self.z != 3)
            def _():
                remote(one, one, v.at[4], v.at[1], self.dev_z[0]).wait_recv()

            remote(one, one, v.at[7], v.at[2], self.dev_a).start()
        elif stage == 2:
            got = buf.at[self.c, self.other_slot]
            remote(got, got, v.at[7], v.at[2], self.dev_a).wait()
            mine = buf.at[self.c, pl.ds(self.pair, 2)]
            remote(mine, mine, v.at[8], v.at[3], self.dev_b).start()
        elif stage == 3:
            got = buf.at[self.c, pl.ds(self.other_pair, 2)]
            remote(got, got, v.at[8], v.at[3], self.dev_b).wait()
            mine = buf.at[self.c]
            remote(mine, mine, v.at[9], v.at[10], self.dev_c).start()
        else:
            got = buf.at[1 - self.c]
            remote(got, got, v.at[9], v.at[10], self.dev_c).wait()
            r["vec"][...] = buf[1, 3].astype(f32)

    def tail_copy(self):
        t = self.refs["tail"]
        return remote(t, self.refs["tail_in"], self.refs["vsem"].at[11], self.refs["vsem"].at[12], self.dev_after)

    def load_own(self):
        r = self.refs
        flat_a, flat_f = r["flat_a"], r["flat_f"]
        own_a, own_f = r["attn_own"], r["ffn_own"]
        whole_a, whole_f = ATT_ROWS * 128, FFN_ROWS * 128
        flat_a[ATT_HEAD + ATT_ROWS : ATT_HEAD + ATT_ROWS + 16, :] = jnp.zeros((16, 128), f32)
        flat_f[FFN_HEAD + FFN_ROWS : FFN_HEAD + FFN_ROWS + 16, :] = jnp.zeros((16, 128), f32)
        flat_a[pl.ds(ATT_HEAD, ATT_ROWS), :] = own_a[0:whole_a].reshape(ATT_ROWS, 128).astype(f32)
        flat_f[pl.ds(FFN_HEAD, FFN_ROWS), :] = own_f[0:whole_f].reshape(FFN_ROWS, 128).astype(f32)
        at = ATT_HEAD + ATT_ROWS
        flat_a[at : at + 1, 0:120] = own_a[whole_a : whole_a + 120].reshape(1, 120).astype(f32)
        at = FFN_HEAD + FFN_ROWS
        flat_f[at : at + 1, :] = own_f[whole_f : whole_f + 128].reshape(1, 128).astype(f32)
        flat_f[at + 1 : at + 2, 0:40] = own_f[whole_f + 128 : whole_f + 168].reshape(1, 40).astype(f32)
        lane = lax.broadcasted_iota(jnp.int32, (32, 128), 1)
        v = pltpu.roll(flat_a[ATT_HEAD + 546 : ATT_HEAD + 586, :], 8, 1)
        r["tail"][0:32, :] = jnp.where(lane < 8, v[0:32], v[1:33]).astype(bf16)
        lane = lax.broadcasted_iota(jnp.int32, (48, 128), 1)
        v = pltpu.roll(flat_f[FFN_HEAD + 1111 : FFN_HEAD + 1167, :], 88, 1)
        r["tail"][32:80, :] = jnp.where(lane < 88, v[0:48], v[1:49]).astype(bf16)

    def place_own(self, kind):
        r = self.refs
        if kind == ATT:
            flat, rows, head, size, moved, at = r["flat_a"], r["attn_sum"], ATT_HEAD, ATT_ROWS, 120, 0
        else:
            flat, rows, head, size, moved, at = r["flat_f"], r["ffn_sum"], FFN_HEAD, FFN_ROWS, 168, 32
        flat[0:head, :] = r["tail_in"][at : at + head, :].astype(f32)
        shift = head * 128 - moved * self.me

        def step(n, carry):
            rows[pl.ds(pl.multiple_of(n * 64, 64), 64), :] = self.shifted(flat, shift, n)
            return carry

        lax.fori_loop(0, size // 64, step, 0)
        slot = self.buf[kind].at[self.z, self.c, self.slot]
        self.by_kind(kind, lambda tiles, n, at: self.to_tiles(rows, slot, tiles, n, at))

    def by_kind(self, kind, fn):
        if kind == ATT:
            pl.when(self.z < 3)(lambda: fn(18, 32, lambda t: (t % 6 * 3 + t // 6) * 32))
            pl.when(self.z == 3)(lambda: fn(6, 96, lambda t: t * 96))
        else:
            pl.when(self.z < 2)(lambda: fn(24, 48, lambda t: t * 48))
            pl.when(self.z >= 2)(lambda: fn(6, 192, lambda t: t * 192))

    def to_tiles(self, rows, slot, tiles, n, at):
        for t in range(tiles):
            slot[at(t) : at(t) + n, :] = rows[pl.ds(t, n, stride=tiles), :].astype(bf16)

    def from_tiles(self, total, flat, tiles, n, at):
        for t in range(tiles):
            flat[pl.ds(t, n, stride=tiles), :] = total[at(t) : at(t) + n, :]

    def shifted(self, src, shift, n):
        row, turn = lax.div(shift, 128), lax.rem(shift, 128)
        lane = lax.broadcasted_iota(jnp.int32, (64, 128), 1)
        back = lax.rem(128 - turn, 128)
        low = pltpu.roll(src[pl.ds(n * 64 + row, 64), :], back, 1)
        high = pltpu.roll(src[pl.ds(n * 64 + row + 1, 64), :], back, 1)
        return jnp.where(lane < 128 - turn, low, high)

    def start(self):
        self.load_own()
        self.barrier()
        pl.when(self.me < 31)(lambda: self.tail_copy().start())
        self.vectors(0)
        pl.when(self.me > 0)(lambda: self.tail_copy().wait_recv())
        self.place_own(ATT)
        for g in range(len(ATT_GROUPS)):
            self.run(1000 * Z + 10 * g)
        self.place_own(FFN)
        for who, table in ((self.is_end, GATHER_ENDS), (self.is_middle, GATHER_MIDDLE)):

            @pl.when(who)
            def _(table=table):
                first = [v for v in table[0] if v >= 1000 * Z + 10 * len(ATT_GROUPS)]
                cuts = [0] + [first.index(v) + 1 for v in VECTOR_MARKS] + [len(first)]
                for stage in range(4):
                    for s in first[cuts[stage] : cuts[stage + 1]]:
                        self.run(s)
                    self.vectors(stage + 1)

    def before_pair(self, i):
        for v in range(PAIRS):

            @pl.when(i == v)
            def _(v=v):
                if v:
                    self.steps(2 * v)
                if v * len(ATT_GROUPS) % PAIRS == 0:
                    self.ready(v * len(ATT_GROUPS) // PAIRS, 0, 4)

    def step(self, n):
        self.steps(12 + n)

    def before_in(self, j):
        at = 0
        for n, rows in enumerate(FFN_GROUPS):

            @pl.when(j == at // 96)
            def _(n=n):
                self.steps(14 + n)
                self.ready(len(ATT_GROUPS) + n, self.half, 2)

            at += rows

    def before_out(self, j):
        seen = 0
        for v in range(3):
            more, at = [], 0
            for n, rows in enumerate(FFN_GROUPS):
                if n >= seen and at < 384 * (v + 1):
                    more.append(n)
                at += rows
            seen += len(more)

            @pl.when(j == v)
            def _(v=v, more=more):
                self.steps(14 + len(FFN_GROUPS) + v)
                for n in more:
                    self.ready(len(ATT_GROUPS) + n, self.other_half, 2)

    def finish(self):
        self.steps(17 + len(FFN_GROUPS))
        r = self.refs
        z, c, gs = self.z, self.c, r["gs"]
        attn, ffn = self.buf
        rest = pl.ds(PLANE_ROWS, FFN_ROWS - PLANE_ROWS)
        front = pl.ds(0, PLANE_ROWS)

        def sent(n, ref):
            remote(ref, ref, gs.at[n], r["zr"].at[0, 0], self.dev_c).wait_send()

        sent(0, attn.at[:, c, self.slot])
        sent(1, ffn.at[z, c, self.slot])
        sent(2, ffn.at[pl.ds(0, 3), c, self.slot, rest])
        sent(3, attn.at[:, c, pl.ds(self.pair, 2)])
        sent(4, ffn.at[z, c, pl.ds(self.pair, 2)])
        sent(5, ffn.at[pl.ds(0, 3), c, pl.ds(self.pair, 2), rest])
        sent(6, attn.at[:, c])
        sent(7, ffn.at[:, c])
        for k in range(2):
            sent(8 + k, attn.at[z, c, self.slot])
            sent(11 + k, ffn.at[z, c, self.slot, rest])
        if PLANE_GROUPS:
            sent(16, ffn.at[z, c, :, front])

        @pl.when(self.is_middle)
        def _():
            sent(10, attn.at[z, c, self.slot])
            sent(13, ffn.at[z, c, self.slot, rest])
            sent(14, attn.at[z, c, self.slot])
            sent(15, ffn.at[z, c, self.slot, rest])
            if PLANE_GROUPS:
                for n in range(17, 21):
                    sent(n, ffn.at[z, c, :, front])

        pl.when(self.me < 31)(lambda: self.tail_copy().wait_send())


W_FC, W_IN, W_OUT, W_QKV = 0, 8, 14, 15
N_ITEMS = W_QKV + PAIRS


class Scatter:
    def __init__(self, refs, gather):
        self.refs, self.g = refs, gather

    def part(self, item):
        if item < 2:
            return "fc_g", "ffn", range(2, 3), pl.ds(288 * item, 288), 288, 0
        if item >= W_QKV:
            return "qkv_g", "attn", range(0, 3), pl.ds(96 * (item - W_QKV), 96), 96, 2
        if item == W_OUT:
            return "attn", "attn", range(3, 4), pl.ds(0, 576), 576, 1
        if item >= W_IN:
            return "ffn", "ffn", range(0, 2), pl.ds(192 * (item - W_IN), 192), 192, 0
        z = 2 + item // 4
        return "ffn", "ffn", range(z, z + 1), pl.ds(288 * (item % 4), 288), 288, 0

    def span(self, zz):
        return pl.ds(zz[0], len(zz))

    def at(self, buf, z):
        return z - 2 if buf == "fc_g" else z

    def add(self, pairs, rows, count):
        def step(n, carry):
            at = pl.ds(pl.multiple_of(rows.start + n * 96, 96), 96)
            for dst, src in pairs:
                d = dst.at[at]
                d[...] = d[...] + src.at[at][...]
            return carry

        if count == 96:
            step(0, 0)
        else:
            lax.fori_loop(0, count // 96, step, 0)

    def c_copy(self, g):
        buf, kind, zz, rows, _, s = self.part(g)
        r, t = self.refs, self.g
        return remote(
            r[buf].at[self.span([self.at(buf, z) for z in zz]), 1 - t.c, :, rows],
            r[kind + "_rc"].at[self.span(zz), :, rows],
            r["ss"].at[s, 0],
            r["sr"].at[0, g],
            t.dev_c,
        )

    def b_copy(self, g):
        buf, kind, zz, rows, _, s = self.part(g)
        r, t = self.refs, self.g
        return remote(
            r[buf].at[self.span([self.at(buf, z) for z in zz]), t.c, pl.ds(t.other_pair, 2), rows],
            r[kind + "_rb"].at[self.span(zz), :, rows],
            r["ss"].at[s, 1],
            r["sr"].at[1, g],
            t.dev_b,
        )

    def a_copy(self, g):
        buf, kind, zz, rows, _, s = self.part(g)
        r, t = self.refs, self.g
        return remote(
            r[buf].at[self.span([self.at(buf, z) for z in zz]), t.c, t.other_slot, rows],
            r[kind + "_ra"].at[self.span(zz), rows],
            r["ss"].at[s, 2],
            r["sr"].at[2, g],
            t.dev_a,
        )

    def z_copy(self, g, k):
        buf, kind, zz, rows, _, s = self.part(g)
        r, t = self.refs, self.g
        return remote(
            r[buf].at[self.at(buf, t.zs[k]), t.c, t.slot, rows],
            r[kind + "_rz"].at[k, rows],
            r["ss"].at[s, 3 + k],
            r["sr"].at[3, g],
            t.dev_z[k],
        )

    def inside(self, value, zz):
        return (value >= zz[0]) & (value <= zz[-1])

    def c_send(self, g):
        self.c_copy(g).start()

    def b_send(self, g):
        buf, kind, zz, rows, n, _ = self.part(g)
        r, t = self.refs, self.g
        self.c_copy(g).wait_recv()
        self.add([(r[buf].at[self.at(buf, z), t.c, i], r[kind + "_rc"].at[z, i]) for z in zz for i in range(4)], rows, n)
        self.b_copy(g).start()

    def a_send(self, g):
        buf, kind, zz, rows, n, _ = self.part(g)
        r, t = self.refs, self.g
        self.b_copy(g).wait_recv()
        self.add([(r[buf].at[self.at(buf, z), t.c, t.pair + i], r[kind + "_rb"].at[z, i]) for z in zz for i in range(2)], rows, n)
        self.a_copy(g).start()

    def z_send(self, g):
        buf, kind, zz, rows, n, _ = self.part(g)
        r, t = self.refs, self.g
        self.a_copy(g).wait_recv()
        self.add([(r[buf].at[self.at(buf, z), t.c, t.slot], r[kind + "_ra"].at[z]) for z in zz], rows, n)
        for k in range(3):

            @pl.when(self.inside(t.zs[k], zz))
            def _():
                self.z_copy(g, k).start()

    def take(self, g):
        buf, kind, zz, rows, n, _ = self.part(g)
        r, t = self.refs, self.g

        @pl.when(self.inside(t.z, zz))
        def _():
            got = r[kind + "_rz"].at[:, rows]
            remote(got, got, r["ss"].at[0, 3], r["sr"].at[3, g], t.dev_c).wait_recv()

            def step(i, carry):
                at = pl.ds(pl.multiple_of(rows.start + i * 96, 96), 96)
                total = r[buf][self.at(buf, t.z), t.c, t.slot, at, :].astype(f32)
                for k in range(3):
                    total = total + r[kind + "_rz"][k, at, :].astype(f32)
                r[kind + "_sum"][at, :] = total
                return carry

            lax.fori_loop(0, n // 96, step, 0)

    def vectors(self, stage):
        r, t = self.refs, self.g
        own, got, s, v = r["vg"], r["vg_r"], r["vs"], r["vr"]
        if stage > 0:
            target = (t.dev_c, t.dev_b, t.dev_a)[stage - 1]
            remote(own, got.at[stage - 1], s.at[stage - 1], v.at[stage - 1], target).wait()
            own[...] = own[...] + got[stage - 1]
        if stage < 3:
            target = (t.dev_c, t.dev_b, t.dev_a)[stage]
            remote(own, got.at[stage], s.at[stage], v.at[stage], target).start()
        else:
            for k in range(3):

                @pl.when(t.zs[k] == 3)
                def _():
                    remote(own, got.at[3 + k], s.at[3 + k], v.at[3 + k], t.dev_z[k]).start()

    def take_vectors(self):
        r, t = self.refs, self.g
        own, got, s, v = r["vg"], r["vg_r"], r["vs"], r["vr"]
        for k in range(3):

            @pl.when(t.zs[k] == 3)
            def _():
                remote(own, got.at[3 + k], s.at[3 + k], v.at[3 + k], t.dev_z[k]).wait_send()

        @pl.when(t.z == 3)
        def _():
            for k in range(3):
                remote(own, got.at[3 + k], s.at[3 + k], v.at[3 + k], t.dev_z[k]).wait_recv()
            own[...] = own[...] + got[3] + got[4] + got[5]

    def sent(self):
        r, t = self.refs, self.g
        ss = r["ss"]

        def one(s, n, ref):
            remote(ref, ref, ss.at[s, n], r["sr"].at[0, 0], t.dev_c).wait_send()

        for s, ref in enumerate((r["ffn"], r["attn"].at[pl.ds(3, 1)], r["qkv_g"])):
            one(s, 0, ref.at[:, 1 - t.c])
            one(s, 1, ref.at[:, t.c, pl.ds(t.other_pair, 2)])
            one(s, 2, ref.at[:, t.c, t.other_slot])
        for k in range(3):
            one(0, 3 + k, r["ffn"].at[0, t.c, t.slot])
            pl.when(t.zs[k] == 3)(lambda k=k: one(1, 3 + k, r["attn"].at[3, t.c, t.slot]))
            pl.when(t.zs[k] != 3)(lambda k=k: one(2, 3 + k, r["qkv_g"].at[0, t.c, t.slot]))

    def step(self, key):
        for s in SCATTER.get(key, ()):
            self.one(s)

    def one(self, s):
        kinds = (None, self.c_send, self.b_send, self.a_send, self.z_send, self.take)
        kinds[s // 100](s % 100)

    def loop(self, i, first, stride, count):
        for v in range(count):
            if first + stride * v in SCATTER:
                pl.when(i == v)(lambda v=v: self.step(first + stride * v))

    def in_first(self, m):
        self.loop(m, 40, 1, 4)

    def in_fc(self, m):
        self.loop(m, 0, 1, 8)

    def in_in(self, j):
        self.loop(j, 8, 1, 6)

    def between(self, n):
        self.step(14 + n)

    def pair_start(self, i):
        self.loop(i, 17, 3, PAIRS)

    def pair_end(self, i):
        self.loop(i, 19, 3, PAIRS)

    def tail(self, n):
        if n < 3:
            self.step(35 + n)
            self.vectors(n)
            return
        self.vectors(3)
        order = SCATTER[38]
        ffn_left = max(i for i, s in enumerate(order) if s // 100 == 5 and s % 100 < W_OUT) + 1
        relays_left = max(i for i, s in enumerate(order) if s // 100 < 5) + 1
        for s in order[:ffn_left]:
            self.one(s)
        self.hand_over(FFN)
        for s in order[ffn_left:relays_left]:
            self.one(s)
        self.take_vectors()
        self.finish(FFN)
        for s in order[relays_left:]:
            self.one(s)
        self.hand_over(ATT)
        self.finish(ATT)
        self.sent()

    def head_copy(self, kind):
        r, t = self.refs, self.g
        count = (32, 48)[kind]
        head, got = r[("flat_a", "flat_f")[kind]].at[pl.ds(0, count)], r["head_in"].at[pl.ds(32 * kind, count)]
        return remote(head, got, r["hs"].at[2 * kind], r["hs"].at[2 * kind + 1], t.dev_before)

    def hand_over(self, kind):
        r, t = self.refs, self.g
        total, flat = r[("attn_sum", "ffn_sum")[kind]], r[("flat_a", "flat_f")[kind]]
        t.by_kind(kind, lambda tiles, n, at: t.from_tiles(total, flat, tiles, n, at))
        pl.when(t.me > 0)(self.head_copy(kind).start)

    def finish(self, kind):
        r, t = self.refs, self.g
        size, count, moved = ((ATT_ROWS, 32, 120), (FFN_ROWS, 48, 168))[kind]
        flat, out = r[("flat_a", "flat_f")[kind]], r[("attn_out", "ffn_out")[kind]]
        copy = self.head_copy(kind)
        pl.when(t.me < 31)(copy.wait_recv)
        mine = jnp.where(t.me == 31, r["vg"][32 * kind : 32 * kind + count, :], r["head_in"][32 * kind : 32 * kind + count, :])
        flat[size : size + count, :] = mine

        def step(n, carry):
            out[pl.ds(pl.multiple_of(n * 8192, 8192), 8192)] = t.shifted(flat, moved * t.me, n).reshape(8192)
            return carry

        lax.fori_loop(0, size // 64, step, 0)
        whole = size * 128
        rest = t.shifted(flat, moved * t.me, size // 64)
        if kind == ATT:
            out[whole : whole + 120] = rest[0:1, 0:120].reshape(120)
        else:
            out[whole : whole + 128] = rest[0:1, :].reshape(128)
            out[whole + 128 : whole + 168] = rest[1:2, 0:40].reshape(40)
        pl.when(t.me > 0)(copy.wait_send)


class Kept:
    def in_fc(self, m):
        pass

    in_first = in_in = between = pair_start = pair_end = tail = in_fc


SCRATCH = dict(
    x=((R, D), bf16),
    mix=((R, D), bf16),
    cot_b=((2, ROWS, D), bf16),
    out_b=((2, ROWS, D), bf16),
    attn=((4, 2, 4, ATT_ROWS, 128), bf16),
    ffn=((4, 2, 4, FFN_ROWS, 128), bf16),
    vec=((VEC_ROWS, 128), f32),
    qx=((R, 1536), bf16),
    k=((R, D), bf16),
    v=((R, D), bf16),
    xh1=((R, D), f32),
    rs1=((R, 128), f32),
    n1=((R, D), bf16),
    act=((R, FF), bf16),
    gp=((R, FF), bf16),
    r2=((R, D), f32),
    gf=((R, D), bf16),
    qkv_g=((3, 2, 4, ATT_ROWS, 128), bf16),
    fc_g=((1, 2, 4, FFN_ROWS // 2, 128), bf16),
)


def run_layer(linked, length, x, cot, attn_in, ffn_in, vec_in=None):
    dma = pltpu.SemaphoreType.DMA
    vmem, anywhere = pl.BlockSpec(memory_space=pltpu.VMEM), pl.BlockSpec(memory_space=pl.ANY)
    names = ["length", "x_in", "cot"] + (["attn_own", "ffn_own"] if linked else ["attn_in", "ffn_in", "vec_in"])
    names += ["out", "gin"] + (["attn_out", "ffn_out"] if linked else ["attn_g", "ffn_g", "vg"])
    more = dict(io=dma((10,)))
    if linked:
        more.update(
            vg=pltpu.VMEM((VEC_ROWS, 128), f32),
            vec_all=pltpu.VMEM((2, 4, VEC_ROWS, 128), bf16),
            tail=pltpu.VMEM((VEC_ROWS, 128), bf16),
            tail_in=pltpu.VMEM((VEC_ROWS, 128), bf16),
            head_in=pltpu.VMEM((VEC_ROWS, 128), f32),
            flat_a=pltpu.VMEM((704, 128), f32),
            flat_f=pltpu.VMEM((1280, 128), f32),
            gs=dma((21,)),
            zr=dma((N_GROUPS, 4)),
            ar=dma((N_GROUPS, 4)),
            br=dma((N_GROUPS, 4)),
            cr=dma((N_GROUPS, 4)),
            vsem=dma((13,)),
            ss=dma((3, 6)),
            sr=dma((4, N_ITEMS)),
            vs=dma((6,)),
            vr=dma((6,)),
            hs=dma((4,)),
            vg_r=pltpu.VMEM((6, VEC_ROWS, 128), f32),
        )
        for kind, rows in (("attn", ATT_ROWS), ("ffn", FFN_ROWS)):
            more[kind + "_rc"] = pltpu.VMEM((4, 4, rows, 128), bf16)
            more[kind + "_rb"] = pltpu.VMEM((4, 2, rows, 128), bf16)
            more[kind + "_ra"] = pltpu.VMEM((4, rows, 128), bf16)
            more[kind + "_rz"] = pltpu.VMEM((3, rows, 128), bf16)
            more[kind + "_sum"] = pltpu.VMEM((rows, 128), f32)
    names += list(SCRATCH) + list(more)
    scratch = [pltpu.VMEM(*s) for s in SCRATCH.values()] + list(more.values())

    def body(*args):
        refs = dict(zip(names, args, strict=True))
        refs["vg"][...] = jnp.zeros((VEC_ROWS, 128), f32)
        if linked:
            gather = Gather(refs)
            layer_kernel(gather, Scatter(refs, gather), refs)
            return
        layer_kernel(Loaded(refs), Kept(), refs)
        copies = [
            pltpu.make_async_copy(refs["qkv_g"], refs["attn_g"].at[0:3], refs["io"].at[0]),
            pltpu.make_async_copy(refs["attn"].at[3], refs["attn_g"].at[3], refs["io"].at[1]),
            pltpu.make_async_copy(refs["ffn"].at[0:2], refs["ffn_g"].at[0:2], refs["io"].at[2]),
            pltpu.make_async_copy(refs["fc_g"], refs["ffn_g"].at[2:3, :, :, 0:576], refs["io"].at[3]),
            pltpu.make_async_copy(refs["ffn"].at[2:3, :, :, 576:], refs["ffn_g"].at[2:3, :, :, 576:], refs["io"].at[4]),
            pltpu.make_async_copy(refs["ffn"].at[3], refs["ffn_g"].at[3], refs["io"].at[5]),
        ]
        for c in copies:
            c.start()
        for c in copies:
            c.wait()

    act_out = jax.ShapeDtypeStruct((R, D), bf16)
    if linked:
        grads = tuple(jax.ShapeDtypeStruct(a.shape, f32) for a in (attn_in, ffn_in))
    else:
        grads = tuple(jax.ShapeDtypeStruct(SCRATCH[k][0], bf16) for k in ("attn", "ffn"))
        grads += (jax.ShapeDtypeStruct((VEC_ROWS, 128), f32),)
    smem = pl.BlockSpec(memory_space=pltpu.SMEM)
    args = (length, x, cot, attn_in, ffn_in) + (() if linked else (vec_in,))
    return pl.pallas_call(
        body,
        out_shape=(act_out, act_out) + grads,
        in_specs=[smem, anywhere, anywhere] + ([vmem, vmem] if linked else [anywhere, anywhere, vmem]),
        out_specs=(anywhere,) * 2 + ((vmem,) * 2 if linked else (anywhere, anywhere, vmem)),
        scratch_shapes=scratch,
        compiler_params=pltpu.CompilerParams(
            vmem_limit_bytes=64 * 1024 * 1024 - 65536,
            has_side_effects=True,
            **(dict(collective_id=0) if linked else {}),
        ),
    )(*args)


def copy_results(*arrays):
    n = len(arrays)

    def body(*refs):
        src, dst, held, sems = refs[:n], refs[n : 2 * n], refs[2 * n : 3 * n], refs[3 * n]
        takes = [pltpu.make_async_copy(src[i], held[i], sems.at[i]) for i in range(n)]
        gives = [pltpu.make_async_copy(held[i], dst[i], sems.at[n + i]) for i in range(n)]
        for copy in takes:
            copy.start()
        for take, give in zip(takes, gives):
            take.wait()
            give.start()
        for copy in gives:
            copy.wait()

    anywhere = pl.BlockSpec(memory_space=pl.ANY)
    return pl.pallas_call(
        body,
        out_shape=tuple(jax.ShapeDtypeStruct(a.shape, a.dtype) for a in arrays),
        in_specs=[anywhere] * n,
        out_specs=(anywhere,) * n,
        scratch_shapes=[pltpu.VMEM(a.shape, a.dtype) for a in arrays] + [pltpu.SemaphoreType.DMA((2 * n,))],
    )(*arrays)


def qkv_chunk(flat):
    return flat.reshape(-1, 32, 3, 6, 128).transpose(0, 3, 2, 1, 4).reshape(-1, ATT_ROWS, 128)


def qkv_flat(chunk):
    return chunk.reshape(-1, 6, 3, 32, 128).transpose(0, 3, 2, 1, 4).reshape(-1)


def tiled_chunk(flat, rows, tiles):
    return flat.reshape(-1, rows, tiles, 128).transpose(0, 2, 1, 3).reshape(-1, rows * tiles, 128)


def tiled_flat(chunk, rows, tiles):
    return chunk.reshape(-1, tiles, rows, 128).transpose(0, 2, 1, 3).reshape(-1)


def pack_vectors(attn_vec, ffn_vec):
    return jnp.concatenate(
        [
            attn_vec.reshape(30, 128),
            jnp.zeros((2, 128), attn_vec.dtype),
            ffn_vec.reshape(42, 128),
            jnp.zeros((6, 128), attn_vec.dtype),
        ]
    )


def shards_linked(frames, lengths, attn_params, ffn_params, cotangent):
    out, gin, attn_grad, ffn_grad = copy_results(
        *run_layer(True, lengths, frames[0], cotangent[0], attn_params, ffn_params)
    )
    return out[None], gin[None], attn_grad, ffn_grad


def in_places(chunks):
    g = chunks.reshape(4, 2, 2, 2, -1, 128)
    p0 = g[:, :, :, 0].transpose(0, 2, 1, 3, 4).reshape(4, 4, -1, 128)
    p1 = g[:, :, :, 1].reshape(4, 4, -1, 128)
    return jnp.stack([p0, p1], axis=1)


def from_places(g):
    p0 = g[:, 0].reshape(4, 2, 2, -1, 128).transpose(0, 2, 1, 3, 4)
    p1 = g[:, 1].reshape(4, 2, 2, -1, 128)
    return jnp.stack([p0, p1], axis=3).reshape(32, -1, 128)


def shards_any(frames, lengths, attn_params, ffn_params, cotangent):
    devices = lax.axis_size(AXES)
    attn_flat = lax.all_gather(attn_params, AXES, axis=0, tiled=True)
    ffn_flat = lax.all_gather(ffn_params, AXES, axis=0, tiled=True)
    cut_a, cut_f = 3 * D * D, D * FF
    attn_in = in_places(
        jnp.concatenate([qkv_chunk(attn_flat[:cut_a]), tiled_chunk(attn_flat[cut_a:ATT_MAT], 96, 6)])
    )
    ffn_in = in_places(
        jnp.concatenate([tiled_chunk(ffn_flat[:cut_f], 48, 24), tiled_chunk(ffn_flat[cut_f:FFN_MAT], 192, 6)])
    )
    vec_in = pack_vectors(attn_flat[ATT_MAT : ATT_MAT + ATT_VEC], ffn_flat[FFN_MAT : FFN_MAT + FFN_VEC])
    outs, gins, sums = [], [], None
    for u in range(frames.shape[0]):
        out, gin, attn_g, ffn_g, vg = run_layer(False, lengths[u : u + 1], frames[u], cotangent[u], attn_in, ffn_in, vec_in)
        outs.append(out)
        gins.append(gin)
        grads = [g.astype(f32) for g in (attn_g, ffn_g, vg)]
        sums = grads if sums is None else [s + g for s, g in zip(sums, grads)]
    attn_c, ffn_c = from_places(sums[0]), from_places(sums[1])
    pad_a = attn_params.shape[0] * devices - ATT_MAT - ATT_VEC
    pad_f = ffn_params.shape[0] * devices - FFN_MAT - FFN_VEC
    attn_terms = jnp.concatenate(
        [qkv_flat(attn_c[:24]), tiled_flat(attn_c[24:], 96, 6), sums[2][:30].reshape(-1), jnp.zeros((pad_a,), f32)]
    )
    ffn_terms = jnp.concatenate(
        [
            tiled_flat(ffn_c[:16], 48, 24),
            tiled_flat(ffn_c[16:], 192, 6),
            sums[2][32:74].reshape(-1),
            jnp.zeros((pad_f,), f32),
        ]
    )
    attn_grad = lax.psum_scatter(attn_terms, AXES, scatter_dimension=0, tiled=True)
    ffn_grad = lax.psum_scatter(ffn_terms, AXES, scatter_dimension=0, tiled=True)
    return jnp.stack(outs), jnp.stack(gins), attn_grad, ffn_grad


def solution(mesh):
    linked = tuple(mesh.shape[a] for a in AXES) == (8, 4)
    return jax.shard_map(
        shards_linked if linked else shards_any,
        mesh=mesh,
        in_specs=(P(AXES, None, None), P(AXES), P(AXES), P(AXES), P(AXES, None, None)),
        out_specs=(P(AXES, None, None), P(AXES, None, None), P(AXES), P(AXES)),
        check_vma=False,
    )
```

```python
from functools import partial

import jax
import jax.numpy as jnp
from jax import lax
from jax.experimental import pallas as pl
from jax.experimental.pallas import tpu as pltpu
from jax.sharding import PartitionSpec as P

D = 768
H = 12
FF = 3072
R = 768
PAIRS = 6
ATT_MAT = 4 * D * D
FFN_MAT = 2 * D * FF
ATT_VEC = 5 * D
FFN_VEC = FF + 3 * D
ATT_ROWS = 576
FFN_ROWS = 1152
VEC_ROWS = 80
AXES = ("dp", "fsdp")
bf16 = jnp.bfloat16
f32 = jnp.float32
MESH = pl.DeviceIdType.MESH

B_Q, B_V, B_OUT, G1, B1 = 0, 6, 12, 18, 24
B_IN, B_FC, G2, B2 = 32, 56, 62, 68


def nn(a, b):
    return jnp.dot(a, b, preferred_element_type=f32)


def nt(a, b):
    return lax.dot_general(a, b, (((1,), (1,)), ((), ())), preferred_element_type=f32)


def tn(a, b):
    return lax.dot_general(a, b, (((0,), (0,)), ((), ())), preferred_element_type=f32)


def split3(v):
    hi = v.astype(bf16)
    rest = v - hi.astype(f32)
    mid = rest.astype(bf16)
    return hi, mid, (rest - mid.astype(f32)).astype(bf16)


def place(chunk):
    z, x, y, c = chunk // 8, chunk // 4 % 2, chunk // 2 % 2, chunk % 2
    return z, c, (y * 2 + x if c == 0 else x * 2 + y)


def block(ref, chunk, rows):
    z, c, i = place(chunk)
    return ref[z, c, i, rows, :]


def aligned(start, size):
    return pl.ds(pl.multiple_of(start, size), size)


def w_qkv_pair(attn, i):
    blocks = [block(attn, d, aligned(i * 96, 96)) for d in range(24)]
    return jnp.concatenate(
        [jnp.concatenate([b[32 * p : 32 * p + 32] for b in blocks], axis=0) for p in range(3)], axis=1
    )


def put_w_qkv_pair(attn, i, value):
    for d in range(24):
        z, c, s = place(d)
        for p in range(3):
            attn[z, c, s, pl.ds(pl.multiple_of(i * 96 + 32 * p, 32), 32), :] = value[
                32 * d : 32 * d + 32, 128 * p : 128 * p + 128
            ]


def w_qkv_rows(attn, chunks, part):
    return jnp.concatenate(
        [
            jnp.concatenate(
                [block(attn, d, slice(96 * i + 32 * part, 96 * i + 32 * part + 32)) for i in range(PAIRS)], axis=1
            )
            for d in chunks
        ],
        axis=0,
    )


def w_out_cols(attn, j):
    blocks = [block(attn, d, slice(192 * j, 192 * j + 192)) for d in range(24, 32)]
    return jnp.concatenate(
        [jnp.concatenate([b[96 * p : 96 * p + 96] for b in blocks], axis=0) for p in range(2)], axis=1
    )


def w_out_rows(attn, chunks):
    return jnp.concatenate(
        [
            jnp.concatenate([block(attn, d, slice(96 * j, 96 * j + 96)) for j in range(6)], axis=1)
            for d in chunks
        ],
        axis=0,
    )


def w_in_cols(ffn, j, tiles):
    blocks = [block(ffn, d, aligned(j * 48 * tiles, 48 * tiles)) for d in range(16)]
    return jnp.concatenate(
        [jnp.concatenate([b[48 * p : 48 * p + 48] for b in blocks], axis=0) for p in range(tiles)], axis=1
    )


def put_w_in_cols(ffn, j, tiles, value):
    for d in range(16):
        z, c, s = place(d)
        for p in range(tiles):
            ffn[z, c, s, pl.ds(pl.multiple_of(j * 48 * tiles + 48 * p, 48), 48), :] = value[
                48 * d : 48 * d + 48, 128 * p : 128 * p + 128
            ]


def w_fc_cols(ffn, j):
    blocks = [block(ffn, d, aligned(j * 384, 384)) for d in range(16, 32)]
    return jnp.concatenate(
        [jnp.concatenate([b[192 * p : 192 * p + 192] for b in blocks], axis=0) for p in range(2)], axis=1
    )


def chip_slot(m):
    z, x, y = 2 + m // 4, m // 2 % 2, m % 2
    return z, (y * 2 + x, x * 2 + y)


def w_fc_rows(ffn, m):
    z, at = chip_slot(m)
    return jnp.concatenate(
        [
            jnp.concatenate([ffn[z, c, at[c], 192 * j : 192 * j + 192, :] for j in range(6)], axis=1)
            for c in range(2)
        ],
        axis=0,
    )


def put_w_fc_rows(ffn, m, value, tiles=range(6), base=0):
    z, at = chip_slot(m)
    z = z - base
    for c in range(2):
        for n, j in enumerate(tiles):
            ffn[z, c, at[c], 192 * j : 192 * j + 192, :] = value[192 * c : 192 * c + 192, 128 * n : 128 * n + 128]


def wide(vec, row, n=6):
    return jnp.concatenate([vec[row + j : row + j + 1, :] for j in range(n)], axis=1)


def put_wide(vec, row, value):
    for j in range(value.shape[1] // 128):
        vec[row + j : row + j + 1, :] = value[:, 128 * j : 128 * j + 128]


def lane_ids():
    return lax.broadcasted_iota(jnp.int32, (R, 128), 1)


def attend_pair(qp, kp, vp, dead, lane):
    one, zero = jnp.ones((), bf16), jnp.zeros((), bf16)
    v_one = jnp.concatenate([vp, jnp.ones((R, 128), bf16)], axis=1)
    outs, augmented = [], []
    for h in range(2):
        own = (lane < 64) if h == 0 else (lane >= 64)
        e = 64 if h == 0 else 0
        qh = jnp.where(own, qp, jnp.where(lane == e, one, zero))
        kh = jnp.where(own, kp, jnp.where(lane == e, dead, zero))
        mixed, lses = [], []
        for b in range(3):
            rows = slice(256 * b, 256 * b + 256)
            s = nt(qh[rows], kh)
            top = jnp.max(s, axis=-1, keepdims=True)
            p = jnp.exp(s - top).astype(bf16)
            both = nn(p, v_one)
            total = both[:, 128:]
            mixed.append(both[:, :128] / total)
            lses.append(top + jnp.log(total))
        outs.append(jnp.concatenate(mixed, axis=0))
        hi, mid, low = split3(jnp.concatenate(lses, axis=0))
        for k, part in enumerate((hi, mid, low)):
            qh = jnp.where(lane == e + 1 + k, part, qh)
        augmented.append(qh)
    return jnp.where(lane < 64, outs[0], outs[1]), augmented


def attend_pair_back(q_aug, kp, vp, dop, mixed, dead, lane):
    zero, minus = jnp.zeros((), bf16), -jnp.ones((), bf16)
    weighted = dop.astype(f32) * mixed.astype(f32)
    k_t = kp.T
    dks, dvs, dqs = [], [], []
    for h in range(2):
        own = (lane < 64) if h == 0 else (lane >= 64)
        e = 64 if h == 0 else 0
        dot = jnp.sum(jnp.where(own, weighted, 0.0), axis=-1, keepdims=True)
        do_aug = jnp.where(own, dop, zero)
        for k, part in enumerate(split3(dot)):
            do_aug = jnp.where(lane == e + k, part, do_aug)
        v_aug = jnp.where(own, vp, jnp.where((lane >= e) & (lane < e + 3), minus, zero))
        k_aug = jnp.where(own, kp, jnp.where((lane > e) & (lane < e + 4), minus, jnp.where(lane == e, dead, zero)))
        p = jnp.exp(nt(k_aug, q_aug[h]))
        ds = (p * nt(v_aug, do_aug)).astype(bf16)
        dvs.append(nn(p.astype(bf16), dop))
        dks.append(nn(ds, q_aug[h]))
        dqs.append(nn(k_t, ds))
    row = lax.broadcasted_iota(jnp.int32, (128, R), 0)
    dq = (jnp.where(row < 64, dqs[0], dqs[1]) * 0.125).astype(bf16).T
    dk = jnp.where(lane < 64, dks[0], dks[1]).astype(bf16)
    dv = jnp.where(lane < 64, dvs[0], dvs[1]).astype(bf16)
    return dq, dk, dv


def norm_back(g, xhat, gain, rstd):
    gg = g * gain
    m1 = jnp.mean(gg, axis=-1, keepdims=True)
    m2 = jnp.mean(gg * xhat, axis=-1, keepdims=True)
    return rstd * (gg - m1 - xhat * m2)


def column_sum(v):
    return jnp.sum(v.astype(f32), axis=0, keepdims=True)


ROWS = 128
BLOCKS = R // ROWS


def layer_kernel(gather, scatter, refs):
    length = refs["length"][0]
    x, io = refs["x"], refs["io"]

    def cot_copy(b):
        slot = lax.rem(b, 2)
        return pltpu.make_async_copy(refs["cot"].at[aligned(b * ROWS, ROWS)], refs["cot_b"].at[slot], io.at[6 + slot])

    def out_copy(b):
        slot = lax.rem(b, 2)
        return pltpu.make_async_copy(refs["out_b"].at[slot], refs["out"].at[aligned(b * ROWS, ROWS)], io.at[8 + slot])

    x_copy = pltpu.make_async_copy(refs["x_in"], x, io.at[0])
    x_copy.start()
    cot_copy(0).start()
    attn, ffn, vec, vg = refs["attn"], refs["ffn"], refs["vec"], refs["vg"]
    qx, kk, vv = refs["qx"], refs["k"], refs["v"]
    xh1, rs1, n1 = refs["xh1"], refs["rs1"], refs["n1"]
    act, gp, r2, gf = refs["act"], refs["gp"], refs["r2"], refs["gf"]
    do, mix = n1, refs["mix"]

    def dead_keys():
        row = lax.broadcasted_iota(jnp.int32, (R, 128), 0)
        return jnp.where(row < length, 0.0, -1e30).astype(bf16)

    gather.start()
    x_copy.wait()

    def forward_pair(i, carry):
        gather.before_pair(i)
        lane = lane_ids()
        cols = aligned(i * 128, 128)
        bias = jnp.concatenate(
            [vec[pl.ds(B_Q + i, 1), :], jnp.zeros((1, 128), f32), vec[pl.ds(B_V + i, 1), :]], axis=1
        )
        qkv = (nn(x[...], w_qkv_pair(attn, i)) + bias).astype(bf16)
        qp, kp, vp = qkv[:, :128] * jnp.asarray(0.125, bf16), qkv[:, 128:256], qkv[:, 256:]
        kk[:, cols] = kp
        vv[:, cols] = vp
        mixed, augmented = attend_pair(qp, kp, vp, dead_keys(), lane)
        mix[:, cols] = mixed.astype(bf16)
        for h in range(2):
            qx[:, pl.ds(pl.multiple_of(i * 256 + 128 * h, 128), 128)] = augmented[h]
        return carry

    lax.fori_loop(0, PAIRS, forward_pair, 0)
    gather.step(0)
    for j in range(3):
        cols = slice(256 * j, 256 * j + 256)
        xh1[:, cols] = nn(mix[...], w_out_cols(attn, j)) + wide(vec, B_OUT + 2 * j, 2) + x[:, cols].astype(f32)

    def norm1(b, carry):
        rows = aligned(b * ROWS, ROWS)
        r = xh1[rows, :]
        cen = r - jnp.mean(r, axis=-1, keepdims=True)
        rstd = lax.rsqrt(jnp.mean(cen * cen, axis=-1, keepdims=True) + 1e-05)
        xhat = cen * rstd
        xh1[rows, :] = xhat
        rs1[rows, :] = jnp.broadcast_to(rstd, (ROWS, 128))
        n1[rows, :] = (xhat * wide(vec, G1) + wide(vec, B1)).astype(bf16)
        return carry

    gather.step(1)
    lax.fori_loop(0, BLOCKS, norm1, 0)

    def ffn_in(j, carry):
        gather.before_in(j)
        cols = aligned(j * 256, 256)
        bias = jnp.concatenate([vec[pl.ds(B_IN + 2 * j, 1), :], vec[pl.ds(B_IN + 2 * j + 1, 1), :]], axis=1)
        pre = nn(n1[...], w_in_cols(ffn, j, 2)) + bias
        cdf = 0.5 + 0.5 * lax.erf(pre * 0.7071067811865476)
        act[:, cols] = (pre * cdf).astype(bf16)
        gp[:, cols] = (cdf + pre * (jnp.exp(-0.5 * pre * pre) * 0.3989422804014327)).astype(bf16)
        return carry

    lax.fori_loop(0, 12, ffn_in, 0)

    def ffn_out(j, carry):
        gather.before_out(j)
        cols = aligned(j * 256, 256)
        row = lambda base: jnp.concatenate(
            [vec[pl.ds(base + 2 * j, 1), :], vec[pl.ds(base + 2 * j + 1, 1), :]], axis=1
        )
        n1_full = xh1[:, cols] * row(G1) + row(B1)
        r2[:, cols] = nn(act[...], w_fc_cols(ffn, j)) + row(B_FC) + n1_full
        return carry

    lax.fori_loop(0, 3, ffn_out, 0)
    gather.finish()

    def norm2(b, sums):
        rows = aligned(b * ROWS, ROWS)
        r = r2[rows, :]
        cen = r - jnp.mean(r, axis=-1, keepdims=True)
        rstd = lax.rsqrt(jnp.mean(cen * cen, axis=-1, keepdims=True) + 1e-05)
        xhat = cen * rstd
        pl.when(b + 1 < BLOCKS)(lambda: cot_copy(b + 1).start())
        cot_copy(b).wait()
        pl.when(b >= 2)(lambda: out_copy(b - 2).wait())
        row = lax.broadcasted_iota(jnp.int32, (ROWS, D), 0) + b * ROWS
        valid = jnp.where(row < length, 1.0, 0.0)
        slot = lax.rem(b, 2)
        refs["out_b"][slot] = ((xhat * wide(vec, G2) + wide(vec, B2)) * valid).astype(bf16)
        out_copy(b).start()
        g = refs["cot_b"][slot].astype(f32) * valid
        grad = norm_back(g, xhat, wide(vec, G2), rstd)
        r2[rows, :] = grad
        low = grad.astype(bf16)
        gf[rows, :] = low
        return sums[0] + column_sum(g * xhat), sums[1] + column_sum(g), sums[2] + column_sum(low)

    zeros = jnp.zeros((1, D), f32)
    d_g2, d_b2, d_bfc = lax.fori_loop(0, BLOCKS, norm2, (zeros, zeros, zeros))
    for b in (BLOCKS - 2, BLOCKS - 1):
        out_copy(b).wait()
    put_wide(vg, G2, d_g2)
    put_wide(vg, B2, d_b2)
    put_wide(vg, B_FC, d_bfc)

    def back_first(m, carry):
        scatter.in_first(m)
        grad = tn(act[:, aligned(m * 384, 384)], gf[:, 0:384]).astype(bf16)
        put_w_fc_rows(refs["fc_g"], m, grad, range(0, 3), 2)
        return carry

    lax.fori_loop(0, 4, back_first, 0)

    def back_hidden(m):
        scatter.in_fc(m)
        cols = aligned(m * 384, 384)
        grad_act = nt(gf[...], w_fc_rows(ffn, m))
        low = (grad_act * gp[:, cols].astype(f32)).astype(bf16)
        gp[:, cols] = low
        sums = column_sum(low)
        for j in range(3):
            vg[pl.ds(B_IN + 3 * m + j, 1), :] = sums[:, 128 * j : 128 * j + 128]
        return cols

    def back_near(m, carry):
        cols = back_hidden(m)
        put_w_fc_rows(ffn, m, tn(act[:, cols], gf[:, 384:768]).astype(bf16), range(3, 6))
        return carry

    def back_fc(m, carry):
        cols = back_hidden(m)
        put_w_fc_rows(ffn, m, tn(act[:, cols], gf[...]).astype(bf16))
        return carry

    lax.fori_loop(0, 4, back_near, 0)
    lax.fori_loop(4, 8, back_fc, 0)

    def back_in(j, carry):
        scatter.in_in(j)
        cols = aligned(j * 512, 512)
        g = gp[:, cols]
        r2[...] += nt(g, w_in_cols(ffn, j, 4))
        put_w_in_cols(ffn, j, 4, tn(n1[...], g).astype(bf16))
        return carry

    lax.fori_loop(0, 6, back_in, 0)
    scatter.between(0)

    def back_norm1(b, sums):
        rows = aligned(b * ROWS, ROWS)
        g, xhat = r2[rows, :], xh1[rows, :]
        grad = norm_back(g, xhat, wide(vec, G1), rs1[rows, 0:1])
        r2[rows, :] = grad
        low = grad.astype(bf16)
        gf[rows, :] = low
        return sums[0] + column_sum(g * xhat), sums[1] + column_sum(g), sums[2] + column_sum(low)

    d_g1, d_b1, d_bout = lax.fori_loop(0, BLOCKS, back_norm1, (zeros, zeros, zeros))
    put_wide(vg, G1, d_g1)
    put_wide(vg, B1, d_b1)
    put_wide(vg, B_OUT, d_bout)
    scatter.between(1)

    for half in range(2):
        do[:, 384 * half : 384 * half + 384] = nt(
            gf[...], w_out_rows(attn, range(24 + 4 * half, 28 + 4 * half))
        ).astype(bf16)
    scatter.between(2)
    for half in range(2):
        cols = slice(384 * half, 384 * half + 384)
        grad = tn(mix[:, cols], gf[...]).astype(bf16)
        for d in range(4):
            z, c, s = place(24 + 4 * half + d)
            for j in range(6):
                attn[z, c, s, 96 * j : 96 * j + 96, :] = grad[96 * d : 96 * d + 96, 128 * j : 128 * j + 128]

    def backward_pair(i, carry):
        scatter.pair_start(i)
        lane = lane_ids()
        cols = aligned(i * 128, 128)
        q_aug = [qx[:, pl.ds(pl.multiple_of(i * 256 + 128 * h, 128), 128)] for h in range(2)]
        dq, dk, dv = attend_pair_back(
            q_aug, kk[:, cols], vv[:, cols], do[:, cols], mix[:, cols], dead_keys(), lane
        )
        do[:, cols] = dq
        kk[:, cols] = dk
        vv[:, cols] = dv
        scatter.pair_end(i)
        vg[pl.ds(B_Q + i, 1), :] = column_sum(dq)
        vg[pl.ds(B_V + i, 1), :] = column_sum(dv)
        put_w_qkv_pair(refs["qkv_g"], i, tn(x[...], jnp.concatenate([dq, dk, dv], axis=1)).astype(bf16))
        return carry

    lax.fori_loop(0, PAIRS, backward_pair, 0)
    gin_copies = []
    for n in range(3):
        scatter.tail(n)
        cols = slice(256 * n, 256 * n + 256)
        total = r2[:, cols]
        for p, g in enumerate((do, kk, vv)):
            total = total + nt(g[...], w_qkv_rows(attn, range(8 * n, 8 * n + 8), p))
        mix[:, cols] = total.astype(bf16)
        gin_copies.append(pltpu.make_async_copy(mix.at[:, cols], refs["gin"].at[:, cols], io.at[1 + n]))
        gin_copies[-1].start()
    scatter.tail(3)
    for copy in gin_copies:
        copy.wait()


class Loaded:
    def __init__(self, refs):
        self.refs = refs

    def start(self):
        r = self.refs
        copies = [
            pltpu.make_async_copy(r["attn_in"], r["attn"], r["io"].at[8]),
            pltpu.make_async_copy(r["ffn_in"], r["ffn"], r["io"].at[9]),
        ]
        for c in copies:
            c.start()
        r["vec"][...] = r["vec_in"][...].astype(f32)
        for c in copies:
            c.wait()

    def before_pair(self, i):
        pass

    before_in = before_out = step = before_pair

    def finish(self):
        pass


def position():
    dp, fs = lax.axis_index("dp"), lax.axis_index("fsdp")
    return lax.div(dp, 2), lax.rem(dp, 2), lax.div(fs, 2), lax.rem(fs, 2)


def device(z, x, y, c):
    return (z * 2 + x, y * 2 + c)


def remote(src, dst, send, recv, target):
    return pltpu.make_async_remote_copy(
        src_ref=src, dst_ref=dst, send_sem=send, recv_sem=recv, device_id=target, device_id_type=MESH
    )


ATT_GROUPS = (288, 288)
FFN_GROUPS = (192, 96, 192, 192, 192, 288)
PLANE_GROUPS = 2
Z, PASS, A, B, C, HOP = range(1, 7)
VECTOR_MARKS = (3003, 4003, 5003)
GATHER_ENDS = {
    0: (3020, 3030, 1000, 1010, 1040, 3000, 3040, 3050, 3060, 3010, 3070, 4020, 4030, 4000, 3001, 4040, 3011, 6020, 4010, 6030, 1050, 1060, 1070, 3002, 3003, 4001, 5000, 4011, 5040, 4002, 3012, 4003, 6021, 5010, 6031, 4012, 5001, 3013, 5011, 3041, 5002, 3051, 4050, 4013, 3061, 3042, 5003,),
    2: (4041, 3043, 3052, 4042, 4051, 3071, 5012, 5050,),
    4: (4060, 3062, 5013,),
    6: (5041, 4043, 6022, 4052,),
    8: (5042, 5051, 4061, 6032, 4070, 3072, 5060,),
    10: (5043, 5052, 3053, 3063, 4062,),
    12: (5061, 4071, 3073,),
    13: (5070, 5062, 4053, 4063, 4072,),
    14: (6023, 5071, 4073,),
    15: (5053, 6033, 5063,),
    17: (5072,),
    18: (5073,),
}
GATHER_MIDDLE = {
    0: (3020, 3030, 1000, 1010, 3000, 3040, 3050, 3060, 3010, 3070, 4020, 4030, 4000, 4040, 3002, 2003, 3003, 6020, 3001, 4010, 6030, 3012, 4002, 2013, 1040, 1050, 1060, 1070, 5000, 4003, 3011, 3013, 5040, 4001, 2043, 3043, 3041, 4012, 5010, 4011, 6022, 4013, 6021, 5002, 6032, 3042, 6031, 5003, 5001, 2053, 3053, 3051, 3052,),
    2: (4041, 5012,),
    4: (2063, 4050, 3061, 4042, 4051, 3062, 3063, 5011, 5013,),
    6: (2073, 5041, 4060, 3071, 3072, 3073,),
    8: (5050, 5042, 4043, 4052,),
    10: (5051, 4061,),
    12: (6023, 5060, 4070, 5043, 4053,),
    13: (6033, 5052, 5061, 4062, 4071,),
    14: (5070, 5053, 4063, 4072,),
    15: (5062, 4073,),
    16: (5071,),
    17: (5063,),
    19: (5072, 5073,),
}
SCATTER = {
    0: (100, 101,),
    2: (200, 201,),
    4: (102, 103,),
    5: (202,),
    6: (300, 203,),
    7: (301,),
    8: (302, 104, 105, 106, 107,),
    9: (400, 204, 205, 206, 108,),
    10: (401, 402, 303, 207, 208, 109,),
    11: (304, 209, 110,),
    12: (403, 210, 305, 111, 500,),
    13: (211, 404, 112,),
    14: (306, 212, 113,),
    15: (501, 405, 307, 213, 406,),
    16: (502, 308,),
    17: (114,),
    19: (503, 309, 407, 214, 408,),
    20: (310, 504, 115,),
    22: (409, 311, 215,),
    23: (116, 505,),
    25: (410, 411, 312, 216,),
    26: (506, 313, 117,),
    28: (508, 509, 412, 217,),
    29: (507, 118,),
    31: (314, 413, 315, 510, 218,),
    32: (316, 119,),
    34: (414, 511, 317, 219,),
    35: (415, 318, 120,),
    36: (416, 220,),
    37: (512, 417,),
    38: (418, 319, 513, 320, 419, 515, 420, 514, 516, 517, 518, 519, 520,),
}

ATT, FFN = 0, 1


def group_of(g):
    if g < len(ATT_GROUPS):
        return ATT, pl.ds(sum(ATT_GROUPS[:g]), ATT_GROUPS[g])
    g -= len(ATT_GROUPS)
    return FFN, pl.ds(sum(FFN_GROUPS[:g]), FFN_GROUPS[g])


ATT_HEAD, FFN_HEAD = 30, 42

N_GROUPS = len(ATT_GROUPS) + len(FFN_GROUPS)
PLANE_ROWS = sum(FFN_GROUPS[:PLANE_GROUPS])


def is_plane_group(g):
    return len(ATT_GROUPS) <= g < len(ATT_GROUPS) + PLANE_GROUPS


class Gather:
    def __init__(self, refs):
        self.refs = refs
        self.z, self.x, self.y, self.c = z, x, y, c = position()
        self.me = z * 8 + x * 4 + y * 2 + c
        first = c == 0
        a, b = jnp.where(first, x, y), jnp.where(first, y, x)
        self.slot, self.pair = b * 2 + a, b * 2
        self.other_slot, self.other_pair = b * 2 + 1 - a, (1 - b) * 2
        self.dev_a = device(z, jnp.where(first, 1 - x, x), jnp.where(first, y, 1 - y), c)
        self.dev_b = device(z, jnp.where(first, x, 1 - x), jnp.where(first, 1 - y, y), c)
        self.dev_c = device(z, x, y, 1 - c)
        self.zs = [lax.rem(z + k, 4) for k in (1, 2, 3)]
        self.dev_z = [device(t, x, y, c) for t in self.zs]
        upper = lax.div(z, 2)
        self.near = [z, z + 1 - 2 * lax.rem(z, 2), 2 - upper, 3 - 3 * upper]
        self.dev_near = [device(t, x, y, c) for t in self.near]
        self.is_end = (z == 0) | (z == 3)
        self.is_middle = (z == 1) | (z == 2)
        self.from_me = 2 + jnp.where(self.is_end, 1, 0)
        self.half = upper * 2
        self.other_half = 2 - upper * 2
        last = lax.rem(self.me + 1, 32)
        before = lax.rem(self.me + 31, 32)
        self.dev_after = (lax.div(last, 4), lax.rem(last, 4))
        self.dev_before = (lax.div(before, 4), lax.rem(before, 4))
        self.buf = (refs["attn"], refs["ffn"])

    def barrier(self, own_work):
        bar = pltpu.get_barrier_semaphore()
        targets = [self.dev_a, self.dev_b, self.dev_c, self.dev_after, self.dev_before] + self.dev_z
        for t in targets:
            pl.semaphore_signal(bar, inc=1, device_id=t, device_id_type=MESH)
        own_work()
        pl.semaphore_wait(bar, len(targets))

    def z_copy(self, g, k):
        kind, rows = group_of(g)
        ref = self.buf[kind].at[self.z, self.c, self.slot, rows]
        index = 1 if k == 1 else self.from_me
        r = self.refs
        return remote(ref, ref, r["gs"].at[8 + 3 * kind + k - 1], r["zr"].at[g, index], self.dev_near[k])

    def pass_copy(self, g):
        kind, rows = group_of(g)
        ref = self.buf[kind].at[self.near[3], self.c, self.slot, rows]
        return remote(ref, ref, self.refs["gs"].at[14 + kind], self.refs["zr"].at[g, 3], self.dev_near[1])

    def z_arrival(self, g, k):
        kind, rows = group_of(g)
        wide_ = pl.ds(0, 4) if is_plane_group(g) else self.slot
        ref = self.buf[kind].at[self.near[k], self.c, wide_, rows]
        return remote(ref, ref, self.refs["gs"].at[8], self.refs["zr"].at[g, k], self.dev_near[1])

    def hop_copy(self, g, k, n):
        _, rows = group_of(g)
        layer = self.near[max(n - 1, 0)]
        ref = self.refs["ffn"].at[layer, self.c, :, rows]
        target = self.dev_near[2 if n in (1, 2) else 1]
        index = (1, 2, 3, 2, 3)[n]
        return remote(ref, ref, self.refs["gs"].at[16 + n], self.refs["zr"].at[g, index], target)

    def plane_copy(self, step, g, k):
        kind, rows = group_of(g)
        r = self.refs
        at = self.buf[kind].at[self.near[k], self.c]
        later = 0 if kind == ATT else 1 if k == 0 else 2
        if step == A:
            src, send, recv, target = at.at[self.slot, rows], later, "ar", self.dev_a
        elif step == B:
            src, send, recv, target = at.at[pl.ds(self.pair, 2), rows], 3 + later, "br", self.dev_b
        else:
            src, send, recv, target = at.at[:, rows], 6 + kind, "cr", self.dev_c
        return remote(src, src, r["gs"].at[send], r[recv].at[g, k], target)

    def run(self, code):
        kind, g, k = code // 1000, code // 10 % 100, code % 10
        if kind == Z:
            self.z_copy(g, 1).start()
            self.z_copy(g, 2).start()
            pl.when(self.is_middle)(lambda: self.z_copy(g, 3).start())
            return
        if kind == PASS:
            self.z_arrival(g, 3).wait_recv()
            self.pass_copy(g).start()
            return
        if kind == HOP:
            if k == 0:
                self.plane_copy(B, g, 0).wait_recv()
                self.hop_copy(g, 0, 0).start()
                pl.when(self.is_middle)(lambda: self.hop_copy(g, 0, 1).start())
            else:
                self.z_arrival(g, k).wait_recv()
                pl.when(self.is_middle)(lambda: self.hop_copy(g, k, k + 1).start())
            self.plane_copy(C, g, k).start()
            return
        if kind == A and k in (1, 2):
            self.z_arrival(g, k).wait_recv()
        elif kind == A and k == 3:
            pl.when(self.is_end)(lambda: self.z_arrival(g, 3).wait_recv())
        elif kind == B:
            self.plane_copy(A, g, k).wait_recv()
        elif kind == C:
            self.plane_copy(B, g, k).wait_recv()
        self.plane_copy(kind, g, k).start()

    def ready(self, g, first, count):
        kind, rows = group_of(g)
        r = self.refs
        for n in range(count):
            ref = self.buf[kind].at[0, 1 - self.c, :, rows]
            remote(ref, ref, r["gs"].at[6 + kind], r["cr"].at[g, first + n], self.dev_c).wait_recv()

    def steps(self, key):
        for who, table in ((self.is_end, GATHER_ENDS), (self.is_middle, GATHER_MIDDLE)):
            if key in table:

                @pl.when(who)
                def _(table=table):
                    for s in table[key]:
                        self.run(s)

    def vectors(self, stage):
        r = self.refs
        buf, own, v = r["vec_all"], r["tail"], r["vsem"]
        one = buf.at[self.c, self.slot]
        if stage == 0:

            @pl.when(self.z == 3)
            def _():
                one[...] = own[...]
                for k in range(3):
                    remote(own, one, v.at[4 + k], v.at[1], self.dev_z[k]).start()

        elif stage == 1:

            @pl.when(self.z == 3)
            def _():
                for k in range(3):
                    remote(own, one, v.at[4 + k], v.at[1], self.dev_z[k]).wait_send()

            @pl.when(self.z != 3)
            def _():
                remote(one, one, v.at[4], v.at[1], self.dev_z[0]).wait_recv()

            remote(one, one, v.at[7], v.at[2], self.dev_a).start()
        elif stage == 2:
            got = buf.at[self.c, self.other_slot]
            remote(got, got, v.at[7], v.at[2], self.dev_a).wait()
            mine = buf.at[self.c, pl.ds(self.pair, 2)]
            remote(mine, mine, v.at[8], v.at[3], self.dev_b).start()
        elif stage == 3:
            got = buf.at[self.c, pl.ds(self.other_pair, 2)]
            remote(got, got, v.at[8], v.at[3], self.dev_b).wait()
            mine = buf.at[self.c]
            remote(mine, mine, v.at[9], v.at[10], self.dev_c).start()
        else:
            got = buf.at[1 - self.c]
            remote(got, got, v.at[9], v.at[10], self.dev_c).wait()
            r["vec"][...] = buf[1, 3].astype(f32)

    def tail_copy(self):
        t = self.refs["tail"]
        return remote(t, self.refs["tail_in"], self.refs["vsem"].at[11], self.refs["vsem"].at[12], self.dev_after)

    def load_own(self):
        r = self.refs
        flat_a, flat_f = r["flat_a"], r["flat_f"]
        own_a, own_f = r["attn_own"], r["ffn_own"]
        whole_a, whole_f = ATT_ROWS * 128, FFN_ROWS * 128
        flat_a[ATT_HEAD + ATT_ROWS : ATT_HEAD + ATT_ROWS + 16, :] = jnp.zeros((16, 128), f32)
        flat_f[FFN_HEAD + FFN_ROWS : FFN_HEAD + FFN_ROWS + 16, :] = jnp.zeros((16, 128), f32)
        flat_a[pl.ds(ATT_HEAD, ATT_ROWS), :] = own_a[0:whole_a].reshape(ATT_ROWS, 128).astype(f32)
        flat_f[pl.ds(FFN_HEAD, FFN_ROWS), :] = own_f[0:whole_f].reshape(FFN_ROWS, 128).astype(f32)
        at = ATT_HEAD + ATT_ROWS
        flat_a[at : at + 1, 0:120] = own_a[whole_a : whole_a + 120].reshape(1, 120).astype(f32)
        at = FFN_HEAD + FFN_ROWS
        flat_f[at : at + 1, :] = own_f[whole_f : whole_f + 128].reshape(1, 128).astype(f32)
        flat_f[at + 1 : at + 2, 0:40] = own_f[whole_f + 128 : whole_f + 168].reshape(1, 40).astype(f32)
        lane = lax.broadcasted_iota(jnp.int32, (32, 128), 1)
        v = pltpu.roll(flat_a[ATT_HEAD + 546 : ATT_HEAD + 586, :], 8, 1)
        r["tail"][0:32, :] = jnp.where(lane < 8, v[0:32], v[1:33]).astype(bf16)
        lane = lax.broadcasted_iota(jnp.int32, (48, 128), 1)
        v = pltpu.roll(flat_f[FFN_HEAD + 1111 : FFN_HEAD + 1167, :], 88, 1)
        r["tail"][32:80, :] = jnp.where(lane < 88, v[0:48], v[1:49]).astype(bf16)

    def place_own(self, kind):
        r = self.refs
        if kind == ATT:
            flat, rows, head, size, moved, at = r["flat_a"], r["attn_sum"], ATT_HEAD, ATT_ROWS, 120, 0
        else:
            flat, rows, head, size, moved, at = r["flat_f"], r["ffn_sum"], FFN_HEAD, FFN_ROWS, 168, 32
        flat[0:head, :] = r["tail_in"][at : at + head, :].astype(f32)
        shift = head * 128 - moved * self.me

        def step(n, carry):
            rows[pl.ds(pl.multiple_of(n * 64, 64), 64), :] = self.shifted(flat, shift, n)
            return carry

        lax.fori_loop(0, size // 64, step, 0)
        slot = self.buf[kind].at[self.z, self.c, self.slot]
        self.by_kind(kind, lambda tiles, n, at: self.to_tiles(rows, slot, tiles, n, at))

    def by_kind(self, kind, fn):
        if kind == ATT:
            pl.when(self.z < 3)(lambda: fn(18, 32, lambda t: (t % 6 * 3 + t // 6) * 32))
            pl.when(self.z == 3)(lambda: fn(6, 96, lambda t: t * 96))
        else:
            pl.when(self.z < 2)(lambda: fn(24, 48, lambda t: t * 48))
            pl.when(self.z >= 2)(lambda: fn(6, 192, lambda t: t * 192))

    def to_tiles(self, rows, slot, tiles, n, at):
        for t in range(tiles):
            slot[at(t) : at(t) + n, :] = rows[pl.ds(t, n, stride=tiles), :].astype(bf16)

    def from_tiles(self, total, flat, tiles, n, at):
        for t in range(tiles):
            flat[pl.ds(t, n, stride=tiles), :] = total[at(t) : at(t) + n, :]

    def shifted(self, src, shift, n):
        row, turn = lax.div(shift, 128), lax.rem(shift, 128)
        lane = lax.broadcasted_iota(jnp.int32, (64, 128), 1)
        back = lax.rem(128 - turn, 128)
        low = pltpu.roll(src[pl.ds(n * 64 + row, 64), :], back, 1)
        high = pltpu.roll(src[pl.ds(n * 64 + row + 1, 64), :], back, 1)
        return jnp.where(lane < 128 - turn, low, high)

    def start(self):
        self.barrier(self.load_own)
        pl.when(self.me < 31)(lambda: self.tail_copy().start())
        self.vectors(0)
        pl.when(self.me > 0)(lambda: self.tail_copy().wait_recv())
        self.place_own(ATT)
        for g in range(len(ATT_GROUPS)):
            self.run(1000 * Z + 10 * g)
        self.place_own(FFN)
        for who, table in ((self.is_end, GATHER_ENDS), (self.is_middle, GATHER_MIDDLE)):

            @pl.when(who)
            def _(table=table):
                first = [v for v in table[0] if v >= 1000 * Z + 10 * len(ATT_GROUPS)]
                cuts = [0] + [first.index(v) + 1 for v in VECTOR_MARKS] + [len(first)]
                for stage in range(4):
                    for s in first[cuts[stage] : cuts[stage + 1]]:
                        self.run(s)
                    self.vectors(stage + 1)

    def before_pair(self, i):
        for v in range(PAIRS):

            @pl.when(i == v)
            def _(v=v):
                if v:
                    self.steps(2 * v)
                if v * len(ATT_GROUPS) % PAIRS == 0:
                    self.ready(v * len(ATT_GROUPS) // PAIRS, 0, 4)

    def step(self, n):
        self.steps(12 + n)

    def before_in(self, j):
        at = 0
        for n, rows in enumerate(FFN_GROUPS):

            @pl.when(j == at // 96)
            def _(n=n):
                self.steps(14 + n)
                self.ready(len(ATT_GROUPS) + n, self.half, 2)

            at += rows

    def before_out(self, j):
        seen = 0
        for v in range(3):
            more, at = [], 0
            for n, rows in enumerate(FFN_GROUPS):
                if n >= seen and at < 384 * (v + 1):
                    more.append(n)
                at += rows
            seen += len(more)

            @pl.when(j == v)
            def _(v=v, more=more):
                self.steps(14 + len(FFN_GROUPS) + v)
                for n in more:
                    self.ready(len(ATT_GROUPS) + n, self.other_half, 2)

    def finish(self):
        self.steps(17 + len(FFN_GROUPS))
        r = self.refs
        z, c, gs = self.z, self.c, r["gs"]
        attn, ffn = self.buf
        rest = pl.ds(PLANE_ROWS, FFN_ROWS - PLANE_ROWS)
        front = pl.ds(0, PLANE_ROWS)

        def sent(n, ref):
            remote(ref, ref, gs.at[n], r["zr"].at[0, 0], self.dev_c).wait_send()

        sent(0, attn.at[:, c, self.slot])
        sent(1, ffn.at[z, c, self.slot])
        sent(2, ffn.at[pl.ds(0, 3), c, self.slot, rest])
        sent(3, attn.at[:, c, pl.ds(self.pair, 2)])
        sent(4, ffn.at[z, c, pl.ds(self.pair, 2)])
        sent(5, ffn.at[pl.ds(0, 3), c, pl.ds(self.pair, 2), rest])
        sent(6, attn.at[:, c])
        sent(7, ffn.at[:, c])
        for k in range(2):
            sent(8 + k, attn.at[z, c, self.slot])
            sent(11 + k, ffn.at[z, c, self.slot, rest])
        if PLANE_GROUPS:
            sent(16, ffn.at[z, c, :, front])

        @pl.when(self.is_middle)
        def _():
            sent(10, attn.at[z, c, self.slot])
            sent(13, ffn.at[z, c, self.slot, rest])
            sent(14, attn.at[z, c, self.slot])
            sent(15, ffn.at[z, c, self.slot, rest])
            if PLANE_GROUPS:
                for n in range(17, 21):
                    sent(n, ffn.at[z, c, :, front])

        pl.when(self.me < 31)(lambda: self.tail_copy().wait_send())


W_FC, W_IN, W_OUT, W_QKV = 0, 8, 14, 15
N_ITEMS = W_QKV + PAIRS


class Scatter:
    def __init__(self, refs, gather):
        self.refs, self.g = refs, gather

    def part(self, item):
        if item < 2:
            return "fc_g", "ffn", range(2, 3), pl.ds(288 * item, 288), 288, 0
        if item >= W_QKV:
            return "qkv_g", "attn", range(0, 3), pl.ds(96 * (item - W_QKV), 96), 96, 2
        if item == W_OUT:
            return "attn", "attn", range(3, 4), pl.ds(0, 576), 576, 1
        if item >= W_IN:
            return "ffn", "ffn", range(0, 2), pl.ds(192 * (item - W_IN), 192), 192, 0
        z = 2 + item // 4
        return "ffn", "ffn", range(z, z + 1), pl.ds(288 * (item % 4), 288), 288, 0

    def span(self, zz):
        return pl.ds(zz[0], len(zz))

    def at(self, buf, z):
        return z - 2 if buf == "fc_g" else z

    def add(self, pairs, rows, count):
        def step(n, carry):
            at = pl.ds(pl.multiple_of(rows.start + n * 96, 96), 96)
            for dst, src in pairs:
                d = dst.at[at]
                d[...] = d[...] + src.at[at][...]
            return carry

        if count == 96:
            step(0, 0)
        else:
            lax.fori_loop(0, count // 96, step, 0)

    def c_copy(self, g):
        buf, kind, zz, rows, _, s = self.part(g)
        r, t = self.refs, self.g
        return remote(
            r[buf].at[self.span([self.at(buf, z) for z in zz]), 1 - t.c, :, rows],
            r[kind + "_rc"].at[self.span(zz), :, rows],
            r["ss"].at[s, 0],
            r["sr"].at[0, g],
            t.dev_c,
        )

    def b_copy(self, g):
        buf, kind, zz, rows, _, s = self.part(g)
        r, t = self.refs, self.g
        return remote(
            r[buf].at[self.span([self.at(buf, z) for z in zz]), t.c, pl.ds(t.other_pair, 2), rows],
            r[kind + "_rb"].at[self.span(zz), :, rows],
            r["ss"].at[s, 1],
            r["sr"].at[1, g],
            t.dev_b,
        )

    def a_copy(self, g):
        buf, kind, zz, rows, _, s = self.part(g)
        r, t = self.refs, self.g
        return remote(
            r[buf].at[self.span([self.at(buf, z) for z in zz]), t.c, t.other_slot, rows],
            r[kind + "_ra"].at[self.span(zz), rows],
            r["ss"].at[s, 2],
            r["sr"].at[2, g],
            t.dev_a,
        )

    def z_copy(self, g, k):
        buf, kind, zz, rows, _, s = self.part(g)
        r, t = self.refs, self.g
        return remote(
            r[buf].at[self.at(buf, t.zs[k]), t.c, t.slot, rows],
            r[kind + "_rz"].at[k, rows],
            r["ss"].at[s, 3 + k],
            r["sr"].at[3, g],
            t.dev_z[k],
        )

    def inside(self, value, zz):
        return (value >= zz[0]) & (value <= zz[-1])

    def c_send(self, g):
        self.c_copy(g).start()

    def b_send(self, g):
        buf, kind, zz, rows, n, _ = self.part(g)
        r, t = self.refs, self.g
        self.c_copy(g).wait_recv()
        self.add([(r[buf].at[self.at(buf, z), t.c, i], r[kind + "_rc"].at[z, i]) for z in zz for i in range(4)], rows, n)
        self.b_copy(g).start()

    def a_send(self, g):
        buf, kind, zz, rows, n, _ = self.part(g)
        r, t = self.refs, self.g
        self.b_copy(g).wait_recv()
        self.add([(r[buf].at[self.at(buf, z), t.c, t.pair + i], r[kind + "_rb"].at[z, i]) for z in zz for i in range(2)], rows, n)
        self.a_copy(g).start()

    def z_send(self, g):
        buf, kind, zz, rows, n, _ = self.part(g)
        r, t = self.refs, self.g
        self.a_copy(g).wait_recv()
        self.add([(r[buf].at[self.at(buf, z), t.c, t.slot], r[kind + "_ra"].at[z]) for z in zz], rows, n)
        for k in range(3):

            @pl.when(self.inside(t.zs[k], zz))
            def _():
                self.z_copy(g, k).start()

    def take(self, g):
        buf, kind, zz, rows, n, _ = self.part(g)
        r, t = self.refs, self.g

        @pl.when(self.inside(t.z, zz))
        def _():
            got = r[kind + "_rz"].at[:, rows]
            remote(got, got, r["ss"].at[0, 3], r["sr"].at[3, g], t.dev_c).wait_recv()

            def step(i, carry):
                at = pl.ds(pl.multiple_of(rows.start + i * 96, 96), 96)
                total = r[buf][self.at(buf, t.z), t.c, t.slot, at, :].astype(f32)
                for k in range(3):
                    total = total + r[kind + "_rz"][k, at, :].astype(f32)
                r[kind + "_sum"][at, :] = total
                return carry

            lax.fori_loop(0, n // 96, step, 0)

    def vectors(self, stage):
        r, t = self.refs, self.g
        own, got, s, v = r["vg"], r["vg_r"], r["vs"], r["vr"]
        if stage > 0:
            target = (t.dev_c, t.dev_b, t.dev_a)[stage - 1]
            remote(own, got.at[stage - 1], s.at[stage - 1], v.at[stage - 1], target).wait()
            own[...] = own[...] + got[stage - 1]
        if stage < 3:
            target = (t.dev_c, t.dev_b, t.dev_a)[stage]
            remote(own, got.at[stage], s.at[stage], v.at[stage], target).start()
        else:
            for k in range(3):

                @pl.when(t.zs[k] == 3)
                def _():
                    remote(own, got.at[3 + k], s.at[3 + k], v.at[3 + k], t.dev_z[k]).start()

    def take_vectors(self):
        r, t = self.refs, self.g
        own, got, s, v = r["vg"], r["vg_r"], r["vs"], r["vr"]
        for k in range(3):

            @pl.when(t.zs[k] == 3)
            def _():
                remote(own, got.at[3 + k], s.at[3 + k], v.at[3 + k], t.dev_z[k]).wait_send()

        @pl.when(t.z == 3)
        def _():
            for k in range(3):
                remote(own, got.at[3 + k], s.at[3 + k], v.at[3 + k], t.dev_z[k]).wait_recv()
            own[...] = own[...] + got[3] + got[4] + got[5]

    def sent(self):
        r, t = self.refs, self.g
        ss = r["ss"]

        def one(s, n, ref):
            remote(ref, ref, ss.at[s, n], r["sr"].at[0, 0], t.dev_c).wait_send()

        for s, ref in enumerate((r["ffn"], r["attn"].at[pl.ds(3, 1)], r["qkv_g"])):
            one(s, 0, ref.at[:, 1 - t.c])
            one(s, 1, ref.at[:, t.c, pl.ds(t.other_pair, 2)])
            one(s, 2, ref.at[:, t.c, t.other_slot])
        for k in range(3):
            one(0, 3 + k, r["ffn"].at[0, t.c, t.slot])
            pl.when(t.zs[k] == 3)(lambda k=k: one(1, 3 + k, r["attn"].at[3, t.c, t.slot]))
            pl.when(t.zs[k] != 3)(lambda k=k: one(2, 3 + k, r["qkv_g"].at[0, t.c, t.slot]))

    def step(self, key):
        for s in SCATTER.get(key, ()):
            self.one(s)

    def one(self, s):
        kinds = (None, self.c_send, self.b_send, self.a_send, self.z_send, self.take)
        kinds[s // 100](s % 100)

    def loop(self, i, first, stride, count):
        for v in range(count):
            if first + stride * v in SCATTER:
                pl.when(i == v)(lambda v=v: self.step(first + stride * v))

    def in_first(self, m):
        self.loop(m, 40, 1, 4)

    def in_fc(self, m):
        self.loop(m, 0, 1, 8)

    def in_in(self, j):
        self.loop(j, 8, 1, 6)

    def between(self, n):
        self.step(14 + n)

    def pair_start(self, i):
        self.loop(i, 17, 3, PAIRS)

    def pair_end(self, i):
        self.loop(i, 19, 3, PAIRS)

    def tail(self, n):
        if n < 3:
            self.step(35 + n)
            self.vectors(n)
            return
        order = SCATTER[38]
        ffn_left = max(i for i, s in enumerate(order) if s // 100 == 5 and s % 100 < W_OUT) + 1
        relays_left = max(i for i, s in enumerate(order) if s // 100 < 5) + 1
        at = order.index(300 + N_ITEMS - 1) + 1
        for n, s in enumerate(order[:ffn_left]):
            self.one(s)
            if n + 1 == at:
                self.vectors(3)
        self.hand_over(FFN)
        for n, s in enumerate(order[ffn_left:relays_left]):
            self.one(s)
            if n + 1 + ffn_left == at:
                self.vectors(3)
        self.take_vectors()
        self.finish(FFN)
        for s in order[relays_left:]:
            self.one(s)
        self.hand_over(ATT)
        self.finish(ATT)
        self.sent()

    def head_copy(self, kind):
        r, t = self.refs, self.g
        count = (32, 48)[kind]
        head, got = r[("flat_a", "flat_f")[kind]].at[pl.ds(0, count)], r["head_in"].at[pl.ds(32 * kind, count)]
        return remote(head, got, r["hs"].at[2 * kind], r["hs"].at[2 * kind + 1], t.dev_before)

    def hand_over(self, kind):
        r, t = self.refs, self.g
        total, flat = r[("attn_sum", "ffn_sum")[kind]], r[("flat_a", "flat_f")[kind]]
        t.by_kind(kind, lambda tiles, n, at: t.from_tiles(total, flat, tiles, n, at))
        pl.when(t.me > 0)(self.head_copy(kind).start)

    def finish(self, kind):
        r, t = self.refs, self.g
        size, count, moved = ((ATT_ROWS, 32, 120), (FFN_ROWS, 48, 168))[kind]
        flat, out = r[("flat_a", "flat_f")[kind]], r[("attn_out", "ffn_out")[kind]]
        copy = self.head_copy(kind)
        pl.when(t.me < 31)(copy.wait_recv)
        mine = jnp.where(t.me == 31, r["vg"][32 * kind : 32 * kind + count, :], r["head_in"][32 * kind : 32 * kind + count, :])
        flat[size : size + count, :] = mine

        def step(n, carry):
            out[pl.ds(pl.multiple_of(n * 8192, 8192), 8192)] = t.shifted(flat, moved * t.me, n).reshape(8192)
            return carry

        lax.fori_loop(0, size // 64, step, 0)
        whole = size * 128
        rest = t.shifted(flat, moved * t.me, size // 64)
        if kind == ATT:
            out[whole : whole + 120] = rest[0:1, 0:120].reshape(120)
        else:
            out[whole : whole + 128] = rest[0:1, :].reshape(128)
            out[whole + 128 : whole + 168] = rest[1:2, 0:40].reshape(40)
        pl.when(t.me > 0)(copy.wait_send)


class Kept:
    def in_fc(self, m):
        pass

    in_first = in_in = between = pair_start = pair_end = tail = in_fc


SCRATCH = dict(
    x=((R, D), bf16),
    mix=((R, D), bf16),
    cot_b=((2, ROWS, D), bf16),
    out_b=((2, ROWS, D), bf16),
    attn=((4, 2, 4, ATT_ROWS, 128), bf16),
    ffn=((4, 2, 4, FFN_ROWS, 128), bf16),
    vec=((VEC_ROWS, 128), f32),
    qx=((R, 1536), bf16),
    k=((R, D), bf16),
    v=((R, D), bf16),
    xh1=((R, D), f32),
    rs1=((R, 128), f32),
    n1=((R, D), bf16),
    act=((R, FF), bf16),
    gp=((R, FF), bf16),
    r2=((R, D), f32),
    gf=((R, D), bf16),
    qkv_g=((3, 2, 4, ATT_ROWS, 128), bf16),
    fc_g=((1, 2, 4, FFN_ROWS // 2, 128), bf16),
)


def run_layer(linked, length, x, cot, attn_in, ffn_in, vec_in=None):
    dma = pltpu.SemaphoreType.DMA
    vmem, anywhere = pl.BlockSpec(memory_space=pltpu.VMEM), pl.BlockSpec(memory_space=pl.ANY)
    names = ["length", "x_in", "cot"] + (["attn_own", "ffn_own"] if linked else ["attn_in", "ffn_in", "vec_in"])
    names += ["out", "gin"] + (["attn_out", "ffn_out"] if linked else ["attn_g", "ffn_g", "vg"])
    more = dict(io=dma((10,)))
    if linked:
        more.update(
            vg=pltpu.VMEM((VEC_ROWS, 128), f32),
            vec_all=pltpu.VMEM((2, 4, VEC_ROWS, 128), bf16),
            tail=pltpu.VMEM((VEC_ROWS, 128), bf16),
            tail_in=pltpu.VMEM((VEC_ROWS, 128), bf16),
            head_in=pltpu.VMEM((VEC_ROWS, 128), f32),
            flat_a=pltpu.VMEM((704, 128), f32),
            flat_f=pltpu.VMEM((1280, 128), f32),
            gs=dma((21,)),
            zr=dma((N_GROUPS, 4)),
            ar=dma((N_GROUPS, 4)),
            br=dma((N_GROUPS, 4)),
            cr=dma((N_GROUPS, 4)),
            vsem=dma((13,)),
            ss=dma((3, 6)),
            sr=dma((4, N_ITEMS)),
            vs=dma((6,)),
            vr=dma((6,)),
            hs=dma((4,)),
            vg_r=pltpu.VMEM((6, VEC_ROWS, 128), f32),
        )
        for kind, rows in (("attn", ATT_ROWS), ("ffn", FFN_ROWS)):
            more[kind + "_rc"] = pltpu.VMEM((4, 4, rows, 128), bf16)
            more[kind + "_rb"] = pltpu.VMEM((4, 2, rows, 128), bf16)
            more[kind + "_ra"] = pltpu.VMEM((4, rows, 128), bf16)
            more[kind + "_rz"] = pltpu.VMEM((3, rows, 128), bf16)
            more[kind + "_sum"] = pltpu.VMEM((rows, 128), f32)
    names += list(SCRATCH) + list(more)
    scratch = [pltpu.VMEM(*s) for s in SCRATCH.values()] + list(more.values())

    def body(*args):
        refs = dict(zip(names, args, strict=True))
        refs["vg"][...] = jnp.zeros((VEC_ROWS, 128), f32)
        if linked:
            gather = Gather(refs)
            layer_kernel(gather, Scatter(refs, gather), refs)
            return
        layer_kernel(Loaded(refs), Kept(), refs)
        copies = [
            pltpu.make_async_copy(refs["qkv_g"], refs["attn_g"].at[0:3], refs["io"].at[0]),
            pltpu.make_async_copy(refs["attn"].at[3], refs["attn_g"].at[3], refs["io"].at[1]),
            pltpu.make_async_copy(refs["ffn"].at[0:2], refs["ffn_g"].at[0:2], refs["io"].at[2]),
            pltpu.make_async_copy(refs["fc_g"], refs["ffn_g"].at[2:3, :, :, 0:576], refs["io"].at[3]),
            pltpu.make_async_copy(refs["ffn"].at[2:3, :, :, 576:], refs["ffn_g"].at[2:3, :, :, 576:], refs["io"].at[4]),
            pltpu.make_async_copy(refs["ffn"].at[3], refs["ffn_g"].at[3], refs["io"].at[5]),
        ]
        for c in copies:
            c.start()
        for c in copies:
            c.wait()

    act_out = jax.ShapeDtypeStruct((R, D), bf16)
    if linked:
        grads = tuple(jax.ShapeDtypeStruct(a.shape, f32) for a in (attn_in, ffn_in))
    else:
        grads = tuple(jax.ShapeDtypeStruct(SCRATCH[k][0], bf16) for k in ("attn", "ffn"))
        grads += (jax.ShapeDtypeStruct((VEC_ROWS, 128), f32),)
    smem = pl.BlockSpec(memory_space=pltpu.SMEM)
    args = (length, x, cot, attn_in, ffn_in) + (() if linked else (vec_in,))
    return pl.pallas_call(
        body,
        out_shape=(act_out, act_out) + grads,
        in_specs=[smem, anywhere, anywhere] + ([vmem, vmem] if linked else [anywhere, anywhere, vmem]),
        out_specs=(anywhere,) * 2 + ((vmem,) * 2 if linked else (anywhere, anywhere, vmem)),
        scratch_shapes=scratch,
        compiler_params=pltpu.CompilerParams(
            vmem_limit_bytes=64 * 1024 * 1024 - 65536,
            has_side_effects=True,
            **(dict(collective_id=0) if linked else {}),
        ),
    )(*args)


def copy_results(*arrays):
    n = len(arrays)
    parts = [(i, p) for p in range(3) for i in range(n) if arrays[i].ndim == 2] + [
        (i, None) for i in range(n) if arrays[i].ndim == 1
    ]

    def body(*refs):
        src, dst, held, sems = refs[:n], refs[n : 2 * n], refs[2 * n : 3 * n], refs[3 * n]

        def view(ref, p):
            return ref if p is None else ref.at[pl.ds(256 * p, 256)]

        takes = [
            pltpu.make_async_copy(view(src[i], p), view(held[i], p), sems.at[0, j]) for j, (i, p) in enumerate(parts)
        ]
        gives = [
            pltpu.make_async_copy(view(held[i], p), view(dst[i], p), sems.at[1, j]) for j, (i, p) in enumerate(parts)
        ]
        for copy in takes:
            copy.start()
        for take, give in zip(takes, gives):
            take.wait()
            give.start()
        for copy in gives:
            copy.wait()

    anywhere = pl.BlockSpec(memory_space=pl.ANY)
    return pl.pallas_call(
        body,
        out_shape=tuple(jax.ShapeDtypeStruct(a.shape, a.dtype) for a in arrays),
        in_specs=[anywhere] * n,
        out_specs=(anywhere,) * n,
        scratch_shapes=[pltpu.VMEM(a.shape, a.dtype) for a in arrays] + [pltpu.SemaphoreType.DMA((2, len(parts)))],
    )(*arrays)


def qkv_chunk(flat):
    return flat.reshape(-1, 32, 3, 6, 128).transpose(0, 3, 2, 1, 4).reshape(-1, ATT_ROWS, 128)


def qkv_flat(chunk):
    return chunk.reshape(-1, 6, 3, 32, 128).transpose(0, 3, 2, 1, 4).reshape(-1)


def tiled_chunk(flat, rows, tiles):
    return flat.reshape(-1, rows, tiles, 128).transpose(0, 2, 1, 3).reshape(-1, rows * tiles, 128)


def tiled_flat(chunk, rows, tiles):
    return chunk.reshape(-1, tiles, rows, 128).transpose(0, 2, 1, 3).reshape(-1)


def pack_vectors(attn_vec, ffn_vec):
    return jnp.concatenate(
        [
            attn_vec.reshape(30, 128),
            jnp.zeros((2, 128), attn_vec.dtype),
            ffn_vec.reshape(42, 128),
            jnp.zeros((6, 128), attn_vec.dtype),
        ]
    )


def shards_linked(frames, lengths, attn_params, ffn_params, cotangent):
    out, gin, attn_grad, ffn_grad = copy_results(
        *run_layer(True, lengths, frames[0], cotangent[0], attn_params, ffn_params)
    )
    return out[None], gin[None], attn_grad, ffn_grad


def in_places(chunks):
    g = chunks.reshape(4, 2, 2, 2, -1, 128)
    p0 = g[:, :, :, 0].transpose(0, 2, 1, 3, 4).reshape(4, 4, -1, 128)
    p1 = g[:, :, :, 1].reshape(4, 4, -1, 128)
    return jnp.stack([p0, p1], axis=1)


def from_places(g):
    p0 = g[:, 0].reshape(4, 2, 2, -1, 128).transpose(0, 2, 1, 3, 4)
    p1 = g[:, 1].reshape(4, 2, 2, -1, 128)
    return jnp.stack([p0, p1], axis=3).reshape(32, -1, 128)


def shards_any(frames, lengths, attn_params, ffn_params, cotangent):
    devices = lax.axis_size(AXES)
    attn_flat = lax.all_gather(attn_params, AXES, axis=0, tiled=True)
    ffn_flat = lax.all_gather(ffn_params, AXES, axis=0, tiled=True)
    cut_a, cut_f = 3 * D * D, D * FF
    attn_in = in_places(
        jnp.concatenate([qkv_chunk(attn_flat[:cut_a]), tiled_chunk(attn_flat[cut_a:ATT_MAT], 96, 6)])
    )
    ffn_in = in_places(
        jnp.concatenate([tiled_chunk(ffn_flat[:cut_f], 48, 24), tiled_chunk(ffn_flat[cut_f:FFN_MAT], 192, 6)])
    )
    vec_in = pack_vectors(attn_flat[ATT_MAT : ATT_MAT + ATT_VEC], ffn_flat[FFN_MAT : FFN_MAT + FFN_VEC])
    outs, gins, sums = [], [], None
    for u in range(frames.shape[0]):
        out, gin, attn_g, ffn_g, vg = run_layer(False, lengths[u : u + 1], frames[u], cotangent[u], attn_in, ffn_in, vec_in)
        outs.append(out)
        gins.append(gin)
        grads = [g.astype(f32) for g in (attn_g, ffn_g, vg)]
        sums = grads if sums is None else [s + g for s, g in zip(sums, grads)]
    attn_c, ffn_c = from_places(sums[0]), from_places(sums[1])
    pad_a = attn_params.shape[0] * devices - ATT_MAT - ATT_VEC
    pad_f = ffn_params.shape[0] * devices - FFN_MAT - FFN_VEC
    attn_terms = jnp.concatenate(
        [qkv_flat(attn_c[:24]), tiled_flat(attn_c[24:], 96, 6), sums[2][:30].reshape(-1), jnp.zeros((pad_a,), f32)]
    )
    ffn_terms = jnp.concatenate(
        [
            tiled_flat(ffn_c[:16], 48, 24),
            tiled_flat(ffn_c[16:], 192, 6),
            sums[2][32:74].reshape(-1),
            jnp.zeros((pad_f,), f32),
        ]
    )
    attn_grad = lax.psum_scatter(attn_terms, AXES, scatter_dimension=0, tiled=True)
    ffn_grad = lax.psum_scatter(ffn_terms, AXES, scatter_dimension=0, tiled=True)
    return jnp.stack(outs), jnp.stack(gins), attn_grad, ffn_grad


def solution(mesh):
    linked = tuple(mesh.shape[a] for a in AXES) == (8, 4)
    return jax.shard_map(
        shards_linked if linked else shards_any,
        mesh=mesh,
        in_specs=(P(AXES, None, None), P(AXES), P(AXES), P(AXES), P(AXES, None, None)),
        out_specs=(P(AXES, None, None), P(AXES, None, None), P(AXES), P(AXES)),
        check_vma=False,
    )
```

```python
from functools import partial

import jax
import jax.numpy as jnp
from jax import lax
from jax.experimental import pallas as pl
from jax.experimental.pallas import tpu as pltpu
from jax.sharding import PartitionSpec as P

D = 768
H = 12
FF = 3072
R = 768
PAIRS = 6
ATT_MAT = 4 * D * D
FFN_MAT = 2 * D * FF
ATT_VEC = 5 * D
FFN_VEC = FF + 3 * D
ATT_ROWS = 576
FFN_ROWS = 1152
VEC_ROWS = 80
AXES = ("dp", "fsdp")
bf16 = jnp.bfloat16
f32 = jnp.float32
MESH = pl.DeviceIdType.MESH

B_Q, B_V, B_OUT, G1, B1 = 0, 6, 12, 18, 24
B_IN, B_FC, G2, B2 = 32, 56, 62, 68


def nn(a, b):
    return jnp.dot(a, b, preferred_element_type=f32)


def nt(a, b):
    return lax.dot_general(a, b, (((1,), (1,)), ((), ())), preferred_element_type=f32)


def tn(a, b):
    return lax.dot_general(a, b, (((0,), (0,)), ((), ())), preferred_element_type=f32)


def split3(v):
    hi = v.astype(bf16)
    rest = v - hi.astype(f32)
    mid = rest.astype(bf16)
    return hi, mid, (rest - mid.astype(f32)).astype(bf16)


def place(chunk):
    z, x, y, c = chunk // 8, chunk // 4 % 2, chunk // 2 % 2, chunk % 2
    return z, c, (y * 2 + x if c == 0 else x * 2 + y)


def block(ref, chunk, rows):
    z, c, i = place(chunk)
    return ref[z, c, i, rows, :]


def aligned(start, size):
    return pl.ds(pl.multiple_of(start, size), size)


def w_qkv_pair(attn, i):
    blocks = [block(attn, d, aligned(i * 96, 96)) for d in range(24)]
    return jnp.concatenate(
        [jnp.concatenate([b[32 * p : 32 * p + 32] for b in blocks], axis=0) for p in range(3)], axis=1
    )


def put_w_qkv_pair(attn, i, value):
    for d in range(24):
        z, c, s = place(d)
        for p in range(3):
            attn[z, c, s, pl.ds(pl.multiple_of(i * 96 + 32 * p, 32), 32), :] = value[
                32 * d : 32 * d + 32, 128 * p : 128 * p + 128
            ]


def w_qkv_rows(attn, chunks, part):
    return jnp.concatenate(
        [
            jnp.concatenate(
                [block(attn, d, slice(96 * i + 32 * part, 96 * i + 32 * part + 32)) for i in range(PAIRS)], axis=1
            )
            for d in chunks
        ],
        axis=0,
    )


def w_out_cols(attn, j):
    blocks = [block(attn, d, slice(192 * j, 192 * j + 192)) for d in range(24, 32)]
    return jnp.concatenate(
        [jnp.concatenate([b[96 * p : 96 * p + 96] for b in blocks], axis=0) for p in range(2)], axis=1
    )


def w_out_rows(attn, chunks):
    return jnp.concatenate(
        [
            jnp.concatenate([block(attn, d, slice(96 * j, 96 * j + 96)) for j in range(6)], axis=1)
            for d in chunks
        ],
        axis=0,
    )


def w_in_cols(ffn, j, tiles):
    blocks = [block(ffn, d, aligned(j * 48 * tiles, 48 * tiles)) for d in range(16)]
    return jnp.concatenate(
        [jnp.concatenate([b[48 * p : 48 * p + 48] for b in blocks], axis=0) for p in range(tiles)], axis=1
    )


def put_w_in_cols(ffn, j, tiles, value):
    for d in range(16):
        z, c, s = place(d)
        for p in range(tiles):
            ffn[z, c, s, pl.ds(pl.multiple_of(j * 48 * tiles + 48 * p, 48), 48), :] = value[
                48 * d : 48 * d + 48, 128 * p : 128 * p + 128
            ]


def w_fc_cols(ffn, j):
    blocks = [block(ffn, d, aligned(j * 384, 384)) for d in range(16, 32)]
    return jnp.concatenate(
        [jnp.concatenate([b[192 * p : 192 * p + 192] for b in blocks], axis=0) for p in range(2)], axis=1
    )


def chip_slot(m):
    z, x, y = 2 + m // 4, m // 2 % 2, m % 2
    return z, (y * 2 + x, x * 2 + y)


def w_fc_rows(ffn, m):
    z, at = chip_slot(m)
    return jnp.concatenate(
        [
            jnp.concatenate([ffn[z, c, at[c], 192 * j : 192 * j + 192, :] for j in range(6)], axis=1)
            for c in range(2)
        ],
        axis=0,
    )


def put_w_fc_rows(ffn, m, value, tiles=range(6), base=0):
    z, at = chip_slot(m)
    z = z - base
    for c in range(2):
        for n, j in enumerate(tiles):
            ffn[z, c, at[c], 192 * j : 192 * j + 192, :] = value[192 * c : 192 * c + 192, 128 * n : 128 * n + 128]


def wide(vec, row, n=6):
    return jnp.concatenate([vec[row + j : row + j + 1, :] for j in range(n)], axis=1)


def put_wide(vec, row, value):
    for j in range(value.shape[1] // 128):
        vec[row + j : row + j + 1, :] = value[:, 128 * j : 128 * j + 128]


def lane_ids():
    return lax.broadcasted_iota(jnp.int32, (R, 128), 1)


def attend_pair(qp, kp, vp, dead, lane):
    one, zero = jnp.ones((), bf16), jnp.zeros((), bf16)
    v_one = jnp.concatenate([vp, jnp.ones((R, 128), bf16)], axis=1)
    outs, augmented = [], []
    for h in range(2):
        own = (lane < 64) if h == 0 else (lane >= 64)
        e = 64 if h == 0 else 0
        qh = jnp.where(own, qp, jnp.where(lane == e, one, zero))
        kh = jnp.where(own, kp, jnp.where(lane == e, dead, zero))
        mixed, lses = [], []
        for b in range(3):
            rows = slice(256 * b, 256 * b + 256)
            s = nt(qh[rows], kh)
            top = jnp.max(s, axis=-1, keepdims=True)
            p = jnp.exp(s - top).astype(bf16)
            both = nn(p, v_one)
            total = both[:, 128:]
            mixed.append(both[:, :128] / total)
            lses.append(top + jnp.log(total))
        outs.append(jnp.concatenate(mixed, axis=0))
        hi, mid, low = split3(jnp.concatenate(lses, axis=0))
        for k, part in enumerate((hi, mid, low)):
            qh = jnp.where(lane == e + 1 + k, part, qh)
        augmented.append(qh)
    return jnp.where(lane < 64, outs[0], outs[1]), augmented


def attend_pair_back(q_aug, kp, vp, dop, mixed, dead, lane):
    zero, minus = jnp.zeros((), bf16), -jnp.ones((), bf16)
    weighted = dop.astype(f32) * mixed.astype(f32)
    k_t = kp.T
    dks, dvs, dqs = [], [], []
    for h in range(2):
        own = (lane < 64) if h == 0 else (lane >= 64)
        e = 64 if h == 0 else 0
        dot = jnp.sum(jnp.where(own, weighted, 0.0), axis=-1, keepdims=True)
        do_aug = jnp.where(own, dop, zero)
        for k, part in enumerate(split3(dot)):
            do_aug = jnp.where(lane == e + k, part, do_aug)
        v_aug = jnp.where(own, vp, jnp.where((lane >= e) & (lane < e + 3), minus, zero))
        k_aug = jnp.where(own, kp, jnp.where((lane > e) & (lane < e + 4), minus, jnp.where(lane == e, dead, zero)))
        p = jnp.exp(nt(k_aug, q_aug[h]))
        ds = (p * nt(v_aug, do_aug)).astype(bf16)
        dvs.append(nn(p.astype(bf16), dop))
        dks.append(nn(ds, q_aug[h]))
        dqs.append(nn(k_t, ds))
    row = lax.broadcasted_iota(jnp.int32, (128, R), 0)
    dq = (jnp.where(row < 64, dqs[0], dqs[1]) * 0.125).astype(bf16).T
    dk = jnp.where(lane < 64, dks[0], dks[1]).astype(bf16)
    dv = jnp.where(lane < 64, dvs[0], dvs[1]).astype(bf16)
    return dq, dk, dv


def norm_back(g, xhat, gain, rstd):
    gg = g * gain
    m1 = jnp.mean(gg, axis=-1, keepdims=True)
    m2 = jnp.mean(gg * xhat, axis=-1, keepdims=True)
    return rstd * (gg - m1 - xhat * m2)


def column_sum(v):
    return jnp.sum(v.astype(f32), axis=0, keepdims=True)


ROWS = 128
BLOCKS = R // ROWS


def layer_kernel(gather, scatter, refs):
    length = refs["length"][0]
    x, io = refs["x"], refs["io"]

    def cot_copy(b):
        slot = lax.rem(b, 2)
        return pltpu.make_async_copy(refs["cot"].at[aligned(b * ROWS, ROWS)], refs["cot_b"].at[slot], io.at[6 + slot])

    def out_copy(b):
        slot = lax.rem(b, 2)
        return pltpu.make_async_copy(refs["out_b"].at[slot], refs["out"].at[aligned(b * ROWS, ROWS)], io.at[8 + slot])

    x_copy = pltpu.make_async_copy(refs["x_in"], x, io.at[0])
    x_copy.start()
    cot_copy(0).start()
    attn, ffn, vec, vg = refs["attn"], refs["ffn"], refs["vec"], refs["vg"]
    qx, kk, vv = refs["qx"], refs["k"], refs["v"]
    xh1, rs1, n1 = refs["xh1"], refs["rs1"], refs["n1"]
    act, gp, r2, gf = refs["act"], refs["gp"], refs["r2"], refs["gf"]
    do, mix = n1, refs["mix"]

    def dead_keys():
        row = lax.broadcasted_iota(jnp.int32, (R, 128), 0)
        return jnp.where(row < length, 0.0, -1e30).astype(bf16)

    gather.start()
    x_copy.wait()

    def forward_pair(i, carry):
        gather.before_pair(i)
        lane = lane_ids()
        cols = aligned(i * 128, 128)
        bias = jnp.concatenate(
            [vec[pl.ds(B_Q + i, 1), :], jnp.zeros((1, 128), f32), vec[pl.ds(B_V + i, 1), :]], axis=1
        )
        qkv = (nn(x[...], w_qkv_pair(attn, i)) + bias).astype(bf16)
        qp, kp, vp = qkv[:, :128] * jnp.asarray(0.125, bf16), qkv[:, 128:256], qkv[:, 256:]
        kk[:, cols] = kp
        vv[:, cols] = vp
        mixed, augmented = attend_pair(qp, kp, vp, dead_keys(), lane)
        mix[:, cols] = mixed.astype(bf16)
        for h in range(2):
            qx[:, pl.ds(pl.multiple_of(i * 256 + 128 * h, 128), 128)] = augmented[h]
        return carry

    lax.fori_loop(0, PAIRS, forward_pair, 0)
    gather.step(0)
    for j in range(3):
        cols = slice(256 * j, 256 * j + 256)
        xh1[:, cols] = nn(mix[...], w_out_cols(attn, j)) + wide(vec, B_OUT + 2 * j, 2) + x[:, cols].astype(f32)

    def norm1(b, carry):
        rows = aligned(b * ROWS, ROWS)
        r = xh1[rows, :]
        cen = r - jnp.mean(r, axis=-1, keepdims=True)
        rstd = lax.rsqrt(jnp.mean(cen * cen, axis=-1, keepdims=True) + 1e-05)
        xhat = cen * rstd
        xh1[rows, :] = xhat
        rs1[rows, :] = jnp.broadcast_to(rstd, (ROWS, 128))
        n1[rows, :] = (xhat * wide(vec, G1) + wide(vec, B1)).astype(bf16)
        return carry

    gather.step(1)
    lax.fori_loop(0, BLOCKS, norm1, 0)

    def ffn_in(j, carry):
        gather.before_in(j)
        cols = aligned(j * 256, 256)
        bias = jnp.concatenate([vec[pl.ds(B_IN + 2 * j, 1), :], vec[pl.ds(B_IN + 2 * j + 1, 1), :]], axis=1)
        pre = nn(n1[...], w_in_cols(ffn, j, 2)) + bias
        cdf = 0.5 + 0.5 * lax.erf(pre * 0.7071067811865476)
        act[:, cols] = (pre * cdf).astype(bf16)
        gp[:, cols] = (cdf + pre * (jnp.exp(-0.5 * pre * pre) * 0.3989422804014327)).astype(bf16)
        return carry

    lax.fori_loop(0, 12, ffn_in, 0)

    def ffn_out(j, carry):
        gather.before_out(j)
        cols = aligned(j * 256, 256)
        row = lambda base: jnp.concatenate(
            [vec[pl.ds(base + 2 * j, 1), :], vec[pl.ds(base + 2 * j + 1, 1), :]], axis=1
        )
        n1_full = xh1[:, cols] * row(G1) + row(B1)
        r2[:, cols] = nn(act[...], w_fc_cols(ffn, j)) + row(B_FC) + n1_full
        return carry

    lax.fori_loop(0, 3, ffn_out, 0)
    gather.finish()

    def norm2(b, sums):
        rows = aligned(b * ROWS, ROWS)
        r = r2[rows, :]
        cen = r - jnp.mean(r, axis=-1, keepdims=True)
        rstd = lax.rsqrt(jnp.mean(cen * cen, axis=-1, keepdims=True) + 1e-05)
        xhat = cen * rstd
        pl.when(b + 1 < BLOCKS)(lambda: cot_copy(b + 1).start())
        cot_copy(b).wait()
        pl.when(b >= 2)(lambda: out_copy(b - 2).wait())
        row = lax.broadcasted_iota(jnp.int32, (ROWS, D), 0) + b * ROWS
        valid = jnp.where(row < length, 1.0, 0.0)
        slot = lax.rem(b, 2)
        refs["out_b"][slot] = ((xhat * wide(vec, G2) + wide(vec, B2)) * valid).astype(bf16)
        out_copy(b).start()
        g = refs["cot_b"][slot].astype(f32) * valid
        grad = norm_back(g, xhat, wide(vec, G2), rstd)
        r2[rows, :] = grad
        low = grad.astype(bf16)
        gf[rows, :] = low
        return sums[0] + column_sum(g * xhat), sums[1] + column_sum(g), sums[2] + column_sum(low)

    zeros = jnp.zeros((1, D), f32)
    d_g2, d_b2, d_bfc = lax.fori_loop(0, BLOCKS, norm2, (zeros, zeros, zeros))
    for b in (BLOCKS - 2, BLOCKS - 1):
        out_copy(b).wait()
    put_wide(vg, G2, d_g2)
    put_wide(vg, B2, d_b2)
    put_wide(vg, B_FC, d_bfc)

    def back_first(m, carry):
        scatter.in_first(m)
        grad = tn(act[:, aligned(m * 384, 384)], gf[:, 0:384]).astype(bf16)
        put_w_fc_rows(refs["fc_g"], m, grad, range(0, 3), 2)
        return carry

    lax.fori_loop(0, 4, back_first, 0)

    def back_hidden(m):
        scatter.in_fc(m)
        cols = aligned(m * 384, 384)
        grad_act = nt(gf[...], w_fc_rows(ffn, m))
        low = (grad_act * gp[:, cols].astype(f32)).astype(bf16)
        gp[:, cols] = low
        sums = column_sum(low)
        for j in range(3):
            vg[pl.ds(B_IN + 3 * m + j, 1), :] = sums[:, 128 * j : 128 * j + 128]
        return cols

    def back_near(m, carry):
        cols = back_hidden(m)
        put_w_fc_rows(ffn, m, tn(act[:, cols], gf[:, 384:768]).astype(bf16), range(3, 6))
        return carry

    def back_fc(m, carry):
        cols = back_hidden(m)
        put_w_fc_rows(ffn, m, tn(act[:, cols], gf[...]).astype(bf16))
        return carry

    lax.fori_loop(0, 4, back_near, 0)
    lax.fori_loop(4, 8, back_fc, 0)

    def back_in(j, carry):
        scatter.in_in(j)
        cols = aligned(j * 512, 512)
        g = gp[:, cols]
        r2[...] += nt(g, w_in_cols(ffn, j, 4))
        put_w_in_cols(ffn, j, 4, tn(n1[...], g).astype(bf16))
        return carry

    lax.fori_loop(0, 6, back_in, 0)
    scatter.between(0)

    def back_norm1(b, sums):
        rows = aligned(b * ROWS, ROWS)
        g, xhat = r2[rows, :], xh1[rows, :]
        grad = norm_back(g, xhat, wide(vec, G1), rs1[rows, 0:1])
        r2[rows, :] = grad
        low = grad.astype(bf16)
        gf[rows, :] = low
        return sums[0] + column_sum(g * xhat), sums[1] + column_sum(g), sums[2] + column_sum(low)

    d_g1, d_b1, d_bout = lax.fori_loop(0, BLOCKS, back_norm1, (zeros, zeros, zeros))
    put_wide(vg, G1, d_g1)
    put_wide(vg, B1, d_b1)
    put_wide(vg, B_OUT, d_bout)
    scatter.between(1)

    for half in range(2):
        do[:, 384 * half : 384 * half + 384] = nt(
            gf[...], w_out_rows(attn, range(24 + 4 * half, 28 + 4 * half))
        ).astype(bf16)
    scatter.between(2)
    for half in range(2):
        cols = slice(384 * half, 384 * half + 384)
        grad = tn(mix[:, cols], gf[...]).astype(bf16)
        for d in range(4):
            z, c, s = place(24 + 4 * half + d)
            for j in range(6):
                attn[z, c, s, 96 * j : 96 * j + 96, :] = grad[96 * d : 96 * d + 96, 128 * j : 128 * j + 128]

    def backward_pair(i, carry):
        scatter.pair_start(i)
        lane = lane_ids()
        cols = aligned(i * 128, 128)
        q_aug = [qx[:, pl.ds(pl.multiple_of(i * 256 + 128 * h, 128), 128)] for h in range(2)]
        dq, dk, dv = attend_pair_back(
            q_aug, kk[:, cols], vv[:, cols], do[:, cols], mix[:, cols], dead_keys(), lane
        )
        do[:, cols] = dq
        kk[:, cols] = dk
        vv[:, cols] = dv
        scatter.pair_end(i)
        vg[pl.ds(B_Q + i, 1), :] = column_sum(dq)
        vg[pl.ds(B_V + i, 1), :] = column_sum(dv)
        put_w_qkv_pair(refs["qkv_g"], i, tn(x[...], jnp.concatenate([dq, dk, dv], axis=1)).astype(bf16))
        return carry

    lax.fori_loop(0, PAIRS, backward_pair, 0)
    gin_copies = []
    for n in range(3):
        scatter.tail(n)
        cols = slice(256 * n, 256 * n + 256)
        total = r2[:, cols]
        for p, g in enumerate((do, kk, vv)):
            total = total + nt(g[...], w_qkv_rows(attn, range(8 * n, 8 * n + 8), p))
        mix[:, cols] = total.astype(bf16)
        gin_copies.append(pltpu.make_async_copy(mix.at[:, cols], refs["gin"].at[:, cols], io.at[1 + n]))
        gin_copies[-1].start()
    scatter.tail(3)
    for copy in gin_copies:
        copy.wait()


class Loaded:
    def __init__(self, refs):
        self.refs = refs

    def start(self):
        r = self.refs
        copies = [
            pltpu.make_async_copy(r["attn_in"], r["attn"], r["io"].at[8]),
            pltpu.make_async_copy(r["ffn_in"], r["ffn"], r["io"].at[9]),
        ]
        for c in copies:
            c.start()
        r["vec"][...] = r["vec_in"][...].astype(f32)
        for c in copies:
            c.wait()

    def before_pair(self, i):
        pass

    before_in = before_out = step = before_pair

    def finish(self):
        pass


def position():
    dp, fs = lax.axis_index("dp"), lax.axis_index("fsdp")
    return lax.div(dp, 2), lax.rem(dp, 2), lax.div(fs, 2), lax.rem(fs, 2)


def device(z, x, y, c):
    return (z * 2 + x, y * 2 + c)


def remote(src, dst, send, recv, target):
    return pltpu.make_async_remote_copy(
        src_ref=src, dst_ref=dst, send_sem=send, recv_sem=recv, device_id=target, device_id_type=MESH
    )


ATT_GROUPS = (288, 288)
FFN_GROUPS = (192, 96, 192, 192, 192, 288)
PLANE_GROUPS = 2
Z, PASS, A, B, C, HOP = range(1, 7)
VECTOR_MARKS = (3003, 4003, 5003)
GATHER_ENDS = {
    0: (3020, 3030, 1000, 1010, 1040, 3000, 3040, 3050, 3060, 3010, 3070, 4020, 4030, 4000, 3001, 4040, 3011, 6020, 4010, 6030, 1050, 1060, 1070, 3002, 3003, 4001, 5000, 4011, 5040, 4002, 3012, 4003, 6021, 5010, 6031, 4012, 5001, 3013, 5011, 3041, 5002, 3051, 4050, 4013, 3061, 3042, 5003,),
    2: (4041, 3043, 3052, 4042, 4051, 3071, 5012, 5050,),
    4: (4060, 3062, 5013,),
    6: (5041, 4043, 6022, 4052,),
    8: (5042, 5051, 4061, 6032, 4070, 3072, 5060,),
    10: (5043, 5052, 3053, 3063, 4062,),
    12: (5061, 4071, 3073,),
    13: (5070, 5062, 4053, 4063, 4072,),
    14: (6023, 5071, 4073,),
    15: (5053, 6033, 5063,),
    17: (5072,),
    18: (5073,),
}
GATHER_MIDDLE = {
    0: (3020, 3030, 1000, 1010, 3000, 3040, 3050, 3060, 3010, 3070, 4020, 4030, 4000, 4040, 3002, 2003, 3003, 6020, 3001, 4010, 6030, 3012, 4002, 2013, 1040, 1050, 1060, 1070, 5000, 4003, 3011, 3013, 5040, 4001, 2043, 3043, 3041, 4012, 5010, 4011, 6022, 4013, 6021, 5002, 6032, 3042, 6031, 5003, 5001, 2053, 3053, 3051, 3052,),
    2: (4041, 5012,),
    4: (2063, 4050, 3061, 4042, 4051, 3062, 3063, 5011, 5013,),
    6: (2073, 5041, 4060, 3071, 3072, 3073,),
    8: (5050, 5042, 4043, 4052,),
    10: (5051, 4061,),
    12: (6023, 5060, 4070, 5043, 4053,),
    13: (6033, 5052, 5061, 4062, 4071,),
    14: (5070, 5053, 4063, 4072,),
    15: (5062, 4073,),
    16: (5071,),
    17: (5063,),
    19: (5072, 5073,),
}
SCATTER = {
    0: (100, 101,),
    2: (200, 201,),
    4: (102, 103,),
    5: (202,),
    6: (300, 203,),
    7: (301,),
    8: (302, 104, 105, 106, 107,),
    9: (400, 204, 205, 206, 108,),
    10: (401, 402, 303, 207, 208, 109,),
    11: (304, 209, 110,),
    12: (403, 210, 305, 111, 500,),
    13: (211, 404, 112,),
    14: (306, 212, 113,),
    15: (501, 405, 307, 213, 406,),
    16: (502, 308,),
    17: (114,),
    19: (503, 309, 407, 214, 408,),
    20: (310, 504, 115,),
    22: (409, 311, 215,),
    23: (116, 505,),
    25: (410, 411, 312, 216,),
    26: (506, 313, 117,),
    28: (508, 509, 412, 217,),
    29: (507, 118,),
    31: (314, 413, 315, 510, 218,),
    32: (316, 119,),
    34: (414, 511, 317, 219,),
    35: (415, 318, 120,),
    36: (416, 220,),
    37: (512, 417,),
    38: (418, 319, 513, 320, 419, 515, 420, 514, 516, 517, 518, 519, 520,),
}

ATT, FFN = 0, 1


def group_of(g):
    if g < len(ATT_GROUPS):
        return ATT, pl.ds(sum(ATT_GROUPS[:g]), ATT_GROUPS[g])
    g -= len(ATT_GROUPS)
    return FFN, pl.ds(sum(FFN_GROUPS[:g]), FFN_GROUPS[g])


ATT_HEAD, FFN_HEAD = 30, 42

N_GROUPS = len(ATT_GROUPS) + len(FFN_GROUPS)
PLANE_ROWS = sum(FFN_GROUPS[:PLANE_GROUPS])


def is_plane_group(g):
    return len(ATT_GROUPS) <= g < len(ATT_GROUPS) + PLANE_GROUPS


class Gather:
    def __init__(self, refs):
        self.refs = refs
        self.z, self.x, self.y, self.c = z, x, y, c = position()
        self.me = z * 8 + x * 4 + y * 2 + c
        first = c == 0
        a, b = jnp.where(first, x, y), jnp.where(first, y, x)
        self.slot, self.pair = b * 2 + a, b * 2
        self.other_slot, self.other_pair = b * 2 + 1 - a, (1 - b) * 2
        self.dev_a = device(z, jnp.where(first, 1 - x, x), jnp.where(first, y, 1 - y), c)
        self.dev_b = device(z, jnp.where(first, x, 1 - x), jnp.where(first, 1 - y, y), c)
        self.dev_c = device(z, x, y, 1 - c)
        self.zs = [lax.rem(z + k, 4) for k in (1, 2, 3)]
        self.dev_z = [device(t, x, y, c) for t in self.zs]
        upper = lax.div(z, 2)
        self.near = [z, z + 1 - 2 * lax.rem(z, 2), 2 - upper, 3 - 3 * upper]
        self.dev_near = [device(t, x, y, c) for t in self.near]
        self.is_end = (z == 0) | (z == 3)
        self.is_middle = (z == 1) | (z == 2)
        self.from_me = 2 + jnp.where(self.is_end, 1, 0)
        self.half = upper * 2
        self.other_half = 2 - upper * 2
        last = lax.rem(self.me + 1, 32)
        before = lax.rem(self.me + 31, 32)
        self.dev_after = (lax.div(last, 4), lax.rem(last, 4))
        self.dev_before = (lax.div(before, 4), lax.rem(before, 4))
        self.buf = (refs["attn"], refs["ffn"])

    def barrier(self, own_work):
        bar = pltpu.get_barrier_semaphore()
        targets = [self.dev_a, self.dev_b, self.dev_c, self.dev_after, self.dev_before] + self.dev_z
        for t in targets:
            pl.semaphore_signal(bar, inc=1, device_id=t, device_id_type=MESH)
        own_work()
        pl.semaphore_wait(bar, len(targets))

    def z_copy(self, g, k):
        kind, rows = group_of(g)
        ref = self.buf[kind].at[self.z, self.c, self.slot, rows]
        index = 1 if k == 1 else self.from_me
        r = self.refs
        return remote(ref, ref, r["gs"].at[8 + 3 * kind + k - 1], r["zr"].at[g, index], self.dev_near[k])

    def pass_copy(self, g):
        kind, rows = group_of(g)
        ref = self.buf[kind].at[self.near[3], self.c, self.slot, rows]
        return remote(ref, ref, self.refs["gs"].at[14 + kind], self.refs["zr"].at[g, 3], self.dev_near[1])

    def z_arrival(self, g, k):
        kind, rows = group_of(g)
        wide_ = pl.ds(0, 4) if is_plane_group(g) else self.slot
        ref = self.buf[kind].at[self.near[k], self.c, wide_, rows]
        return remote(ref, ref, self.refs["gs"].at[8], self.refs["zr"].at[g, k], self.dev_near[1])

    def hop_copy(self, g, k, n):
        _, rows = group_of(g)
        layer = self.near[max(n - 1, 0)]
        ref = self.refs["ffn"].at[layer, self.c, :, rows]
        target = self.dev_near[2 if n in (1, 2) else 1]
        index = (1, 2, 3, 2, 3)[n]
        return remote(ref, ref, self.refs["gs"].at[16 + n], self.refs["zr"].at[g, index], target)

    def plane_copy(self, step, g, k):
        kind, rows = group_of(g)
        r = self.refs
        at = self.buf[kind].at[self.near[k], self.c]
        later = 0 if kind == ATT else 1 if k == 0 else 2
        if step == A:
            src, send, recv, target = at.at[self.slot, rows], later, "ar", self.dev_a
        elif step == B:
            src, send, recv, target = at.at[pl.ds(self.pair, 2), rows], 3 + later, "br", self.dev_b
        else:
            src, send, recv, target = at.at[:, rows], 6 + kind, "cr", self.dev_c
        return remote(src, src, r["gs"].at[send], r[recv].at[g, k], target)

    def run(self, code):
        kind, g, k = code // 1000, code // 10 % 100, code % 10
        if kind == Z:
            self.z_copy(g, 1).start()
            self.z_copy(g, 2).start()
            pl.when(self.is_middle)(lambda: self.z_copy(g, 3).start())
            return
        if kind == PASS:
            self.z_arrival(g, 3).wait_recv()
            self.pass_copy(g).start()
            return
        if kind == HOP:
            if k == 0:
                self.plane_copy(B, g, 0).wait_recv()
                self.hop_copy(g, 0, 0).start()
                pl.when(self.is_middle)(lambda: self.hop_copy(g, 0, 1).start())
            else:
                self.z_arrival(g, k).wait_recv()
                pl.when(self.is_middle)(lambda: self.hop_copy(g, k, k + 1).start())
            self.plane_copy(C, g, k).start()
            return
        if kind == A and k in (1, 2):
            self.z_arrival(g, k).wait_recv()
        elif kind == A and k == 3:
            pl.when(self.is_end)(lambda: self.z_arrival(g, 3).wait_recv())
        elif kind == B:
            self.plane_copy(A, g, k).wait_recv()
        elif kind == C:
            self.plane_copy(B, g, k).wait_recv()
        self.plane_copy(kind, g, k).start()

    def ready(self, g, first, count):
        kind, rows = group_of(g)
        r = self.refs
        for n in range(count):
            ref = self.buf[kind].at[0, 1 - self.c, :, rows]
            remote(ref, ref, r["gs"].at[6 + kind], r["cr"].at[g, first + n], self.dev_c).wait_recv()

    def steps(self, key):
        for who, table in ((self.is_end, GATHER_ENDS), (self.is_middle, GATHER_MIDDLE)):
            if key in table:

                @pl.when(who)
                def _(table=table):
                    for s in table[key]:
                        self.run(s)

    def vectors(self, stage):
        r = self.refs
        buf, own, v = r["vec_all"], r["tail"], r["vsem"]
        one = buf.at[self.c, self.slot]
        if stage == 0:

            @pl.when(self.z == 3)
            def _():
                one[...] = own[...]
                for k in range(3):
                    remote(own, one, v.at[4 + k], v.at[1], self.dev_z[k]).start()

        elif stage == 1:

            @pl.when(self.z == 3)
            def _():
                for k in range(3):
                    remote(own, one, v.at[4 + k], v.at[1], self.dev_z[k]).wait_send()

            @pl.when(self.z != 3)
            def _():
                remote(one, one, v.at[4], v.at[1], self.dev_z[0]).wait_recv()

            remote(one, one, v.at[7], v.at[2], self.dev_a).start()
        elif stage == 2:
            got = buf.at[self.c, self.other_slot]
            remote(got, got, v.at[7], v.at[2], self.dev_a).wait()
            mine = buf.at[self.c, pl.ds(self.pair, 2)]
            remote(mine, mine, v.at[8], v.at[3], self.dev_b).start()
        elif stage == 3:
            got = buf.at[self.c, pl.ds(self.other_pair, 2)]
            remote(got, got, v.at[8], v.at[3], self.dev_b).wait()
            mine = buf.at[self.c]
            remote(mine, mine, v.at[9], v.at[10], self.dev_c).start()
        else:
            got = buf.at[1 - self.c]
            remote(got, got, v.at[9], v.at[10], self.dev_c).wait()
            r["vec"][...] = buf[1, 3].astype(f32)

    def tail_copy(self):
        t = self.refs["tail"]
        return remote(t, self.refs["tail_in"], self.refs["vsem"].at[11], self.refs["vsem"].at[12], self.dev_after)

    def load_own(self):
        r = self.refs
        flat_a, flat_f = r["flat_a"], r["flat_f"]
        own_a, own_f = r["attn_own"], r["ffn_own"]
        whole_a, whole_f = ATT_ROWS * 128, FFN_ROWS * 128
        flat_a[ATT_HEAD + ATT_ROWS : ATT_HEAD + ATT_ROWS + 16, :] = jnp.zeros((16, 128), f32)
        flat_f[FFN_HEAD + FFN_ROWS : FFN_HEAD + FFN_ROWS + 16, :] = jnp.zeros((16, 128), f32)
        flat_a[pl.ds(ATT_HEAD, ATT_ROWS), :] = own_a[0:whole_a].reshape(ATT_ROWS, 128).astype(f32)
        flat_f[pl.ds(FFN_HEAD, FFN_ROWS), :] = own_f[0:whole_f].reshape(FFN_ROWS, 128).astype(f32)
        at = ATT_HEAD + ATT_ROWS
        flat_a[at : at + 1, 0:120] = own_a[whole_a : whole_a + 120].reshape(1, 120).astype(f32)
        at = FFN_HEAD + FFN_ROWS
        flat_f[at : at + 1, :] = own_f[whole_f : whole_f + 128].reshape(1, 128).astype(f32)
        flat_f[at + 1 : at + 2, 0:40] = own_f[whole_f + 128 : whole_f + 168].reshape(1, 40).astype(f32)
        lane = lax.broadcasted_iota(jnp.int32, (32, 128), 1)
        v = pltpu.roll(flat_a[ATT_HEAD + 546 : ATT_HEAD + 586, :], 8, 1)
        r["tail"][0:32, :] = jnp.where(lane < 8, v[0:32], v[1:33]).astype(bf16)
        lane = lax.broadcasted_iota(jnp.int32, (48, 128), 1)
        v = pltpu.roll(flat_f[FFN_HEAD + 1111 : FFN_HEAD + 1167, :], 88, 1)
        r["tail"][32:80, :] = jnp.where(lane < 88, v[0:48], v[1:49]).astype(bf16)

    def place_own(self, kind):
        r = self.refs
        if kind == ATT:
            flat, rows, head, size, moved, at = r["flat_a"], r["attn_sum"], ATT_HEAD, ATT_ROWS, 120, 0
        else:
            flat, rows, head, size, moved, at = r["flat_f"], r["ffn_sum"], FFN_HEAD, FFN_ROWS, 168, 32
        flat[0:head, :] = r["tail_in"][at : at + head, :].astype(f32)
        shift = head * 128 - moved * self.me

        def step(n, carry):
            rows[pl.ds(pl.multiple_of(n * 64, 64), 64), :] = self.shifted(flat, shift, n)
            return carry

        lax.fori_loop(0, size // 64, step, 0)
        slot = self.buf[kind].at[self.z, self.c, self.slot]
        self.by_kind(kind, lambda tiles, n, at: self.to_tiles(rows, slot, tiles, n, at))

    def by_kind(self, kind, fn):
        if kind == ATT:
            pl.when(self.z < 3)(lambda: fn(18, 32, lambda t: (t % 6 * 3 + t // 6) * 32))
            pl.when(self.z == 3)(lambda: fn(6, 96, lambda t: t * 96))
        else:
            pl.when(self.z < 2)(lambda: fn(24, 48, lambda t: t * 48))
            pl.when(self.z >= 2)(lambda: fn(6, 192, lambda t: t * 192))

    def to_tiles(self, rows, slot, tiles, n, at):
        for t in range(tiles):
            slot[at(t) : at(t) + n, :] = rows[pl.ds(t, n, stride=tiles), :].astype(bf16)

    def from_tiles(self, total, flat, tiles, n, at):
        for t in range(tiles):
            flat[pl.ds(t, n, stride=tiles), :] = total[at(t) : at(t) + n, :]

    def shifted(self, src, shift, n):
        row, turn = lax.div(shift, 128), lax.rem(shift, 128)
        lane = lax.broadcasted_iota(jnp.int32, (64, 128), 1)
        back = lax.rem(128 - turn, 128)
        low = pltpu.roll(src[pl.ds(n * 64 + row, 64), :], back, 1)
        high = pltpu.roll(src[pl.ds(n * 64 + row + 1, 64), :], back, 1)
        return jnp.where(lane < 128 - turn, low, high)

    def start(self):
        self.barrier(self.load_own)
        pl.when(self.me < 31)(lambda: self.tail_copy().start())
        self.vectors(0)
        pl.when(self.me > 0)(lambda: self.tail_copy().wait_recv())
        self.place_own(ATT)
        for g in range(len(ATT_GROUPS)):
            self.run(1000 * Z + 10 * g)
        for g in range(len(ATT_GROUPS)):
            self.run(1000 * A + 10 * g)
        self.place_own(FFN)
        for who, table in ((self.is_end, GATHER_ENDS), (self.is_middle, GATHER_MIDDLE)):

            @pl.when(who)
            def _(table=table):
                done = [1000 * kind + 10 * g for kind in (Z, A) for g in range(len(ATT_GROUPS))]
                first = [v for v in table[0] if v not in done]
                cuts = [0] + [first.index(v) + 1 for v in VECTOR_MARKS] + [len(first)]
                for stage in range(4):
                    for s in first[cuts[stage] : cuts[stage + 1]]:
                        self.run(s)
                    self.vectors(stage + 1)

    def before_pair(self, i):
        for v in range(PAIRS):

            @pl.when(i == v)
            def _(v=v):
                if v:
                    self.steps(2 * v)
                if v * len(ATT_GROUPS) % PAIRS == 0:
                    self.ready(v * len(ATT_GROUPS) // PAIRS, 0, 4)

    def step(self, n):
        self.steps(12 + n)

    def before_in(self, j):
        at = 0
        for n, rows in enumerate(FFN_GROUPS):

            @pl.when(j == at // 96)
            def _(n=n):
                self.steps(14 + n)
                self.ready(len(ATT_GROUPS) + n, self.half, 2)

            at += rows

    def before_out(self, j):
        seen = 0
        for v in range(3):
            more, at = [], 0
            for n, rows in enumerate(FFN_GROUPS):
                if n >= seen and at < 384 * (v + 1):
                    more.append(n)
                at += rows
            seen += len(more)

            @pl.when(j == v)
            def _(v=v, more=more):
                self.steps(14 + len(FFN_GROUPS) + v)
                for n in more:
                    self.ready(len(ATT_GROUPS) + n, self.other_half, 2)

    def finish(self):
        self.steps(17 + len(FFN_GROUPS))
        r = self.refs
        z, c, gs = self.z, self.c, r["gs"]
        attn, ffn = self.buf
        rest = pl.ds(PLANE_ROWS, FFN_ROWS - PLANE_ROWS)
        front = pl.ds(0, PLANE_ROWS)

        def sent(n, ref):
            remote(ref, ref, gs.at[n], r["zr"].at[0, 0], self.dev_c).wait_send()

        sent(0, attn.at[:, c, self.slot])
        sent(1, ffn.at[z, c, self.slot])
        sent(2, ffn.at[pl.ds(0, 3), c, self.slot, rest])
        sent(3, attn.at[:, c, pl.ds(self.pair, 2)])
        sent(4, ffn.at[z, c, pl.ds(self.pair, 2)])
        sent(5, ffn.at[pl.ds(0, 3), c, pl.ds(self.pair, 2), rest])
        sent(6, attn.at[:, c])
        sent(7, ffn.at[:, c])
        for k in range(2):
            sent(8 + k, attn.at[z, c, self.slot])
            sent(11 + k, ffn.at[z, c, self.slot, rest])
        if PLANE_GROUPS:
            sent(16, ffn.at[z, c, :, front])

        @pl.when(self.is_middle)
        def _():
            sent(10, attn.at[z, c, self.slot])
            sent(13, ffn.at[z, c, self.slot, rest])
            sent(14, attn.at[z, c, self.slot])
            sent(15, ffn.at[z, c, self.slot, rest])
            if PLANE_GROUPS:
                for n in range(17, 21):
                    sent(n, ffn.at[z, c, :, front])

        pl.when(self.me < 31)(lambda: self.tail_copy().wait_send())


W_FC, W_IN, W_OUT, W_QKV = 0, 8, 14, 15
N_ITEMS = W_QKV + PAIRS


class Scatter:
    def __init__(self, refs, gather):
        self.refs, self.g = refs, gather

    def part(self, item):
        if item < 2:
            return "fc_g", "ffn", range(2, 3), pl.ds(288 * item, 288), 288, 0
        if item >= W_QKV:
            return "qkv_g", "attn", range(0, 3), pl.ds(96 * (item - W_QKV), 96), 96, 2
        if item == W_OUT:
            return "attn", "attn", range(3, 4), pl.ds(0, 576), 576, 1
        if item >= W_IN:
            return "ffn", "ffn", range(0, 2), pl.ds(192 * (item - W_IN), 192), 192, 0
        z = 2 + item // 4
        return "ffn", "ffn", range(z, z + 1), pl.ds(288 * (item % 4), 288), 288, 0

    def span(self, zz):
        return pl.ds(zz[0], len(zz))

    def at(self, buf, z):
        return z - 2 if buf == "fc_g" else z

    def add(self, pairs, rows, count):
        def step(n, carry):
            at = pl.ds(pl.multiple_of(rows.start + n * 96, 96), 96)
            for dst, src in pairs:
                d = dst.at[at]
                d[...] = d[...] + src.at[at][...]
            return carry

        if count == 96:
            step(0, 0)
        else:
            lax.fori_loop(0, count // 96, step, 0)

    def c_copy(self, g):
        buf, kind, zz, rows, _, s = self.part(g)
        r, t = self.refs, self.g
        return remote(
            r[buf].at[self.span([self.at(buf, z) for z in zz]), 1 - t.c, :, rows],
            r[kind + "_rc"].at[self.span(zz), :, rows],
            r["ss"].at[s, 0],
            r["sr"].at[0, g],
            t.dev_c,
        )

    def b_copy(self, g):
        buf, kind, zz, rows, _, s = self.part(g)
        r, t = self.refs, self.g
        return remote(
            r[buf].at[self.span([self.at(buf, z) for z in zz]), t.c, pl.ds(t.other_pair, 2), rows],
            r[kind + "_rb"].at[self.span(zz), :, rows],
            r["ss"].at[s, 1],
            r["sr"].at[1, g],
            t.dev_b,
        )

    def a_copy(self, g):
        buf, kind, zz, rows, _, s = self.part(g)
        r, t = self.refs, self.g
        return remote(
            r[buf].at[self.span([self.at(buf, z) for z in zz]), t.c, t.other_slot, rows],
            r[kind + "_ra"].at[self.span(zz), rows],
            r["ss"].at[s, 2],
            r["sr"].at[2, g],
            t.dev_a,
        )

    def z_copy(self, g, k):
        buf, kind, zz, rows, _, s = self.part(g)
        r, t = self.refs, self.g
        return remote(
            r[buf].at[self.at(buf, t.zs[k]), t.c, t.slot, rows],
            r[kind + "_rz"].at[k, rows],
            r["ss"].at[s, 3 + k],
            r["sr"].at[3, g],
            t.dev_z[k],
        )

    def inside(self, value, zz):
        return (value >= zz[0]) & (value <= zz[-1])

    def c_send(self, g):
        self.c_copy(g).start()

    def b_send(self, g):
        buf, kind, zz, rows, n, _ = self.part(g)
        r, t = self.refs, self.g
        self.c_copy(g).wait_recv()
        self.add([(r[buf].at[self.at(buf, z), t.c, i], r[kind + "_rc"].at[z, i]) for z in zz for i in range(4)], rows, n)
        self.b_copy(g).start()

    def a_send(self, g):
        buf, kind, zz, rows, n, _ = self.part(g)
        r, t = self.refs, self.g
        self.b_copy(g).wait_recv()
        self.add([(r[buf].at[self.at(buf, z), t.c, t.pair + i], r[kind + "_rb"].at[z, i]) for z in zz for i in range(2)], rows, n)
        self.a_copy(g).start()

    def z_send(self, g):
        buf, kind, zz, rows, n, _ = self.part(g)
        r, t = self.refs, self.g
        self.a_copy(g).wait_recv()
        self.add([(r[buf].at[self.at(buf, z), t.c, t.slot], r[kind + "_ra"].at[z]) for z in zz], rows, n)
        for k in range(3):

            @pl.when(self.inside(t.zs[k], zz))
            def _():
                self.z_copy(g, k).start()

    def take(self, g):
        buf, kind, zz, rows, n, _ = self.part(g)
        r, t = self.refs, self.g

        @pl.when(self.inside(t.z, zz))
        def _():
            got = r[kind + "_rz"].at[:, rows]
            remote(got, got, r["ss"].at[0, 3], r["sr"].at[3, g], t.dev_c).wait_recv()

            def step(i, carry):
                at = pl.ds(pl.multiple_of(rows.start + i * 96, 96), 96)
                total = r[buf][self.at(buf, t.z), t.c, t.slot, at, :].astype(f32)
                for k in range(3):
                    total = total + r[kind + "_rz"][k, at, :].astype(f32)
                r[kind + "_sum"][at, :] = total
                return carry

            lax.fori_loop(0, n // 96, step, 0)

    def vectors(self, stage):
        r, t = self.refs, self.g
        own, got, s, v = r["vg"], r["vg_r"], r["vs"], r["vr"]
        if stage > 0:
            target = (t.dev_c, t.dev_b, t.dev_a)[stage - 1]
            remote(own, got.at[stage - 1], s.at[stage - 1], v.at[stage - 1], target).wait()
            own[...] = own[...] + got[stage - 1]
        if stage < 3:
            target = (t.dev_c, t.dev_b, t.dev_a)[stage]
            remote(own, got.at[stage], s.at[stage], v.at[stage], target).start()
        else:
            for k in range(3):

                @pl.when(t.zs[k] == 3)
                def _():
                    remote(own, got.at[3 + k], s.at[3 + k], v.at[3 + k], t.dev_z[k]).start()

    def take_vectors(self):
        r, t = self.refs, self.g
        own, got, s, v = r["vg"], r["vg_r"], r["vs"], r["vr"]
        for k in range(3):

            @pl.when(t.zs[k] == 3)
            def _():
                remote(own, got.at[3 + k], s.at[3 + k], v.at[3 + k], t.dev_z[k]).wait_send()

        @pl.when(t.z == 3)
        def _():
            for k in range(3):
                remote(own, got.at[3 + k], s.at[3 + k], v.at[3 + k], t.dev_z[k]).wait_recv()
            own[...] = own[...] + got[3] + got[4] + got[5]

    def sent(self):
        r, t = self.refs, self.g
        ss = r["ss"]

        def one(s, n, ref):
            remote(ref, ref, ss.at[s, n], r["sr"].at[0, 0], t.dev_c).wait_send()

        for s, ref in enumerate((r["ffn"], r["attn"].at[pl.ds(3, 1)], r["qkv_g"])):
            one(s, 0, ref.at[:, 1 - t.c])
            one(s, 1, ref.at[:, t.c, pl.ds(t.other_pair, 2)])
            one(s, 2, ref.at[:, t.c, t.other_slot])
        for k in range(3):
            one(0, 3 + k, r["ffn"].at[0, t.c, t.slot])
            pl.when(t.zs[k] == 3)(lambda k=k: one(1, 3 + k, r["attn"].at[3, t.c, t.slot]))
            pl.when(t.zs[k] != 3)(lambda k=k: one(2, 3 + k, r["qkv_g"].at[0, t.c, t.slot]))

    def step(self, key):
        for s in SCATTER.get(key, ()):
            self.one(s)

    def one(self, s):
        kinds = (None, self.c_send, self.b_send, self.a_send, self.z_send, self.take)
        kinds[s // 100](s % 100)

    def loop(self, i, first, stride, count):
        for v in range(count):
            if first + stride * v in SCATTER:
                pl.when(i == v)(lambda v=v: self.step(first + stride * v))

    def in_first(self, m):
        self.loop(m, 40, 1, 4)

    def in_fc(self, m):
        self.loop(m, 0, 1, 8)

    def in_in(self, j):
        self.loop(j, 8, 1, 6)

    def between(self, n):
        self.step(14 + n)

    def pair_start(self, i):
        self.loop(i, 17, 3, PAIRS)

    def pair_end(self, i):
        self.loop(i, 19, 3, PAIRS)

    def tail(self, n):
        if n < 3:
            self.step(35 + n)
            self.vectors(n)
            return
        order = SCATTER[38]
        ffn_left = max(i for i, s in enumerate(order) if s // 100 == 5 and s % 100 < W_OUT) + 1
        relays_left = max(i for i, s in enumerate(order) if s // 100 < 5) + 1
        at = order.index(300 + N_ITEMS - 1) + 1
        for n, s in enumerate(order[:ffn_left]):
            self.one(s)
            if n + 1 == at:
                self.vectors(3)
        self.hand_over(FFN)
        for n, s in enumerate(order[ffn_left:relays_left]):
            self.one(s)
            if n + 1 + ffn_left == at:
                self.vectors(3)
        for s in order[relays_left:]:
            self.one(s)
        self.hand_over(ATT)
        self.take_vectors()
        self.finish(FFN)
        self.finish(ATT)
        self.sent()

    def head_copy(self, kind):
        r, t = self.refs, self.g
        count = (32, 48)[kind]
        head, got = r[("flat_a", "flat_f")[kind]].at[pl.ds(0, count)], r["head_in"].at[pl.ds(32 * kind, count)]
        return remote(head, got, r["hs"].at[2 * kind], r["hs"].at[2 * kind + 1], t.dev_before)

    def hand_over(self, kind):
        r, t = self.refs, self.g
        total, flat = r[("attn_sum", "ffn_sum")[kind]], r[("flat_a", "flat_f")[kind]]
        t.by_kind(kind, lambda tiles, n, at: t.from_tiles(total, flat, tiles, n, at))
        pl.when(t.me > 0)(self.head_copy(kind).start)

    def finish(self, kind):
        r, t = self.refs, self.g
        size, count, moved = ((ATT_ROWS, 32, 120), (FFN_ROWS, 48, 168))[kind]
        flat, out = r[("flat_a", "flat_f")[kind]], r[("attn_out", "ffn_out")[kind]]
        copy = self.head_copy(kind)
        pl.when(t.me < 31)(copy.wait_recv)
        mine = jnp.where(t.me == 31, r["vg"][32 * kind : 32 * kind + count, :], r["head_in"][32 * kind : 32 * kind + count, :])
        flat[size : size + count, :] = mine

        def step(n, carry):
            out[pl.ds(pl.multiple_of(n * 8192, 8192), 8192)] = t.shifted(flat, moved * t.me, n).reshape(8192)
            return carry

        lax.fori_loop(0, size // 64, step, 0)
        whole = size * 128
        rest = t.shifted(flat, moved * t.me, size // 64)
        if kind == ATT:
            out[whole : whole + 120] = rest[0:1, 0:120].reshape(120)
        else:
            out[whole : whole + 128] = rest[0:1, :].reshape(128)
            out[whole + 128 : whole + 168] = rest[1:2, 0:40].reshape(40)
        pl.when(t.me > 0)(copy.wait_send)


class Kept:
    def in_fc(self, m):
        pass

    in_first = in_in = between = pair_start = pair_end = tail = in_fc


SCRATCH = dict(
    x=((R, D), bf16),
    mix=((R, D), bf16),
    cot_b=((2, ROWS, D), bf16),
    out_b=((2, ROWS, D), bf16),
    attn=((4, 2, 4, ATT_ROWS, 128), bf16),
    ffn=((4, 2, 4, FFN_ROWS, 128), bf16),
    vec=((VEC_ROWS, 128), f32),
    qx=((R, 1536), bf16),
    k=((R, D), bf16),
    v=((R, D), bf16),
    xh1=((R, D), f32),
    rs1=((R, 128), f32),
    n1=((R, D), bf16),
    act=((R, FF), bf16),
    gp=((R, FF), bf16),
    r2=((R, D), f32),
    gf=((R, D), bf16),
    qkv_g=((3, 2, 4, ATT_ROWS, 128), bf16),
    fc_g=((1, 2, 4, FFN_ROWS // 2, 128), bf16),
)


def run_layer(linked, length, x, cot, attn_in, ffn_in, vec_in=None):
    dma = pltpu.SemaphoreType.DMA
    vmem, anywhere = pl.BlockSpec(memory_space=pltpu.VMEM), pl.BlockSpec(memory_space=pl.ANY)
    names = ["length", "x_in", "cot"] + (["attn_own", "ffn_own"] if linked else ["attn_in", "ffn_in", "vec_in"])
    names += ["out", "gin"] + (["attn_out", "ffn_out"] if linked else ["attn_g", "ffn_g", "vg"])
    more = dict(io=dma((10,)))
    if linked:
        more.update(
            vg=pltpu.VMEM((VEC_ROWS, 128), f32),
            vec_all=pltpu.VMEM((2, 4, VEC_ROWS, 128), bf16),
            tail=pltpu.VMEM((VEC_ROWS, 128), bf16),
            tail_in=pltpu.VMEM((VEC_ROWS, 128), bf16),
            head_in=pltpu.VMEM((VEC_ROWS, 128), f32),
            flat_a=pltpu.VMEM((704, 128), f32),
            flat_f=pltpu.VMEM((1280, 128), f32),
            gs=dma((21,)),
            zr=dma((N_GROUPS, 4)),
            ar=dma((N_GROUPS, 4)),
            br=dma((N_GROUPS, 4)),
            cr=dma((N_GROUPS, 4)),
            vsem=dma((13,)),
            ss=dma((3, 6)),
            sr=dma((4, N_ITEMS)),
            vs=dma((6,)),
            vr=dma((6,)),
            hs=dma((4,)),
            vg_r=pltpu.VMEM((6, VEC_ROWS, 128), f32),
        )
        for kind, rows in (("attn", ATT_ROWS), ("ffn", FFN_ROWS)):
            more[kind + "_rc"] = pltpu.VMEM((4, 4, rows, 128), bf16)
            more[kind + "_rb"] = pltpu.VMEM((4, 2, rows, 128), bf16)
            more[kind + "_ra"] = pltpu.VMEM((4, rows, 128), bf16)
            more[kind + "_rz"] = pltpu.VMEM((3, rows, 128), bf16)
            more[kind + "_sum"] = pltpu.VMEM((rows, 128), f32)
    names += list(SCRATCH) + list(more)
    scratch = [pltpu.VMEM(*s) for s in SCRATCH.values()] + list(more.values())

    def body(*args):
        refs = dict(zip(names, args, strict=True))
        refs["vg"][...] = jnp.zeros((VEC_ROWS, 128), f32)
        if linked:
            gather = Gather(refs)
            layer_kernel(gather, Scatter(refs, gather), refs)
            return
        layer_kernel(Loaded(refs), Kept(), refs)
        copies = [
            pltpu.make_async_copy(refs["qkv_g"], refs["attn_g"].at[0:3], refs["io"].at[0]),
            pltpu.make_async_copy(refs["attn"].at[3], refs["attn_g"].at[3], refs["io"].at[1]),
            pltpu.make_async_copy(refs["ffn"].at[0:2], refs["ffn_g"].at[0:2], refs["io"].at[2]),
            pltpu.make_async_copy(refs["fc_g"], refs["ffn_g"].at[2:3, :, :, 0:576], refs["io"].at[3]),
            pltpu.make_async_copy(refs["ffn"].at[2:3, :, :, 576:], refs["ffn_g"].at[2:3, :, :, 576:], refs["io"].at[4]),
            pltpu.make_async_copy(refs["ffn"].at[3], refs["ffn_g"].at[3], refs["io"].at[5]),
        ]
        for c in copies:
            c.start()
        for c in copies:
            c.wait()

    act_out = jax.ShapeDtypeStruct((R, D), bf16)
    if linked:
        grads = tuple(jax.ShapeDtypeStruct(a.shape, f32) for a in (attn_in, ffn_in))
    else:
        grads = tuple(jax.ShapeDtypeStruct(SCRATCH[k][0], bf16) for k in ("attn", "ffn"))
        grads += (jax.ShapeDtypeStruct((VEC_ROWS, 128), f32),)
    smem = pl.BlockSpec(memory_space=pltpu.SMEM)
    args = (length, x, cot, attn_in, ffn_in) + (() if linked else (vec_in,))
    return pl.pallas_call(
        body,
        out_shape=(act_out, act_out) + grads,
        in_specs=[smem, anywhere, anywhere] + ([vmem, vmem] if linked else [anywhere, anywhere, vmem]),
        out_specs=(anywhere,) * 2 + ((vmem,) * 2 if linked else (anywhere, anywhere, vmem)),
        scratch_shapes=scratch,
        compiler_params=pltpu.CompilerParams(
            vmem_limit_bytes=64 * 1024 * 1024 - 65536,
            has_side_effects=True,
            **(dict(collective_id=0) if linked else {}),
        ),
    )(*args)


def copy_results(*arrays):
    n = len(arrays)
    parts = [(i, p) for p in range(3) for i in range(n) if arrays[i].ndim == 2] + [
        (i, None) for i in range(n) if arrays[i].ndim == 1
    ]

    def body(*refs):
        src, dst, held, sems = refs[:n], refs[n : 2 * n], refs[2 * n : 3 * n], refs[3 * n]

        def view(ref, p):
            return ref if p is None else ref.at[pl.ds(256 * p, 256)]

        takes = [
            pltpu.make_async_copy(view(src[i], p), view(held[i], p), sems.at[0, j]) for j, (i, p) in enumerate(parts)
        ]
        gives = [
            pltpu.make_async_copy(view(held[i], p), view(dst[i], p), sems.at[1, j]) for j, (i, p) in enumerate(parts)
        ]
        for copy in takes:
            copy.start()
        for take, give in zip(takes, gives):
            take.wait()
            give.start()
        for copy in gives:
            copy.wait()

    anywhere = pl.BlockSpec(memory_space=pl.ANY)
    return pl.pallas_call(
        body,
        out_shape=tuple(jax.ShapeDtypeStruct(a.shape, a.dtype) for a in arrays),
        in_specs=[anywhere] * n,
        out_specs=(anywhere,) * n,
        scratch_shapes=[pltpu.VMEM(a.shape, a.dtype) for a in arrays] + [pltpu.SemaphoreType.DMA((2, len(parts)))],
    )(*arrays)


def qkv_chunk(flat):
    return flat.reshape(-1, 32, 3, 6, 128).transpose(0, 3, 2, 1, 4).reshape(-1, ATT_ROWS, 128)


def qkv_flat(chunk):
    return chunk.reshape(-1, 6, 3, 32, 128).transpose(0, 3, 2, 1, 4).reshape(-1)


def tiled_chunk(flat, rows, tiles):
    return flat.reshape(-1, rows, tiles, 128).transpose(0, 2, 1, 3).reshape(-1, rows * tiles, 128)


def tiled_flat(chunk, rows, tiles):
    return chunk.reshape(-1, tiles, rows, 128).transpose(0, 2, 1, 3).reshape(-1)


def pack_vectors(attn_vec, ffn_vec):
    return jnp.concatenate(
        [
            attn_vec.reshape(30, 128),
            jnp.zeros((2, 128), attn_vec.dtype),
            ffn_vec.reshape(42, 128),
            jnp.zeros((6, 128), attn_vec.dtype),
        ]
    )


def shards_linked(frames, lengths, attn_params, ffn_params, cotangent):
    out, gin, attn_grad, ffn_grad = copy_results(
        *run_layer(True, lengths, frames[0], cotangent[0], attn_params, ffn_params)
    )
    return out[None], gin[None], attn_grad, ffn_grad


def in_places(chunks):
    g = chunks.reshape(4, 2, 2, 2, -1, 128)
    p0 = g[:, :, :, 0].transpose(0, 2, 1, 3, 4).reshape(4, 4, -1, 128)
    p1 = g[:, :, :, 1].reshape(4, 4, -1, 128)
    return jnp.stack([p0, p1], axis=1)


def from_places(g):
    p0 = g[:, 0].reshape(4, 2, 2, -1, 128).transpose(0, 2, 1, 3, 4)
    p1 = g[:, 1].reshape(4, 2, 2, -1, 128)
    return jnp.stack([p0, p1], axis=3).reshape(32, -1, 128)


def shards_any(frames, lengths, attn_params, ffn_params, cotangent):
    devices = lax.axis_size(AXES)
    attn_flat = lax.all_gather(attn_params, AXES, axis=0, tiled=True)
    ffn_flat = lax.all_gather(ffn_params, AXES, axis=0, tiled=True)
    cut_a, cut_f = 3 * D * D, D * FF
    attn_in = in_places(
        jnp.concatenate([qkv_chunk(attn_flat[:cut_a]), tiled_chunk(attn_flat[cut_a:ATT_MAT], 96, 6)])
    )
    ffn_in = in_places(
        jnp.concatenate([tiled_chunk(ffn_flat[:cut_f], 48, 24), tiled_chunk(ffn_flat[cut_f:FFN_MAT], 192, 6)])
    )
    vec_in = pack_vectors(attn_flat[ATT_MAT : ATT_MAT + ATT_VEC], ffn_flat[FFN_MAT : FFN_MAT + FFN_VEC])
    outs, gins, sums = [], [], None
    for u in range(frames.shape[0]):
        out, gin, attn_g, ffn_g, vg = run_layer(False, lengths[u : u + 1], frames[u], cotangent[u], attn_in, ffn_in, vec_in)
        outs.append(out)
        gins.append(gin)
        grads = [g.astype(f32) for g in (attn_g, ffn_g, vg)]
        sums = grads if sums is None else [s + g for s, g in zip(sums, grads)]
    attn_c, ffn_c = from_places(sums[0]), from_places(sums[1])
    pad_a = attn_params.shape[0] * devices - ATT_MAT - ATT_VEC
    pad_f = ffn_params.shape[0] * devices - FFN_MAT - FFN_VEC
    attn_terms = jnp.concatenate(
        [qkv_flat(attn_c[:24]), tiled_flat(attn_c[24:], 96, 6), sums[2][:30].reshape(-1), jnp.zeros((pad_a,), f32)]
    )
    ffn_terms = jnp.concatenate(
        [
            tiled_flat(ffn_c[:16], 48, 24),
            tiled_flat(ffn_c[16:], 192, 6),
            sums[2][32:74].reshape(-1),
            jnp.zeros((pad_f,), f32),
        ]
    )
    attn_grad = lax.psum_scatter(attn_terms, AXES, scatter_dimension=0, tiled=True)
    ffn_grad = lax.psum_scatter(ffn_terms, AXES, scatter_dimension=0, tiled=True)
    return jnp.stack(outs), jnp.stack(gins), attn_grad, ffn_grad


def solution(mesh):
    linked = tuple(mesh.shape[a] for a in AXES) == (8, 4)
    return jax.shard_map(
        shards_linked if linked else shards_any,
        mesh=mesh,
        in_specs=(P(AXES, None, None), P(AXES), P(AXES), P(AXES), P(AXES, None, None)),
        out_specs=(P(AXES, None, None), P(AXES, None, None), P(AXES), P(AXES)),
        check_vma=False,
    )
```
